32 devices in a mesh: img: 2 (over y), gx: 4 (over z), gy: 4 (over x, core).
Axes of the slice: x: 2, y: 2, z: 4, core: 2. Of those that a mesh axis runs over, the one named last changes fastest.
Arguments:
- conc_old: float32 [128, 64, 128], P(('img', 'gx'), 'gy'), parts along dimension 0, may hold values from -1 to 1
- chem_old: float32 [128, 64, 128], P(('img', 'gx'), 'gy'), parts along dimension 0, may hold values from -4 to 4
Outputs:
- conc_new: float32 [128, 64, 128], P(('img', 'gx'), 'gy'), parts along dimension 0
- chem_new: float32 [128, 64, 128], P(('img', 'gx'), 'gy'), parts along dimension 0
The draws below stay inside these ranges and needn't reach their ends.
There are 2 independent parts, one for each index of `img`. The reference program is written for one: setup_inputs(seed, part) draws one part's arguments, and reference() takes and returns one part's arrays. A program takes and returns all parts, laid end to end along the dimension named above; each array names one. Nothing has to cross between parts.
All inputs are finite; a program needn't handle non-finite values.
Results may differ from the reference program's by a relative error of at most 0.0001.
Values sent between devices are 32-bit elements; how exact they have to be, the bound alone decides.
No kernel may reach another device: no remote copies, remote signals or barrier semaphores. Data moves between devices by JAX's collectives and lax.ppermute only.
A program may use at most 128 MiB of HBM per device.

```python
import jax
import jax.numpy as jnp

LEVELS = 4
SWEEPS = 2
COARSE = 6
NX = 64
NY = 64
NZ = 128


def shard_levels(stream_key, extent, pieces, smallest, largest):
    gain = 1.0
    for axis_at, parts in pieces:
        heights = jax.random.uniform(jax.random.fold_in(jax.random.fold_in(stream_key, 6), axis_at), (parts,), jnp.float32, smallest / len(pieces), largest / len(pieces))
        gain = gain * jnp.repeat(jnp.exp(heights), extent[axis_at] // parts).reshape((-1,) + (1,) * (len(extent) - 1 - axis_at))
    return gain


def bell_draw(own_key, extent, scale, limit, cuts=(), kind=jnp.bfloat16):
    drawn = jax.random.normal(own_key, extent, jnp.float32) * scale
    if len(cuts) > 0:
        drawn = shard_levels(own_key, extent, cuts, -0.22, 0.18) * drawn
    return jnp.clip(drawn, min=-limit, max=limit).astype(kind)


def setup_inputs(seed: int = 0, part: int = 0) -> dict:
    keys = jax.random.split(jax.random.key(seed), 3)
    own_keys = jax.random.split(jax.random.fold_in(keys[2], part), 3)
    conc_old = jnp.clip(jax.random.uniform(own_keys[0], (NX, NY, NZ), jnp.float32, -1.0, 1.0) * shard_levels(own_keys[0], (NX, NY, NZ), ((0, 4), (1, 4)), -0.4, 0.0), -1.0, 1.0)
    chem_old = bell_draw(own_keys[1], (NX, NY, NZ), 1.0, 4.0, ((0, 4), (1, 4)), jnp.float32)
    return dict(conc_old=conc_old, chem_old=chem_old)


TIME_STEP = 32.0
GRADIENT_ENERGY = 0.5
STABILIZER = 2.0
DAMPING = 0.7


def face_weights(mob_padded, level_scale):
    middle = mob_padded[1:-1, 1:-1, :]
    half_scale = 0.5 * level_scale
    weights = (half_scale * (middle + mob_padded[2:, 1:-1, :]),
               half_scale * (middle + mob_padded[:-2, 1:-1, :]),
               half_scale * (middle + mob_padded[1:-1, 2:, :]),
               half_scale * (middle + mob_padded[1:-1, :-2, :]),
               half_scale * (middle + jnp.roll(middle, -1, axis=2)),
               half_scale * (middle + jnp.roll(middle, 1, axis=2)))
    total_weight = weights[0] + weights[1] + weights[2] + weights[3] + weights[4] + weights[5]
    return weights, total_weight


def neighbour_list(padded, middle):
    return (padded[2:, 1:-1, :], padded[:-2, 1:-1, :], padded[1:-1, 2:, :], padded[1:-1, :-2, :],
            jnp.roll(middle, -1, axis=2), jnp.roll(middle, 1, axis=2))


def apply_operator(padded, weights, level_scale):
    middle = padded[:, 1:-1, 1:-1, :]
    conc_near = neighbour_list(padded[0], middle[0])
    chem_near = neighbour_list(padded[1], middle[1])
    flux = weights[0] * (chem_near[0] - middle[1])
    for position in range(1, 6):
        flux = flux + weights[position] * (chem_near[position] - middle[1])
    laplace = conc_near[0] + conc_near[1] + conc_near[2] + conc_near[3] + conc_near[4] + conc_near[5] - 6.0 * middle[0]
    first_eq = middle[0] - TIME_STEP * flux
    second_eq = middle[1] - STABILIZER * middle[0] + GRADIENT_ENERGY * level_scale * laplace
    return jnp.stack([first_eq, second_eq])


def update(residual, total_weight, level_scale):
    diagonal = STABILIZER + 6.0 * GRADIENT_ENERGY * level_scale
    coupling = TIME_STEP * total_weight
    determinant = 1.0 + coupling * diagonal
    conc_step = (residual[0] - coupling * residual[1]) / determinant
    chem_step = (residual[1] + diagonal * residual[0]) / determinant
    return DAMPING * jnp.stack([conc_step, chem_step])


def sweep_once(padded, right_side, mob_padded, level_scale):
    weights, total_weight = face_weights(mob_padded, level_scale)
    residual = right_side - apply_operator(padded, weights, level_scale)
    return padded[:, 1:-1, 1:-1, :] + update(residual, total_weight, level_scale)


def defect(padded, right_side, mob_padded, level_scale):
    weights = face_weights(mob_padded, level_scale)[0]
    return right_side - apply_operator(padded, weights, level_scale)


def coarsen(values):
    dims_now = values.shape
    grouped = values.reshape(dims_now[:-3] + (dims_now[-3] // 2, 2, dims_now[-2] // 2, 2, dims_now[-1] // 2, 2))
    return jnp.sum(grouped, axis=(-5, -3, -1)) * 0.125


def refine(values):
    for axis_pos in (-3, -2, -1):
        values = jnp.repeat(values, 2, axis=axis_pos)
    return values


def wrap_fields(fields):
    return jnp.pad(fields, ((0, 0), (1, 1), (1, 1), (0, 0)), mode="wrap")


def wrap_cells(cells):
    return jnp.pad(cells, ((1, 1), (1, 1), (0, 0)), mode="wrap")


def reference(conc_old, chem_old):
    mobility = 0.1 + jnp.square(1.0 - conc_old * conc_old)
    level_data = []
    for level_index in range(LEVELS):
        level_data.append((wrap_cells(mobility), 0.25 ** level_index))
        if level_index + 1 < LEVELS:
            mobility = coarsen(mobility)

    def cycle_level(level_index, fields, right_side):
        mob_padded, level_scale = level_data[level_index]
        if level_index == LEVELS - 1:
            fields = jnp.zeros_like(right_side)
            for sweep_index in range(COARSE):
                fields = sweep_once(wrap_fields(fields), right_side, mob_padded, level_scale)
            return fields
        for sweep_index in range(SWEEPS):
            fields = sweep_once(wrap_fields(fields), right_side, mob_padded, level_scale)
        residual = defect(wrap_fields(fields), right_side, mob_padded, level_scale)
        coarse_right = coarsen(residual)
        correction = cycle_level(level_index + 1, jnp.zeros_like(coarse_right), coarse_right)
        fields = fields + refine(correction)
        for sweep_index in range(SWEEPS):
            fields = sweep_once(wrap_fields(fields), right_side, mob_padded, level_scale)
        return fields

    right_side = jnp.stack([conc_old, conc_old * conc_old * conc_old - (1.0 + STABILIZER) * conc_old])
    start_fields = jnp.stack([conc_old, chem_old])
    result = cycle_level(0, start_fields, right_side)
    return result[0], result[1]
```

```python
import jax
import jax.numpy as jnp
from jax import lax
from jax.experimental import pallas as pl
from jax.experimental.pallas import tpu as pltpu
from jax.sharding import PartitionSpec as P

LEVELS = 4
SWEEPS = 2
COARSE = 6


TIME_STEP = 32.0
GRADIENT_ENERGY = 0.5
STABILIZER = 2.0
DAMPING = 0.7


def extended(cells, sides, width):
    for axis, dim in sides:
        count = lax.axis_size(axis)
        head = lax.slice_in_dim(cells, 0, width, axis=dim)
        tail = lax.slice_in_dim(cells, cells.shape[dim] - width, cells.shape[dim], axis=dim)
        cells = jnp.concatenate(
            [
                lax.ppermute(tail, axis, [(i, (i + 1) % count) for i in range(count)]),
                cells,
                lax.ppermute(head, axis, [((i + 1) % count, i) for i in range(count)]),
            ],
            axis=dim,
        )
    return cells


def mobility_of(concentration):
    return 0.1 + jnp.square(1.0 - concentration * concentration)


def right_of(concentration):
    return jnp.stack(
        [
            concentration,
            concentration * concentration * concentration - (1.0 + STABILIZER) * concentration,
        ]
    )


def face_weights(mob_padded, level_scale):
    middle = mob_padded[1:-1, 1:-1, :]
    half_scale = 0.5 * level_scale
    weights = (
        half_scale * (middle + mob_padded[2:, 1:-1, :]),
        half_scale * (middle + mob_padded[:-2, 1:-1, :]),
        half_scale * (middle + mob_padded[1:-1, 2:, :]),
        half_scale * (middle + mob_padded[1:-1, :-2, :]),
        half_scale * (middle + jnp.roll(middle, -1, axis=2)),
        half_scale * (middle + jnp.roll(middle, 1, axis=2)),
    )
    total_weight = weights[0] + weights[1] + weights[2] + weights[3] + weights[4] + weights[5]
    return (weights, total_weight)


def neighbour_list(padded, middle):
    return (
        padded[2:, 1:-1, :],
        padded[:-2, 1:-1, :],
        padded[1:-1, 2:, :],
        padded[1:-1, :-2, :],
        jnp.roll(middle, -1, axis=2),
        jnp.roll(middle, 1, axis=2),
    )


def apply_operator(padded, weights, level_scale):
    middle = padded[:, 1:-1, 1:-1, :]
    conc_near = neighbour_list(padded[0], middle[0])
    chem_near = neighbour_list(padded[1], middle[1])
    flux = weights[0] * (chem_near[0] - middle[1])
    for position in range(1, 6):
        flux = flux + weights[position] * (chem_near[position] - middle[1])
    laplace = (
        conc_near[0]
        + conc_near[1]
        + conc_near[2]
        + conc_near[3]
        + conc_near[4]
        + conc_near[5]
        - 6.0 * middle[0]
    )
    first_eq = middle[0] - TIME_STEP * flux
    second_eq = middle[1] - STABILIZER * middle[0] + GRADIENT_ENERGY * level_scale * laplace
    return jnp.stack([first_eq, second_eq])


def update(residual, total_weight, level_scale):
    diagonal = STABILIZER + 6.0 * GRADIENT_ENERGY * level_scale
    coupling = TIME_STEP * total_weight
    determinant = 1.0 + coupling * diagonal
    conc_step = (residual[0] - coupling * residual[1]) / determinant
    chem_step = (residual[1] + diagonal * residual[0]) / determinant
    return DAMPING * jnp.stack([conc_step, chem_step])


def sweep_once(padded, right_side, mob_padded, level_scale):
    weights, total_weight = face_weights(mob_padded, level_scale)
    residual = right_side - apply_operator(padded, weights, level_scale)
    return padded[:, 1:-1, 1:-1, :] + update(residual, total_weight, level_scale)


def defect(padded, right_side, mob_padded, level_scale):
    weights = face_weights(mob_padded, level_scale)[0]
    return right_side - apply_operator(padded, weights, level_scale)


def coarsen(values):
    dims_now = values.shape
    grouped = values.reshape(
        dims_now[:-3] + (dims_now[-3] // 2, 2, dims_now[-2] // 2, 2, dims_now[-1] // 2, 2)
    )
    return jnp.sum(grouped, axis=(-5, -3, -1)) * 0.125


def refine(values):
    for axis_pos in (-3, -2, -1):
        values = jnp.repeat(values, 2, axis=axis_pos)
    return values


def trim_rim(values, width):
    return values[..., width:-width, width:-width, :]


def field_rim(fields):
    return extended(fields, (("gx", 1), ("gy", 2)), 1)


def coarsest_solve(right_side, mobility, level_scale):
    mob_padded = extended(mobility, (("gx", 0), ("gy", 1)), 1)
    fields = update(right_side, face_weights(mob_padded, level_scale)[1], level_scale)
    for sweep_index in range(COARSE - 1):
        padded = extended(fields, (("gx", 1), ("gy", 2)), 1)
        fields = sweep_once(padded, right_side, mob_padded, level_scale)
    return fields


def plain_solve(start_fields):
    outer_fields = field_rim(start_fields)
    mob_outer = mobility_of(outer_fields[0])
    mobility = trim_rim(mob_outer, 1)
    level_data = []
    for level_index in range(LEVELS - 1):
        if level_index == 0:
            mob_padded = mob_outer
        else:
            mob_padded = extended(mobility, (("gx", 0), ("gy", 1)), 1)
        level_data.append((mob_padded, 0.25**level_index))
        mobility = coarsen(mobility)
    coarsest_scale = 0.25 ** (LEVELS - 1)

    def cycle_level(level_index, right_side):
        if level_index == LEVELS - 1:
            return coarsest_solve(right_side, mobility, coarsest_scale)
        mob_padded, level_scale = level_data[level_index]
        if level_index == 0:
            fields = sweep_once(outer_fields, right_side, mob_padded, level_scale)
        else:
            fields = update(right_side, face_weights(mob_padded, level_scale)[1], level_scale)
        fields = sweep_once(field_rim(fields), right_side, mob_padded, level_scale)
        residual = defect(field_rim(fields), right_side, mob_padded, level_scale)
        fields = fields + refine(cycle_level(level_index + 1, coarsen(residual)))
        for sweep_index in range(SWEEPS):
            fields = sweep_once(field_rim(fields), right_side, mob_padded, level_scale)
        return fields

    return cycle_level(0, right_of(start_fields[0]))


HALO = 4
GRID_BYTES_MAX = 2 * 1024 * 1024


def whole_block():
    return pl.BlockSpec(memory_space=pltpu.VMEM)


def lane_roll(values, shift):
    return pltpu.roll(values, shift % values.shape[1], axis=1)


def row_roll(values, shift):
    return pltpu.roll(values, shift % values.shape[0], axis=0)


def lane_bit(shape, dup):
    return (lax.broadcasted_iota(jnp.int32, shape, 1) // dup) % 2 == 0


def low_rows(shape):
    return lax.broadcasted_iota(jnp.int32, shape, 0) < HALO


def loop_rows(count, unroll, row_group):
    steps, rest = divmod(count, unroll)
    if steps == 1:
        row_group(0, unroll)
    elif steps > 1:

        def step(index, carry):
            row_group(index * unroll, unroll)
            return carry

        lax.fori_loop(0, steps, step, 0)
    if rest:
        row_group(steps * unroll, rest)


def wrapped(row, count):
    if isinstance(row, int):
        return row % count
    return lax.rem(row + count, count)


class Level:
    def __init__(self, level_index, weights):
        self.scale = 0.25**level_index
        self.dup = 2**level_index
        self.diagonal = STABILIZER + 6.0 * GRADIENT_ENERGY * self.scale
        self.face_x, self.face_y, self.face_z, self.coupling, self.gain = weights

    def set_weights(self, mobility, start, count, unroll):
        total = mobility.shape[0]
        half = 0.5 * self.scale * TIME_STEP

        def group(first, size):
            rows = [mobility[wrapped(start + first + i - 1, total)] for i in range(size + 2)]
            before = half * (rows[0] + rows[1])
            for i in range(size):
                at = wrapped(start + first + i, total)
                here = rows[i + 1]
                after = half * (here + rows[i + 2])
                along_y = half * (here + row_roll(here, -1))
                along_z = half * (here + lane_roll(here, -self.dup))
                coupling = (
                    before
                    + after
                    + along_y
                    + row_roll(along_y, 1)
                    + along_z
                    + lane_roll(along_z, self.dup)
                )
                self.face_x[at] = after
                self.face_y[at] = along_y
                self.face_z[at] = along_z
                self.coupling[at] = coupling
                self.gain[at] = DAMPING / (1.0 + coupling * self.diagonal)
                before = after

        loop_rows(count, unroll, group)

    def residuals(self, fields, right, start, first, size):
        conc, chem = fields
        total = conc.shape[0]
        at = [wrapped(start + first + i - 1, total) for i in range(size + 2)]
        u = [chem[r] for r in at]
        c = [conc[r] for r in at]
        before = self.face_x[at[0]] * (u[1] - u[0])
        for i in range(1, size + 1):
            r = at[i]
            after = self.face_x[r] * (u[i + 1] - u[i])
            along_y = self.face_y[r] * (row_roll(u[i], -1) - u[i])
            along_z = self.face_z[r] * (lane_roll(u[i], -self.dup) - u[i])
            flux = (after - before) + (along_y - row_roll(along_y, 1))
            flux = flux + (along_z - lane_roll(along_z, self.dup))
            near = (c[i - 1] + c[i + 1]) + (row_roll(c[i], 1) + row_roll(c[i], -1))
            near = near + (lane_roll(c[i], self.dup) + lane_roll(c[i], -self.dup))
            conc_left = right[0][r] - c[i] + flux
            chem_left = (
                right[1][r] - u[i] + self.diagonal * c[i] - (GRADIENT_ENERGY * self.scale) * near
            )
            before = after
            yield r, c[i], u[i], conc_left, chem_left

    def steps(self, row, conc_left, chem_left):
        gain = self.gain[row]
        return (
            gain * (conc_left - self.coupling[row] * chem_left),
            gain * (chem_left + self.diagonal * conc_left),
        )

    def first_sweep(self, right, out, unroll):
        def group(first, size):
            for i in range(size):
                r = first + i
                conc_step, chem_step = self.steps(r, right[0][r], right[1][r])
                out[0][r] = conc_step
                out[1][r] = chem_step

        loop_rows(right[0].shape[0], unroll, group)

    def sweep(self, fields, right, start, count, unroll, put):
        def group(first, size):
            for r, c, u, conc_left, chem_left in self.residuals(fields, right, start, first, size):
                conc_step, chem_step = self.steps(r, conc_left, chem_left)
                put(r, c + conc_step, u + chem_step)

        loop_rows(count, unroll, group)

    def coarse_right(self, fields, right, start, count, unroll, put):
        def group(first, size):
            lefts = [(a, b) for _, _, _, a, b in self.residuals(fields, right, start, first, size)]
            for i in range(0, size, 2):
                put(
                    (first + i) // 2,
                    lefts[i][0] + lefts[i + 1][0],
                    lefts[i][1] + lefts[i + 1][1],
                )

        loop_rows(count, unroll, group)


def put_in(conc, chem):
    def put(row, conc_value, chem_value):
        conc[row] = conc_value
        chem[row] = chem_value

    return put


def pair_rows(ref, row, count):
    return ref[row, pl.ds(0, count, stride=2), :] + ref[row, pl.ds(1, count, stride=2), :]


def pair_lanes(values, dup):
    swapped = jnp.where(
        lane_bit(values.shape, dup), lane_roll(values, -dup), lane_roll(values, dup)
    )
    return values + swapped


def edge_rows_kernel(conc, chem, low, high):
    rows = conc.shape[0]
    low[0] = conc[:HALO]
    low[1] = chem[:HALO]
    high[0] = conc[rows - HALO :]
    high[1] = chem[rows - HALO :]


def frame_row(row, rows, own, before, after):
    if row < HALO:
        return before[row]
    if row < HALO + rows:
        return own[row - HALO]
    return after[row - HALO - rows]


def edge_columns_kernel(conc, chem, before, after, to_left, to_right):
    rows, columns = conc.shape[0], conc.shape[1]
    for row in range(rows + 2 * HALO):
        c = frame_row(row, rows, conc, before.at[0], after.at[0])
        u = frame_row(row, rows, chem, before.at[1], after.at[1])
        low = low_rows((8, c.shape[1]))
        to_left[row] = jnp.where(low, c[:8], row_roll(u[:8], HALO))
        to_right[row] = jnp.where(low, row_roll(u[columns - 8 :], HALO), c[columns - 8 :])


def fine_down_kernel(
    conc, chem, before, after, from_left, from_right,
    packed, conc_out, chem_out, right_conc, right_chem,
    face_x, face_y, face_z, coupling, gain,
    chem_start, mobility, conc_mid, chem_mid, sums,
):
    rows, columns, lanes = conc.shape
    frame = rows + 2 * HALO
    low = low_rows((8, lanes))
    for row in range(frame):
        c = frame_row(row, rows, conc, before.at[0], after.at[0])
        u = frame_row(row, rows, chem, before.at[1], after.at[1])
        left, right = from_left[row], from_right[row]
        c = jnp.concatenate([c, jnp.where(low, right, left)], axis=0)
        u = jnp.concatenate([u, row_roll(jnp.where(low, left, right), HALO)], axis=0)
        right_conc[row] = c
        chem_start[row] = u
        right_chem[row] = c * (c * c - (1.0 + STABILIZER))
        gap = 1.0 - c * c
        mobility[row] = 0.1 + gap * gap
    level = Level(0, (face_x, face_y, face_z, coupling, gain))
    level.set_weights(mobility, 0, frame, 2)
    right_side = (right_conc, right_chem)
    level.sweep(
        (right_conc, chem_start), right_side, 1, frame - 2, 2, put_in(conc_mid, chem_mid)
    )
    level.sweep(
        (conc_mid, chem_mid), right_side, 2, frame - 4, 2, put_in(conc_out, chem_out)
    )

    def keep(index, conc_sum, chem_sum):
        sums[0, index] = conc_sum
        sums[1, index] = chem_sum

    level.coarse_right((conc_out, chem_out), right_side, HALO, rows, 2, keep)
    for index in range(rows // 2):
        sums[2, index] = mobility[HALO + 2 * index] + mobility[HALO + 2 * index + 1]
    even = lane_bit((columns // 2, lanes), 1)
    for field in range(3):
        for index in range(rows // 4):
            a = pair_rows(sums.at[field], 2 * index, columns // 2)
            b = pair_rows(sums.at[field], 2 * index + 1, columns // 2)
            packed[field, index] = 0.125 * jnp.where(
                even, a + lane_roll(a, -1), b + lane_roll(b, 1)
            )


def spread_rows(ref, row, values):
    count = values.shape[0]
    ref[row, pl.ds(0, count, stride=2), :] = values
    ref[row, pl.ds(1, count, stride=2), :] = values


def coarse_kernel(
    place, packed, conc_in, chem_in, right_conc, right_chem,
    face_x, face_y, face_z, coupling, gain,
    conc_new, chem_new,
    *scratch,
):
    at_x, at_y = place[0], place[1]
    scratch = list(scratch)
    levels = []
    for level_index in (1, 2, 3):
        mobility, right0, right1, a0, a1, b0, b1 = scratch[:7]
        level = Level(level_index, scratch[7:12])
        levels.append((level, mobility, (right0, right1), (a0, a1), (b0, b1)))
        del scratch[:12]
    sums1, sums2, spread2, spread3, spread_fine, fine_a0, fine_a1, fine_b0, fine_b1 = scratch
    one, mob1, right1, a1, b1 = levels[0]
    two, mob2, right2, a2, b2 = levels[1]
    three, mob3, right3, a3, b3 = levels[2]
    rows1, columns1, lanes = mob1.shape
    rows2, columns2 = mob2.shape[:2]
    rows3, columns3 = mob3.shape[:2]
    slots_x, slots_y = packed.shape[1], packed.shape[0]
    own_rows, own_columns = rows1 // slots_x, columns1 // slots_y
    even = lane_bit((own_columns, lanes), 1)
    targets = (right1[0], right1[1], mob1)

    bits = slots_y.bit_length() - 1

    def unpack(slot, carry):
        slot_y, slot_x = slot // slots_x, slot % slots_x
        from_y = at_y
        for bit in range(bits):
            from_y = from_y ^ (((slot_y >> bit) & 1) << (bits - 1 - bit))
        row0 = (at_x ^ slot_x) * own_rows
        column = pl.ds(pl.multiple_of(from_y * own_columns, 8), own_columns)
        for field in range(3):
            for index in range(own_rows // 2):
                pair = packed[slot_y, slot_x, field, index]
                targets[field][row0 + 2 * index, column, :] = jnp.where(
                    even, pair, lane_roll(pair, 1)
                )
                targets[field][row0 + 2 * index + 1, column, :] = jnp.where(
                    even, lane_roll(pair, -1), pair
                )
        return carry

    lax.fori_loop(0, slots_x * slots_y, unpack, 0)

    def coarsen_into(sums, out, count, columns, dup):
        for field in range(len(out)):
            for index in range(count):
                half = pair_rows(sums.at[field], index, columns)
                out[field][index] = 0.125 * pair_lanes(half, dup)

    def mobility_sums(mobility, sums):
        for index in range(mobility.shape[0] // 2):
            sums[2, index] = mobility[2 * index] + mobility[2 * index + 1]

    def keep_in(sums):
        def keep(index, conc_sum, chem_sum):
            sums[0, index] = conc_sum
            sums[1, index] = chem_sum

        return keep

    one.set_weights(mob1, 0, rows1, 2)
    one.first_sweep(right1, a1, 2)
    one.sweep(a1, right1, 0, rows1, 2, put_in(*b1))
    one.coarse_right(b1, right1, 0, rows1, 2, keep_in(sums1))
    mobility_sums(mob1, sums1)
    coarsen_into(sums1, (right2[0], right2[1], mob2), rows2, columns2, 2)

    two.set_weights(mob2, 0, rows2, 4)
    two.first_sweep(right2, a2, 4)
    two.sweep(a2, right2, 0, rows2, 4, put_in(*b2))
    two.coarse_right(b2, right2, 0, rows2, 4, keep_in(sums2))
    mobility_sums(mob2, sums2)
    coarsen_into(sums2, (right3[0], right3[1], mob3), rows3, columns3, 4)

    three.set_weights(mob3, 0, rows3, rows3)
    three.first_sweep(right3, a3, rows3)
    now, other = a3, b3
    for sweep_index in range(COARSE - 1):
        three.sweep(now, right3, 0, rows3, rows3, put_in(*other))
        now, other = other, now

    for field in range(2):
        for row in range(rows3):
            spread_rows(spread3.at[field], row, now[field][row])
            both = spread3[field, row]
            a2[field][2 * row] = b2[field][2 * row] + both
            a2[field][2 * row + 1] = b2[field][2 * row + 1] + both
    two.sweep(a2, right2, 0, rows2, 4, put_in(*b2))
    two.sweep(b2, right2, 0, rows2, 4, put_in(*a2))

    first2 = at_x * (own_rows // 2) - 2
    for field in range(2):
        for index in range(own_rows // 2 + 4):
            row = wrapped(first2 + index, rows2)
            spread_rows(spread2.at[field], index, a2[field][row])
            both = spread2[field, index]
            a1[field][2 * row] = b1[field][2 * row] + both
            a1[field][2 * row + 1] = b1[field][2 * row + 1] + both
    own_first = at_x * own_rows
    one.sweep(a1, right1, own_first - 2, own_rows + 4, 2, put_in(*b1))
    one.sweep(b1, right1, own_first - 1, own_rows + 2, 2, put_in(*a1))

    low = low_rows((8, lanes))
    fine_columns = 2 * own_columns
    for field, (source, target) in enumerate(((conc_in, fine_a0), (chem_in, fine_a1))):
        for index in range(own_rows + 2):
            row = wrapped(own_first - 1 + index, rows1)
            for side in range(3):
                column = lax.rem(at_y + slots_y + side - 1, slots_y) * own_columns
                tile = a1[field][row, pl.ds(pl.multiple_of(column, 8), own_columns), :]
                spread_rows(spread_fine.at[field, side], index, tile)
            rim = jnp.where(
                low,
                spread_fine[field, 2, index, :8],
                spread_fine[field, 0, index, fine_columns - 8 :],
            )
            both = jnp.concatenate([spread_fine[field, 1, index], rim], axis=0)
            for fine in (HALO - 2 + 2 * index, HALO - 1 + 2 * index):
                target[fine] = source[fine] + both
    fine = Level(0, (face_x, face_y, face_z, coupling, gain))
    right_side = (right_conc, right_chem)
    rows = conc_new.shape[0]
    fine.sweep(
        (fine_a0, fine_a1), right_side, HALO - 1, rows + 2, 2, put_in(fine_b0, fine_b1)
    )

    def put_new(row, conc_value, chem_value):
        conc_new[row - HALO] = conc_value[:fine_columns]
        chem_new[row - HALO] = chem_value[:fine_columns]

    fine.sweep((fine_b0, fine_b1), right_side, HALO, rows, 2, put_new)


def call_kernel(kernel, outs, scratch, *args, scalars=0):
    shapes = tuple(jax.ShapeDtypeStruct(shape, jnp.float32) for shape in outs)
    specs = [pl.BlockSpec(memory_space=pltpu.SMEM)] * scalars
    specs += [whole_block()] * (len(args) - scalars)
    return pl.pallas_call(
        kernel,
        out_shape=shapes,
        in_specs=specs,
        out_specs=tuple(whole_block() for _ in outs),
        scratch_shapes=[pltpu.VMEM(shape, jnp.float32) for shape in scratch],
        compiler_params=pltpu.CompilerParams(vmem_limit_bytes=40 * 1024 * 1024),
    )(*args)


def shifted(values, axis, by):
    count = lax.axis_size(axis)
    return lax.ppermute(values, axis, [(i, (i + by) % count) for i in range(count)])


def swapped(values, axis, mask):
    count = lax.axis_size(axis)
    return lax.ppermute(values, axis, [(i, i ^ mask) for i in range(count)])


def gathered(values):
    count_x, count_y = lax.axis_size("gx"), lax.axis_size("gy")
    stack = jnp.stack([values] + [swapped(values, "gx", mask) for mask in range(1, count_x)])
    stack = stack[None]
    for bit in reversed(range(count_y.bit_length() - 1)):
        stack = jnp.concatenate([stack, swapped(stack, "gy", 1 << bit)], axis=0)
    return stack


def two_phase_solve(conc, chem):
    rows, columns, lanes = conc.shape
    frame = (rows + 2 * HALO, columns + 8, lanes)
    edge = (2, HALO, columns, lanes)
    low, high = call_kernel(edge_rows_kernel, (edge, edge), (), conc, chem)
    before, after = shifted(high, "gx", 1), shifted(low, "gx", -1)
    side = (frame[0], 8, lanes)
    to_left, to_right = call_kernel(
        edge_columns_kernel, (side, side), (), conc, chem, before, after
    )
    from_left, from_right = shifted(to_right, "gy", 1), shifted(to_left, "gy", -1)
    packed_shape = (3, rows // 4, columns // 2, lanes)
    packed, *kept = call_kernel(
        fine_down_kernel,
        (packed_shape,) + (frame,) * 9,
        (frame,) * 4 + ((3, rows // 2, columns + 8, lanes),),
        conc, chem, before, after, from_left, from_right,
    )
    place = jnp.stack([lax.axis_index("gx"), lax.axis_index("gy")])
    count_x, count_y = lax.axis_size("gx"), lax.axis_size("gy")
    grids = [
        (count_x * rows >> level, count_y * columns >> level, lanes) for level in range(4)
    ]
    own_rows = rows // 2
    scratch = [grids[level] for level in (1, 2, 3) for _ in range(12)]
    scratch += [(3, grids[2][0], grids[1][1], lanes), (3, grids[3][0], grids[2][1], lanes)]
    scratch += [(2, own_rows // 2 + 4, grids[1][1], lanes), (2, grids[3][0], grids[2][1], lanes)]
    scratch += [(2, 3, own_rows + 2, columns, lanes)] + [frame] * 4
    block = (rows, columns, lanes)
    return call_kernel(
        coarse_kernel, (block, block), scratch, place, gathered(packed), *kept, scalars=1
    )


def body(conc_old, chem_old):
    rows, columns, lanes = conc_old.shape
    count_x, count_y = lax.axis_size("gx"), lax.axis_size("gy")
    grid_bytes = count_x * rows * count_y * columns * lanes
    if (
        grid_bytes <= GRID_BYTES_MAX
        and rows % 16 == 0
        and columns % 16 == 0
        and lanes % 128 == 0
        and count_x * rows >= 32
        and count_x & (count_x - 1) == 0
        and count_y & (count_y - 1) == 0
    ):
        return two_phase_solve(conc_old, chem_old)
    start_fields = jnp.stack([conc_old, chem_old])
    result = plain_solve(start_fields)
    return (result[0], result[1])


def solution(mesh):
    in_specs = (P(("img", "gx"), "gy", None), P(("img", "gx"), "gy", None))
    out_specs = (P(("img", "gx"), "gy", None), P(("img", "gx"), "gy", None))
    return jax.shard_map(body, mesh=mesh, in_specs=in_specs, out_specs=out_specs, check_vma=False)
```

```python
import jax
import jax.numpy as jnp
from jax import lax
from jax.experimental import pallas as pl
from jax.experimental.pallas import tpu as pltpu
from jax.sharding import PartitionSpec as P

LEVELS = 4
SWEEPS = 2
COARSE = 6


TIME_STEP = 32.0
GRADIENT_ENERGY = 0.5
STABILIZER = 2.0
DAMPING = 0.7


def extended(cells, sides, width):
    for axis, dim in sides:
        count = lax.axis_size(axis)
        head = lax.slice_in_dim(cells, 0, width, axis=dim)
        tail = lax.slice_in_dim(cells, cells.shape[dim] - width, cells.shape[dim], axis=dim)
        cells = jnp.concatenate(
            [
                lax.ppermute(tail, axis, [(i, (i + 1) % count) for i in range(count)]),
                cells,
                lax.ppermute(head, axis, [((i + 1) % count, i) for i in range(count)]),
            ],
            axis=dim,
        )
    return cells


def mobility_of(concentration):
    return 0.1 + jnp.square(1.0 - concentration * concentration)


def right_of(concentration):
    return jnp.stack(
        [
            concentration,
            concentration * concentration * concentration - (1.0 + STABILIZER) * concentration,
        ]
    )


def face_weights(mob_padded, level_scale):
    middle = mob_padded[1:-1, 1:-1, :]
    half_scale = 0.5 * level_scale
    weights = (
        half_scale * (middle + mob_padded[2:, 1:-1, :]),
        half_scale * (middle + mob_padded[:-2, 1:-1, :]),
        half_scale * (middle + mob_padded[1:-1, 2:, :]),
        half_scale * (middle + mob_padded[1:-1, :-2, :]),
        half_scale * (middle + jnp.roll(middle, -1, axis=2)),
        half_scale * (middle + jnp.roll(middle, 1, axis=2)),
    )
    total_weight = weights[0] + weights[1] + weights[2] + weights[3] + weights[4] + weights[5]
    return (weights, total_weight)


def neighbour_list(padded, middle):
    return (
        padded[2:, 1:-1, :],
        padded[:-2, 1:-1, :],
        padded[1:-1, 2:, :],
        padded[1:-1, :-2, :],
        jnp.roll(middle, -1, axis=2),
        jnp.roll(middle, 1, axis=2),
    )


def apply_operator(padded, weights, level_scale):
    middle = padded[:, 1:-1, 1:-1, :]
    conc_near = neighbour_list(padded[0], middle[0])
    chem_near = neighbour_list(padded[1], middle[1])
    flux = weights[0] * (chem_near[0] - middle[1])
    for position in range(1, 6):
        flux = flux + weights[position] * (chem_near[position] - middle[1])
    laplace = (
        conc_near[0]
        + conc_near[1]
        + conc_near[2]
        + conc_near[3]
        + conc_near[4]
        + conc_near[5]
        - 6.0 * middle[0]
    )
    first_eq = middle[0] - TIME_STEP * flux
    second_eq = middle[1] - STABILIZER * middle[0] + GRADIENT_ENERGY * level_scale * laplace
    return jnp.stack([first_eq, second_eq])


def update(residual, total_weight, level_scale):
    diagonal = STABILIZER + 6.0 * GRADIENT_ENERGY * level_scale
    coupling = TIME_STEP * total_weight
    determinant = 1.0 + coupling * diagonal
    conc_step = (residual[0] - coupling * residual[1]) / determinant
    chem_step = (residual[1] + diagonal * residual[0]) / determinant
    return DAMPING * jnp.stack([conc_step, chem_step])


def sweep_once(padded, right_side, mob_padded, level_scale):
    weights, total_weight = face_weights(mob_padded, level_scale)
    residual = right_side - apply_operator(padded, weights, level_scale)
    return padded[:, 1:-1, 1:-1, :] + update(residual, total_weight, level_scale)


def defect(padded, right_side, mob_padded, level_scale):
    weights = face_weights(mob_padded, level_scale)[0]
    return right_side - apply_operator(padded, weights, level_scale)


def coarsen(values):
    dims_now = values.shape
    grouped = values.reshape(
        dims_now[:-3] + (dims_now[-3] // 2, 2, dims_now[-2] // 2, 2, dims_now[-1] // 2, 2)
    )
    return jnp.sum(grouped, axis=(-5, -3, -1)) * 0.125


def refine(values):
    for axis_pos in (-3, -2, -1):
        values = jnp.repeat(values, 2, axis=axis_pos)
    return values


def trim_rim(values, width):
    return values[..., width:-width, width:-width, :]


def field_rim(fields):
    return extended(fields, (("gx", 1), ("gy", 2)), 1)


def coarsest_solve(right_side, mobility, level_scale):
    mob_padded = extended(mobility, (("gx", 0), ("gy", 1)), 1)
    fields = update(right_side, face_weights(mob_padded, level_scale)[1], level_scale)
    for sweep_index in range(COARSE - 1):
        padded = extended(fields, (("gx", 1), ("gy", 2)), 1)
        fields = sweep_once(padded, right_side, mob_padded, level_scale)
    return fields


def plain_solve(start_fields):
    outer_fields = field_rim(start_fields)
    mob_outer = mobility_of(outer_fields[0])
    mobility = trim_rim(mob_outer, 1)
    level_data = []
    for level_index in range(LEVELS - 1):
        if level_index == 0:
            mob_padded = mob_outer
        else:
            mob_padded = extended(mobility, (("gx", 0), ("gy", 1)), 1)
        level_data.append((mob_padded, 0.25**level_index))
        mobility = coarsen(mobility)
    coarsest_scale = 0.25 ** (LEVELS - 1)

    def cycle_level(level_index, right_side):
        if level_index == LEVELS - 1:
            return coarsest_solve(right_side, mobility, coarsest_scale)
        mob_padded, level_scale = level_data[level_index]
        if level_index == 0:
            fields = sweep_once(outer_fields, right_side, mob_padded, level_scale)
        else:
            fields = update(right_side, face_weights(mob_padded, level_scale)[1], level_scale)
        fields = sweep_once(field_rim(fields), right_side, mob_padded, level_scale)
        residual = defect(field_rim(fields), right_side, mob_padded, level_scale)
        fields = fields + refine(cycle_level(level_index + 1, coarsen(residual)))
        for sweep_index in range(SWEEPS):
            fields = sweep_once(field_rim(fields), right_side, mob_padded, level_scale)
        return fields

    return cycle_level(0, right_of(start_fields[0]))


HALO = 4
PAD = 8
GRID_BYTES_MAX = 2 * 1024 * 1024


def whole_block():
    return pl.BlockSpec(memory_space=pltpu.VMEM)


def lane_roll(values, shift):
    return pltpu.roll(values, shift % values.shape[1], axis=1)


def lane_even(shape, dup):
    return (lax.broadcasted_iota(jnp.int32, shape, 1) // dup) % 2 == 0


def loop_rows(count, unroll, row_group):
    steps, rest = divmod(count, unroll)
    if steps == 1:
        row_group(0, unroll)
    elif steps > 1:

        def step(index, carry):
            row_group(index * unroll, unroll)
            return carry

        lax.fori_loop(0, steps, step, 0)
    if rest:
        row_group(steps * unroll, rest)


def wrapped(row, count):
    if isinstance(row, int):
        return row % count
    return row & (count - 1) if count & (count - 1) == 0 else row


def chem_right(conc):
    return conc * (conc * conc - (1.0 + STABILIZER))


class Level:
    def __init__(self, level_index, weights, weights_from=PAD, right_from=PAD):
        self.scale = 0.25**level_index
        self.dup = 2**level_index
        self.diagonal = STABILIZER + 6.0 * GRADIENT_ENERGY * self.scale
        self.weights = weights
        self.weights_from, self.right_from = weights_from, right_from

    def set_weights(self, mobility, unroll):
        total, width = mobility.shape[0], self.weights[0].shape[1]
        half = 0.5 * self.scale * TIME_STEP
        face_x, up_y, down_y, up_z, down_z, coupling, gain = self.weights

        def at(row, shift=0):
            return mobility[row, pl.ds(self.weights_from + shift, width), :]

        def group(first, size):
            rows = [at(wrapped(first + i - 1, total)) for i in range(size + 2)]
            before = half * (rows[0] + rows[1])
            for i in range(size):
                r = first + i
                here = rows[i + 1]
                after = half * (here + rows[i + 2])
                to_up_y = half * (here + at(r, 1))
                to_down_y = half * (here + at(r, -1))
                to_up_z = half * (here + lane_roll(here, -self.dup))
                to_down_z = half * (here + lane_roll(here, self.dup))
                total_weight = (before + after) + (to_up_y + to_down_y) + (to_up_z + to_down_z)
                face_x[r] = after
                up_y[r] = to_up_y
                down_y[r] = to_down_y
                up_z[r] = to_up_z
                down_z[r] = to_down_z
                coupling[r] = total_weight
                gain[r] = DAMPING / (1.0 + total_weight * self.diagonal)
                before = after

        loop_rows(total, unroll, group)

    def residuals(self, fields, right, rows, window, fields_from=0):
        conc, chem = fields
        first, width = window
        face_x, up_y, down_y, up_z, down_z, coupling, gain = self.weights

        def at(ref, row, shift=0):
            return ref[row, pl.ds(first - fields_from + shift, width), :]

        def weight(ref, row):
            return ref[row, pl.ds(first - self.weights_from, width), :]

        def right_at(row):
            values = [ref[row, pl.ds(first - self.right_from, width), :] for ref in right]
            return values if len(values) == 2 else values + [chem_right(values[0])]

        u = [at(chem, row) for row in rows]
        c = [at(conc, row) for row in rows]
        for i in range(1, len(rows) - 1):
            r = rows[i]
            here = weight(coupling, r)
            flux = weight(face_x, r) * u[i + 1] + weight(face_x, rows[i - 1]) * u[i - 1]
            flux = flux + weight(up_y, r) * at(chem, r, 1) + weight(down_y, r) * at(chem, r, -1)
            flux = flux + weight(up_z, r) * lane_roll(u[i], -self.dup)
            flux = flux + weight(down_z, r) * lane_roll(u[i], self.dup)
            near = (c[i - 1] + c[i + 1]) + (at(conc, r, 1) + at(conc, r, -1))
            near = near + (lane_roll(c[i], self.dup) + lane_roll(c[i], -self.dup))
            conc_right, chem_right_here = right_at(r)
            conc_left = conc_right - c[i] + (flux - here * u[i])
            chem_left = chem_right_here - u[i] + self.diagonal * c[i]
            chem_left = chem_left - (GRADIENT_ENERGY * self.scale) * near
            yield r, c[i], u[i], conc_left, chem_left, here, weight(gain, r)

    def steps(self, conc_left, chem_left, coupling, gain):
        return (
            gain * (conc_left - coupling * chem_left),
            gain * (chem_left + self.diagonal * conc_left),
        )

    def first_sweep(self, right, unroll, put):
        coupling, gain = self.weights[5:]

        def group(first, size):
            for i in range(size):
                r = first + i
                put(r, *self.steps(right[0][r], right[1][r], coupling[r], gain[r]))

        loop_rows(right[0].shape[0], unroll, group)

    def row_window(self, total, start, first, size):
        return [wrapped(start + first + i - 1, total) for i in range(size + 2)]

    def sweep(self, fields, right, start, count, unroll, window, put):
        def group(first, size):
            rows = self.row_window(fields[0].shape[0], start, first, size)
            for r, c, u, *left in self.residuals(fields, right, rows, window):
                conc_step, chem_step = self.steps(*left)
                put(r, c + conc_step, u + chem_step)

        loop_rows(count, unroll, group)

    def coarse_right(self, fields, right, start, count, unroll, window, put, fields_from=0):
        def group(first, size):
            rows = self.row_window(fields[0].shape[0], start, first, size)
            items = self.residuals(fields, right, rows, window, fields_from)
            lefts = [item[3:5] for item in items]
            for i in range(0, size, 2):
                half = first // 2 if isinstance(first, int) else lax.shift_right_logical(first, 1)
                put(half + i // 2, *(a + b for a, b in zip(lefts[i], lefts[i + 1])))

        loop_rows(count, unroll, group)


def put_padded(refs):
    def put(row, *values):
        for ref, value in zip(refs, values):
            width = value.shape[0]
            ref[row, PAD : PAD + width, :] = value
            ref[row, :PAD, :] = value[width - PAD :]
            ref[row, PAD + width :, :] = value[:PAD]

    return put


def put_window(refs, window):
    def put(row, *values):
        for ref, value in zip(refs, values):
            ref[row, window[0] : window[0] + window[1], :] = value

    return put


def put_sums(sums):
    def put(row, *values):
        for field, value in enumerate(values):
            sums[field, row] = value

    return put


def pair_rows(ref, row, count):
    return ref[row, pl.ds(0, count, stride=2), :] + ref[row, pl.ds(1, count, stride=2), :]


def spread_rows(ref, row, values):
    count = values.shape[0]
    ref[row, pl.ds(0, count, stride=2), :] = values
    ref[row, pl.ds(1, count, stride=2), :] = values


def pair_lanes(values, dup):
    other = jnp.where(
        lane_even(values.shape, dup), lane_roll(values, -dup), lane_roll(values, dup)
    )
    return values + other


def edge_rows_kernel(fields, low, high):
    rows = fields.shape[1]
    low[...] = fields[:, :HALO]
    high[...] = fields[:, rows - HALO :]


def frame_row(row, rows, own, before, after):
    if row < HALO:
        return before[row]
    if row < HALO + rows:
        return own[row - HALO]
    return after[row - HALO - rows]


def half_turn(values):
    return pltpu.roll(values, HALO, axis=0)


def edge_columns_kernel(fields, before, after, to_left, to_right):
    conc, chem = fields.at[0], fields.at[1]
    rows, columns, lanes = conc.shape
    low = lax.broadcasted_iota(jnp.int32, (PAD, lanes), 0) < HALO
    for row in range(rows + 2 * HALO):
        c = frame_row(row, rows, conc, before.at[0], after.at[0])
        u = frame_row(row, rows, chem, before.at[1], after.at[1])
        to_left[row] = jnp.where(low, c[:PAD], half_turn(u[:PAD]))
        to_right[row] = jnp.where(low, half_turn(u[columns - PAD :]), c[columns - PAD :])


def fine_level(weights):
    return Level(0, weights, HALO, 0)


def fine_down_kernel(
    fields, before, after, from_left, from_right,
    packed, kept, right_conc, all_weights,
    chem_start, mobility, conc_mid, chem_mid, sums,
):
    conc, chem = fields.at[0], fields.at[1]
    conc_out, chem_out = kept.at[0], kept.at[1]
    weights = [all_weights.at[i] for i in range(7)]
    rows, columns, lanes = conc.shape
    frame = rows + 2 * HALO
    for row in range(frame):
        left, right = from_left[row], from_right[row]
        c = jnp.concatenate([left, frame_row(row, rows, conc, before.at[0], after.at[0]), right])
        own = frame_row(row, rows, chem, before.at[1], after.at[1])
        right_conc[row] = c
        chem_start[row] = jnp.concatenate([half_turn(left), own, half_turn(right)])
        gap = 1.0 - c * c
        mobility[row] = 0.1 + gap * gap
    level = fine_level(weights)
    level.set_weights(mobility, frame)
    right_side = (right_conc,)
    wide = (PAD - HALO, columns + 2 * HALO)
    level.sweep(
        (right_conc, chem_start), right_side, 1, frame - 2, 11, wide,
        put_window((conc_mid, chem_mid), wide),
    )
    level.sweep(
        (conc_mid, chem_mid), right_side, 2, frame - 4, 10, wide,
        put_window((conc_out, chem_out), (0, wide[1])),
    )
    level.coarse_right(
        (conc_out, chem_out), right_side, HALO, rows, 8, (PAD, columns), put_sums(sums), wide[0]
    )
    for index in range(rows // 2):
        row = HALO + 2 * index
        own = slice(PAD, PAD + columns)
        sums[2, index] = mobility[row, own, :] + mobility[row + 1, own, :]
    even = lane_even((columns // 2, lanes), 1)
    for field in range(3):
        for index in range(rows // 4):
            a = pair_rows(sums.at[field], 2 * index, columns // 2)
            b = pair_rows(sums.at[field], 2 * index + 1, columns // 2)
            packed[field, index] = 0.125 * jnp.where(
                even, a + lane_roll(a, -1), b + lane_roll(b, 1)
            )


def coarse_kernel(
    place, near, far, kept, right_conc, all_weights, conc_new, chem_new, *scratch
):
    conc_in, chem_in = kept.at[0], kept.at[1]
    weights = [all_weights.at[i] for i in range(7)]
    scratch = list(scratch)
    at_x, at_y = place[0], place[1]
    levels = []
    for level_index in (1, 2, 3):
        level = Level(level_index, scratch[5:14][2:])
        mobility, a, b, right = scratch[0], scratch[1:3], scratch[3:5], scratch[5:7]
        levels.append((level, mobility, right, a, b))
        del scratch[:14]
    sums1, sums2, spread2, spread3, spread_fine, fine_a0, fine_a1, fine_b0, fine_b1 = scratch
    one, mob1, right1, a1, b1 = levels[0]
    two, mob2, right2, a2, b2 = levels[1]
    three, mob3, right3, a3, b3 = levels[2]
    rows1, columns1, lanes = right1[0].shape
    rows2, columns2 = right2[0].shape[:2]
    rows3, columns3 = right3[0].shape[:2]
    window1, window2, window3 = (PAD, columns1), (PAD, columns2), (PAD, columns3)
    slots_x, slots_y = near.shape[1], 2 * near.shape[0]
    own_rows, own_columns = rows1 // slots_x, columns1 // slots_y
    even = lane_even((own_columns, lanes), 1)
    bits = slots_y.bit_length() - 1

    def unpack(source, slot_y, from_y):
        offset = from_y * own_columns
        plain = pl.ds(pl.multiple_of(offset, PAD), own_columns)
        padded = pl.ds(pl.multiple_of(offset + PAD, PAD), own_columns)
        for slot_x in range(slots_x):
            row = (at_x ^ slot_x) * own_rows
            for field, (ref, at) in enumerate(
                ((right1[0], plain), (right1[1], plain), (mob1, padded))
            ):
                for index in range(own_rows // 2):
                    pair = source[slot_y, slot_x, field, index]
                    ref[row + 2 * index, at, :] = jnp.where(even, pair, lane_roll(pair, 1))
                    ref[row + 2 * index + 1, at, :] = jnp.where(even, lane_roll(pair, -1), pair)

    for last, source in enumerate((near, far)):
        for slot_y in range(slots_y // 2):
            mask = last
            for bit in range(bits - 1):
                mask |= (slot_y >> bit & 1) << (bits - 1 - bit)
            unpack(source, slot_y, at_y ^ mask)
    for row in range(rows1):
        mob1[row, :PAD, :] = mob1[row, columns1 : columns1 + PAD, :]
        mob1[row, PAD + columns1 :, :] = mob1[row, PAD : 2 * PAD, :]

    def coarsen(mobility, sums, out, out_mobility, dup):
        count, columns = out[0].shape[:2]
        fine = pl.ds(PAD, 2 * columns)
        for index in range(count):
            sums[2, index] = mobility[2 * index, fine, :] + mobility[2 * index + 1, fine, :]
        for index in range(count):
            for field in range(2):
                half = pair_rows(sums.at[field], index, columns)
                out[field][index] = 0.125 * pair_lanes(half, dup)
            half = pair_rows(sums.at[2], index, columns)
            put_padded((out_mobility,))(index, 0.125 * pair_lanes(half, dup))

    one.set_weights(mob1, 16)
    one.first_sweep(right1, 16, put_padded(a1))
    one.sweep(a1, right1, 0, rows1, 16, window1, put_padded(b1))
    one.coarse_right(b1, right1, 0, rows1, 16, window1, put_sums(sums1))
    coarsen(mob1, sums1, right2, mob2, 2)

    two.set_weights(mob2, 16)
    two.first_sweep(right2, 16, put_padded(a2))
    two.sweep(a2, right2, 0, rows2, 16, window2, put_padded(b2))
    two.coarse_right(b2, right2, 0, rows2, 16, window2, put_sums(sums2))
    coarsen(mob2, sums2, right3, mob3, 4)

    three.set_weights(mob3, rows3)
    three.first_sweep(right3, rows3, put_padded(a3))
    now, other = a3, b3
    for sweep_index in range(COARSE - 1):
        three.sweep(now, right3, 0, rows3, rows3, window3, put_padded(other))
        now, other = other, now

    def correct(coarse, coarse_row, fine_in, fine_out, spread, index):
        for field in range(2):
            columns = fine_in[field].shape[1] - 2 * PAD
            spread_rows(
                spread.at[field], index, coarse[field][coarse_row, pl.ds(PAD, columns // 2), :]
            )
            both = spread[field, index]
            for row in (2 * coarse_row, 2 * coarse_row + 1):
                put_padded((fine_out[field],))(
                    row, fine_in[field][row, pl.ds(PAD, columns), :] + both
                )

    for row in range(rows3):
        correct(now, row, b2, a2, spread3, row)
    two.sweep(a2, right2, 0, rows2, 16, window2, put_padded(b2))
    two.sweep(b2, right2, 0, rows2, 16, window2, put_padded(a2))
    for index in range(own_rows // 2 + 4):
        row = wrapped(at_x * (own_rows // 2) - 2 + index, rows2)
        correct(a2, row, b1, a1, spread2, index)
    own_first = at_x * own_rows
    one.sweep(a1, right1, own_first - 2, own_rows + 4, 12, window1, put_padded(b1))
    one.sweep(b1, right1, own_first - 1, own_rows + 2, 10, window1, put_padded(a1))

    rows, columns = conc_new.shape[:2]
    wide = (PAD - HALO, columns + 2 * HALO)
    near_own = pl.ds(pl.multiple_of(at_y * own_columns, PAD), own_columns + 2 * PAD)
    for index in range(own_rows + 2):
        row = wrapped(own_first - 1 + index, rows1)
        for field, (source, target) in enumerate(((conc_in, fine_a0), (chem_in, fine_a1))):
            spread_rows(spread_fine.at[field], index, a1[field][row, near_own, :])
            both = spread_fine[field, index, pl.ds(wide[0] + PAD, wide[1]), :]
            for fine in (HALO - 2 + 2 * index, HALO - 1 + 2 * index):
                put_window((target,), wide)(fine, source[fine] + both)
    fine = fine_level(weights)
    right_side = (right_conc,)
    fine.sweep(
        (fine_a0, fine_a1), right_side, HALO - 1, rows + 2, 9, wide,
        put_window((fine_b0, fine_b1), wide),
    )

    def put_new(row, conc_value, chem_value):
        conc_new[row - HALO] = conc_value
        chem_new[row - HALO] = chem_value

    fine.sweep((fine_b0, fine_b1), right_side, HALO, rows, 8, (PAD, columns), put_new)


def call_kernel(kernel, outs, scratch, *args, specs=None, vmem_mib=8):
    shapes = tuple(jax.ShapeDtypeStruct(shape, jnp.float32) for shape in outs)
    scratch = [pltpu.VMEM(shape, jnp.float32) if isinstance(shape, tuple) else shape for shape in scratch]
    return pl.pallas_call(
        kernel,
        out_shape=shapes,
        in_specs=specs or [whole_block()] * len(args),
        out_specs=tuple(whole_block() for _ in outs),
        scratch_shapes=scratch,
        compiler_params=pltpu.CompilerParams(vmem_limit_bytes=vmem_mib * 1024 * 1024),
    )(*args)


def shifted(values, axis, by):
    count = lax.axis_size(axis)
    return lax.ppermute(values, axis, [(i, (i + by) % count) for i in range(count)])


def swapped(values, axis, mask):
    count = lax.axis_size(axis)
    return lax.ppermute(values, axis, [(i, i ^ mask) for i in range(count)])


def gathered(values):
    count_x, count_y = lax.axis_size("gx"), lax.axis_size("gy")
    stack = jnp.stack([values] + [swapped(values, "gx", mask) for mask in range(1, count_x)])
    stack = stack[None]
    for bit in reversed(range(1, count_y.bit_length() - 1)):
        stack = jnp.concatenate([stack, swapped(stack, "gy", 1 << bit)], axis=0)
    return stack, swapped(stack, "gy", 1)


def two_phase_solve(conc, chem):
    rows, columns, lanes = conc.shape
    frame = (rows + 2 * HALO, columns + 2 * PAD, lanes)
    inner = (frame[0], columns + 2 * HALO, lanes)
    edge = (2, HALO, columns, lanes)
    block = (rows, columns, lanes)
    fields = jnp.concatenate([conc, chem], axis=0).reshape((2,) + block)
    low, high = call_kernel(edge_rows_kernel, (edge, edge), (), fields)
    before, after = shifted(high, "gx", 1), shifted(low, "gx", -1)
    side = (frame[0], PAD, lanes)
    to_left, to_right = call_kernel(
        edge_columns_kernel, (side, side), (), fields, before, after
    )
    from_left, from_right = shifted(to_right, "gy", 1), shifted(to_left, "gy", -1)
    packed, *kept = call_kernel(
        fine_down_kernel,
        ((3, rows // 4, columns // 2, lanes), (2,) + inner, frame, (7,) + inner),
        (frame,) * 4 + ((3, rows // 2, columns, lanes),),
        fields, before, after, from_left, from_right,
    )
    place = jnp.stack([lax.axis_index("gx"), lax.axis_index("gy")])
    count_x, count_y = lax.axis_size("gx"), lax.axis_size("gy")
    grids = [(count_x * rows >> level, count_y * columns >> level) for level in range(4)]
    scratch = []
    for level_rows, level_columns in grids[1:]:
        scratch += [(level_rows, level_columns + 2 * PAD, lanes)] * 5
        scratch += [(level_rows, level_columns, lanes)] * 9
    scratch += [(3, grids[2][0], grids[1][1], lanes), (3, grids[3][0], grids[2][1], lanes)]
    scratch += [(2, rows // 4 + 4, grids[1][1], lanes), (2, grids[3][0], grids[2][1], lanes)]
    scratch += [(2, rows // 2 + 2, columns + 4 * PAD, lanes)] + [frame] * 4
    args = (place, *gathered(packed), *kept)
    specs = [pl.BlockSpec(memory_space=pltpu.SMEM)] + [whole_block()] * (len(args) - 1)
    return call_kernel(coarse_kernel, (block, block), scratch, *args, specs=specs, vmem_mib=24)


def body(conc_old, chem_old):
    rows, columns, lanes = conc_old.shape
    count_x, count_y = lax.axis_size("gx"), lax.axis_size("gy")
    grid_bytes = count_x * rows * count_y * columns * lanes
    if (
        grid_bytes <= GRID_BYTES_MAX
        and rows % 16 == 0
        and columns % 16 == 0
        and lanes % 128 == 0
        and count_x * rows >= 64
        and count_y * columns >= 64
        and count_y >= 2
        and count_x & (count_x - 1) == 0
        and count_y & (count_y - 1) == 0
        and rows & (rows - 1) == 0
        and columns & (columns - 1) == 0
    ):
        return two_phase_solve(conc_old, chem_old)
    start_fields = jnp.stack([conc_old, chem_old])
    result = plain_solve(start_fields)
    return (result[0], result[1])


def solution(mesh):
    in_specs = (P(("img", "gx"), "gy", None), P(("img", "gx"), "gy", None))
    out_specs = (P(("img", "gx"), "gy", None), P(("img", "gx"), "gy", None))
    return jax.shard_map(body, mesh=mesh, in_specs=in_specs, out_specs=out_specs, check_vma=False)
```

```python
import functools

import jax
import jax.numpy as jnp
from jax import lax
from jax.experimental import pallas as pl
from jax.experimental.pallas import tpu as pltpu
from jax.sharding import PartitionSpec as P

LEVELS = 4
SWEEPS = 2
COARSE = 6


TIME_STEP = 32.0
GRADIENT_ENERGY = 0.5
STABILIZER = 2.0
DAMPING = 0.7


def extended(cells, sides, width):
    for axis, dim in sides:
        count = lax.axis_size(axis)
        head = lax.slice_in_dim(cells, 0, width, axis=dim)
        tail = lax.slice_in_dim(cells, cells.shape[dim] - width, cells.shape[dim], axis=dim)
        cells = jnp.concatenate(
            [
                lax.ppermute(tail, axis, [(i, (i + 1) % count) for i in range(count)]),
                cells,
                lax.ppermute(head, axis, [((i + 1) % count, i) for i in range(count)]),
            ],
            axis=dim,
        )
    return cells


def mobility_of(concentration):
    return 0.1 + jnp.square(1.0 - concentration * concentration)


def right_of(concentration):
    return jnp.stack(
        [
            concentration,
            concentration * concentration * concentration - (1.0 + STABILIZER) * concentration,
        ]
    )


def face_weights(mob_padded, level_scale):
    middle = mob_padded[1:-1, 1:-1, :]
    half_scale = 0.5 * level_scale
    weights = (
        half_scale * (middle + mob_padded[2:, 1:-1, :]),
        half_scale * (middle + mob_padded[:-2, 1:-1, :]),
        half_scale * (middle + mob_padded[1:-1, 2:, :]),
        half_scale * (middle + mob_padded[1:-1, :-2, :]),
        half_scale * (middle + jnp.roll(middle, -1, axis=2)),
        half_scale * (middle + jnp.roll(middle, 1, axis=2)),
    )
    total_weight = weights[0] + weights[1] + weights[2] + weights[3] + weights[4] + weights[5]
    return (weights, total_weight)


def neighbour_list(padded, middle):
    return (
        padded[2:, 1:-1, :],
        padded[:-2, 1:-1, :],
        padded[1:-1, 2:, :],
        padded[1:-1, :-2, :],
        jnp.roll(middle, -1, axis=2),
        jnp.roll(middle, 1, axis=2),
    )


def apply_operator(padded, weights, level_scale):
    middle = padded[:, 1:-1, 1:-1, :]
    conc_near = neighbour_list(padded[0], middle[0])
    chem_near = neighbour_list(padded[1], middle[1])
    flux = weights[0] * (chem_near[0] - middle[1])
    for position in range(1, 6):
        flux = flux + weights[position] * (chem_near[position] - middle[1])
    laplace = (
        conc_near[0]
        + conc_near[1]
        + conc_near[2]
        + conc_near[3]
        + conc_near[4]
        + conc_near[5]
        - 6.0 * middle[0]
    )
    first_eq = middle[0] - TIME_STEP * flux
    second_eq = middle[1] - STABILIZER * middle[0] + GRADIENT_ENERGY * level_scale * laplace
    return jnp.stack([first_eq, second_eq])


def update(residual, total_weight, level_scale):
    diagonal = STABILIZER + 6.0 * GRADIENT_ENERGY * level_scale
    coupling = TIME_STEP * total_weight
    determinant = 1.0 + coupling * diagonal
    conc_step = (residual[0] - coupling * residual[1]) / determinant
    chem_step = (residual[1] + diagonal * residual[0]) / determinant
    return DAMPING * jnp.stack([conc_step, chem_step])


def sweep_once(padded, right_side, mob_padded, level_scale):
    weights, total_weight = face_weights(mob_padded, level_scale)
    residual = right_side - apply_operator(padded, weights, level_scale)
    return padded[:, 1:-1, 1:-1, :] + update(residual, total_weight, level_scale)


def defect(padded, right_side, mob_padded, level_scale):
    weights = face_weights(mob_padded, level_scale)[0]
    return right_side - apply_operator(padded, weights, level_scale)


def coarsen(values):
    dims_now = values.shape
    grouped = values.reshape(
        dims_now[:-3] + (dims_now[-3] // 2, 2, dims_now[-2] // 2, 2, dims_now[-1] // 2, 2)
    )
    return jnp.sum(grouped, axis=(-5, -3, -1)) * 0.125


def refine(values):
    for axis_pos in (-3, -2, -1):
        values = jnp.repeat(values, 2, axis=axis_pos)
    return values


def trim_rim(values, width):
    return values[..., width:-width, width:-width, :]


def field_rim(fields):
    return extended(fields, (("gx", 1), ("gy", 2)), 1)


def coarsest_solve(right_side, mobility, level_scale):
    mob_padded = extended(mobility, (("gx", 0), ("gy", 1)), 1)
    fields = update(right_side, face_weights(mob_padded, level_scale)[1], level_scale)
    for sweep_index in range(COARSE - 1):
        padded = extended(fields, (("gx", 1), ("gy", 2)), 1)
        fields = sweep_once(padded, right_side, mob_padded, level_scale)
    return fields


def plain_solve(start_fields):
    outer_fields = field_rim(start_fields)
    mob_outer = mobility_of(outer_fields[0])
    mobility = trim_rim(mob_outer, 1)
    level_data = []
    for level_index in range(LEVELS - 1):
        if level_index == 0:
            mob_padded = mob_outer
        else:
            mob_padded = extended(mobility, (("gx", 0), ("gy", 1)), 1)
        level_data.append((mob_padded, 0.25**level_index))
        mobility = coarsen(mobility)
    coarsest_scale = 0.25 ** (LEVELS - 1)

    def cycle_level(level_index, right_side):
        if level_index == LEVELS - 1:
            return coarsest_solve(right_side, mobility, coarsest_scale)
        mob_padded, level_scale = level_data[level_index]
        if level_index == 0:
            fields = sweep_once(outer_fields, right_side, mob_padded, level_scale)
        else:
            fields = update(right_side, face_weights(mob_padded, level_scale)[1], level_scale)
        fields = sweep_once(field_rim(fields), right_side, mob_padded, level_scale)
        residual = defect(field_rim(fields), right_side, mob_padded, level_scale)
        fields = fields + refine(cycle_level(level_index + 1, coarsen(residual)))
        for sweep_index in range(SWEEPS):
            fields = sweep_once(field_rim(fields), right_side, mob_padded, level_scale)
        return fields

    return cycle_level(0, right_of(start_fields[0]))


HALO = 4
PAD = 8
GRID_BYTES_MAX = 2 * 1024 * 1024


def whole_block():
    return pl.BlockSpec(memory_space=pltpu.VMEM)


def lane_roll(values, shift):
    return pltpu.roll(values, shift % values.shape[1], axis=1)


def lane_even(shape, dup):
    return (lax.broadcasted_iota(jnp.int32, shape, 1) // dup) % 2 == 0


def loop_rows(count, unroll, row_group):
    steps, rest = divmod(count, unroll)
    if steps == 1:
        row_group(0, unroll)
    elif steps > 1:

        def step(index, carry):
            row_group(index * unroll, unroll)
            return carry

        lax.fori_loop(0, steps, step, 0)
    if rest:
        row_group(steps * unroll, rest)


def wrapped(row, count):
    if isinstance(row, int):
        return row % count
    return row & (count - 1) if count & (count - 1) == 0 else row


def chem_right(conc):
    return conc * (conc * conc - (1.0 + STABILIZER))


class Level:
    def __init__(self, level_index, weights, weights_from=PAD, right_from=PAD):
        self.scale = 0.25**level_index
        self.dup = 2**level_index
        self.diagonal = STABILIZER + 6.0 * GRADIENT_ENERGY * self.scale
        self.weights = weights
        self.weights_from, self.right_from = weights_from, right_from

    def set_weights(self, mobility, unroll):
        total, width = mobility.shape[0], self.weights[0].shape[1]
        half = 0.5 * self.scale * TIME_STEP
        face_x, up_y, down_y, up_z, down_z, coupling, gain = self.weights

        def at(row, shift=0):
            return mobility[row, pl.ds(self.weights_from + shift, width), :]

        def group(first, size):
            rows = [at(wrapped(first + i - 1, total)) for i in range(size + 2)]
            before = half * (rows[0] + rows[1])
            for i in range(size):
                r = first + i
                here = rows[i + 1]
                after = half * (here + rows[i + 2])
                to_up_y = half * (here + at(r, 1))
                to_down_y = half * (here + at(r, -1))
                to_up_z = half * (here + lane_roll(here, -self.dup))
                to_down_z = half * (here + lane_roll(here, self.dup))
                total_weight = (before + after) + (to_up_y + to_down_y) + (to_up_z + to_down_z)
                face_x[r] = after
                up_y[r] = to_up_y
                down_y[r] = to_down_y
                up_z[r] = to_up_z
                down_z[r] = to_down_z
                coupling[r] = total_weight
                gain[r] = DAMPING / (1.0 + total_weight * self.diagonal)
                before = after

        loop_rows(total, unroll, group)

    def residuals(self, fields, right, rows, window, fields_from=0):
        conc, chem = fields
        first, width = window
        face_x, up_y, down_y, up_z, down_z, coupling, gain = self.weights

        def at(ref, row, shift=0):
            return ref[row, pl.ds(first - fields_from + shift, width), :]

        def weight(ref, row):
            return ref[row, pl.ds(first - self.weights_from, width), :]

        def right_at(row):
            values = [ref[row, pl.ds(first - self.right_from, width), :] for ref in right]
            return values if len(values) == 2 else values + [chem_right(values[0])]

        u = [at(chem, row) for row in rows]
        c = [at(conc, row) for row in rows]
        for i in range(1, len(rows) - 1):
            r = rows[i]
            here = weight(coupling, r)
            flux = weight(face_x, r) * u[i + 1] + weight(face_x, rows[i - 1]) * u[i - 1]
            flux = flux + weight(up_y, r) * at(chem, r, 1) + weight(down_y, r) * at(chem, r, -1)
            flux = flux + weight(up_z, r) * lane_roll(u[i], -self.dup)
            flux = flux + weight(down_z, r) * lane_roll(u[i], self.dup)
            near = (c[i - 1] + c[i + 1]) + (at(conc, r, 1) + at(conc, r, -1))
            near = near + (lane_roll(c[i], self.dup) + lane_roll(c[i], -self.dup))
            conc_right, chem_right_here = right_at(r)
            conc_left = conc_right - c[i] + (flux - here * u[i])
            chem_left = chem_right_here - u[i] + self.diagonal * c[i]
            chem_left = chem_left - (GRADIENT_ENERGY * self.scale) * near
            yield r, c[i], u[i], conc_left, chem_left, here, weight(gain, r)

    def steps(self, conc_left, chem_left, coupling, gain):
        return (
            gain * (conc_left - coupling * chem_left),
            gain * (chem_left + self.diagonal * conc_left),
        )

    def first_sweep(self, right, unroll, put):
        coupling, gain = self.weights[5:]

        def group(first, size):
            for i in range(size):
                r = first + i
                put(r, *self.steps(right[0][r], right[1][r], coupling[r], gain[r]))

        loop_rows(right[0].shape[0], unroll, group)

    def row_window(self, total, start, first, size):
        return [wrapped(start + first + i - 1, total) for i in range(size + 2)]

    def sweep(self, fields, right, start, count, unroll, window, put):
        def group(first, size):
            rows = self.row_window(fields[0].shape[0], start, first, size)
            for r, c, u, *left in self.residuals(fields, right, rows, window):
                conc_step, chem_step = self.steps(*left)
                put(r, c + conc_step, u + chem_step)

        loop_rows(count, unroll, group)

    def coarse_right(self, fields, right, start, count, unroll, window, put, fields_from=0):
        def group(first, size):
            rows = self.row_window(fields[0].shape[0], start, first, size)
            items = self.residuals(fields, right, rows, window, fields_from)
            lefts = [item[3:5] for item in items]
            for i in range(0, size, 2):
                half = first // 2 if isinstance(first, int) else lax.shift_right_logical(first, 1)
                put(half + i // 2, *(a + b for a, b in zip(lefts[i], lefts[i + 1])))

        loop_rows(count, unroll, group)


def put_padded(refs):
    def put(row, *values):
        for ref, value in zip(refs, values):
            width = value.shape[0]
            ref[row, PAD : PAD + width, :] = value
            ref[row, :PAD, :] = value[width - PAD :]
            ref[row, PAD + width :, :] = value[:PAD]

    return put


def put_window(refs, window):
    def put(row, *values):
        for ref, value in zip(refs, values):
            ref[row, window[0] : window[0] + window[1], :] = value

    return put


def put_sums(sums):
    def put(row, *values):
        for field, value in enumerate(values):
            sums[field, row] = value

    return put


def pair_rows(ref, row, count):
    return ref[row, pl.ds(0, count, stride=2), :] + ref[row, pl.ds(1, count, stride=2), :]


def spread_rows(ref, row, values):
    count = values.shape[0]
    ref[row, pl.ds(0, count, stride=2), :] = values
    ref[row, pl.ds(1, count, stride=2), :] = values


def pair_lanes(values, dup):
    other = jnp.where(
        lane_even(values.shape, dup), lane_roll(values, -dup), lane_roll(values, dup)
    )
    return values + other


def side_tiles(conc, chem, to_left, to_right, at, low):
    columns = conc.shape[0]
    to_left[at] = jnp.where(low, conc[:PAD], half_turn(chem[:PAD]))
    to_right[at] = jnp.where(low, half_turn(chem[columns - PAD :]), conc[columns - PAD :])


def low_half(lanes):
    return lax.broadcasted_iota(jnp.int32, (PAD, lanes), 0) < HALO


def edges_kernel(fields, low_rows, high_rows, to_left, to_right):
    rows, columns, lanes = fields.shape[1:]
    low_rows[...] = fields[:, :HALO]
    high_rows[...] = fields[:, rows - HALO :]
    for row in range(rows):
        side_tiles(fields[0, row], fields[1, row], to_left, to_right, row, low_half(lanes))


def corners_kernel(before, after, to_left, to_right):
    lanes = before.shape[-1]
    for at in range(2 * HALO):
        source, row = (before, at) if at < HALO else (after, at - HALO)
        side_tiles(source[0, row], source[1, row], to_left, to_right, at, low_half(lanes))


def frame_row(row, rows, own, before, after):
    if row < HALO:
        return before[row]
    if row < HALO + rows:
        return own[row - HALO]
    return after[row - HALO - rows]


def half_turn(values):
    return pltpu.roll(values, HALO, axis=0)


def side_row(row, rows, own, corners):
    if row < HALO:
        return corners[row]
    if row < HALO + rows:
        return own[row - HALO]
    return corners[row - rows]


def fine_level(weights):
    return Level(0, weights, HALO, 0)


def fine_down_kernel(
    fields, before, after, own_left, own_right, corner_left, corner_right,
    packed, kept, right_conc, all_weights,
    chem_start, mobility, conc_mid, chem_mid, sums,
):
    conc, chem = fields.at[0], fields.at[1]
    conc_out, chem_out = kept.at[0], kept.at[1]
    weights = [all_weights.at[i] for i in range(7)]
    rows, columns, lanes = conc.shape
    frame = rows + 2 * HALO
    for row in range(frame):
        left = side_row(row, rows, own_left, corner_left)
        right = side_row(row, rows, own_right, corner_right)
        c = jnp.concatenate([left, frame_row(row, rows, conc, before.at[0], after.at[0]), right])
        own = frame_row(row, rows, chem, before.at[1], after.at[1])
        right_conc[row] = c
        chem_start[row] = jnp.concatenate([half_turn(left), own, half_turn(right)])
        gap = 1.0 - c * c
        mobility[row] = 0.1 + gap * gap
    level = fine_level(weights)
    level.set_weights(mobility, frame)
    right_side = (right_conc,)
    wide = (PAD - HALO, columns + 2 * HALO)
    level.sweep(
        (right_conc, chem_start), right_side, 1, frame - 2, 11, wide,
        put_window((conc_mid, chem_mid), wide),
    )
    level.sweep(
        (conc_mid, chem_mid), right_side, 2, frame - 4, 10, wide,
        put_window((conc_out, chem_out), (0, wide[1])),
    )
    level.coarse_right(
        (conc_out, chem_out), right_side, HALO, rows, 8, (PAD, columns), put_sums(sums), wide[0]
    )
    for index in range(rows // 2):
        row = HALO + 2 * index
        own = slice(PAD, PAD + columns)
        sums[2, index] = mobility[row, own, :] + mobility[row + 1, own, :]
    even = lane_even((columns // 2, lanes), 1)
    for field in range(3):
        for index in range(rows // 4):
            a = pair_rows(sums.at[field], 2 * index, columns // 2)
            b = pair_rows(sums.at[field], 2 * index + 1, columns // 2)
            packed[field, index] = 0.125 * jnp.where(
                even, a + lane_roll(a, -1), b + lane_roll(b, 1)
            )


def coarse_kernel(
    slots, grid, place, first, second, first_far, second_far,
    kept, right_conc, all_weights, conc_new, chem_new, *scratch,
):
    conc_in, chem_in = kept.at[0], kept.at[1]
    weights = [all_weights.at[i] for i in range(7)]
    scratch = list(scratch)
    at_x, at_y = place[0], place[1]
    levels = []
    for level_index in (1, 2, 3):
        level = Level(level_index, scratch[5:14][2:])
        mobility, a, b, right = scratch[0], scratch[1:3], scratch[3:5], scratch[5:7]
        levels.append((level, mobility, right, a, b))
        del scratch[:14]
    sums1, sums2, spread2, spread3, spread_fine, fine_a0, fine_a1, fine_b0, fine_b1 = scratch
    one, mob1, right1, a1, b1 = levels[0]
    two, mob2, right2, a2, b2 = levels[1]
    three, mob3, right3, a3, b3 = levels[2]
    rows1, columns1, lanes = right1[0].shape
    rows2, columns2 = right2[0].shape[:2]
    rows3, columns3 = right3[0].shape[:2]
    window1, window2, window3 = (PAD, columns1), (PAD, columns2), (PAD, columns3)
    own_rows, own_columns = rows1 // grid[0], columns1 // grid[1]
    even = lane_even((own_columns, lanes), 1)

    def unpack(source, slot, mask_x, mask_y):
        offset = (at_y ^ mask_y) * own_columns
        plain = pl.ds(pl.multiple_of(offset, PAD), own_columns)
        padded = pl.ds(pl.multiple_of(offset + PAD, PAD), own_columns)
        row = (at_x ^ mask_x) * own_rows
        for field, (ref, at) in enumerate(
            ((right1[0], plain), (right1[1], plain), (mob1, padded))
        ):
            for index in range(own_rows // 2):
                pair = source[slot, field, index]
                ref[row + 2 * index, at, :] = jnp.where(even, pair, lane_roll(pair, 1))
                ref[row + 2 * index + 1, at, :] = jnp.where(even, lane_roll(pair, -1), pair)

    for last, sources in enumerate(((first, second), (first_far, second_far))):
        for source, masks in zip(sources, slots):
            for slot, (mask_x, mask_y) in enumerate(masks):
                unpack(source, slot, mask_x, mask_y ^ last)
    for row in range(rows1):
        mob1[row, :PAD, :] = mob1[row, columns1 : columns1 + PAD, :]
        mob1[row, PAD + columns1 :, :] = mob1[row, PAD : 2 * PAD, :]

    def coarsen(mobility, sums, out, out_mobility, dup):
        count, columns = out[0].shape[:2]
        fine = pl.ds(PAD, 2 * columns)
        for index in range(count):
            sums[2, index] = mobility[2 * index, fine, :] + mobility[2 * index + 1, fine, :]
        for index in range(count):
            for field in range(2):
                half = pair_rows(sums.at[field], index, columns)
                out[field][index] = 0.125 * pair_lanes(half, dup)
            half = pair_rows(sums.at[2], index, columns)
            put_padded((out_mobility,))(index, 0.125 * pair_lanes(half, dup))

    one.set_weights(mob1, 16)
    one.first_sweep(right1, 16, put_padded(a1))
    one.sweep(a1, right1, 0, rows1, 16, window1, put_padded(b1))
    one.coarse_right(b1, right1, 0, rows1, 16, window1, put_sums(sums1))
    coarsen(mob1, sums1, right2, mob2, 2)

    two.set_weights(mob2, 16)
    two.first_sweep(right2, 16, put_padded(a2))
    two.sweep(a2, right2, 0, rows2, 16, window2, put_padded(b2))
    two.coarse_right(b2, right2, 0, rows2, 16, window2, put_sums(sums2))
    coarsen(mob2, sums2, right3, mob3, 4)

    three.set_weights(mob3, rows3)
    three.first_sweep(right3, rows3, put_padded(a3))
    now, other = a3, b3
    for sweep_index in range(COARSE - 1):
        three.sweep(now, right3, 0, rows3, rows3, window3, put_padded(other))
        now, other = other, now

    def correct(coarse, coarse_row, fine_in, fine_out, spread, index):
        for field in range(2):
            columns = fine_in[field].shape[1] - 2 * PAD
            spread_rows(
                spread.at[field], index, coarse[field][coarse_row, pl.ds(PAD, columns // 2), :]
            )
            both = spread[field, index]
            for row in (2 * coarse_row, 2 * coarse_row + 1):
                put_padded((fine_out[field],))(
                    row, fine_in[field][row, pl.ds(PAD, columns), :] + both
                )

    for row in range(rows3):
        correct(now, row, b2, a2, spread3, row)
    two.sweep(a2, right2, 0, rows2, 16, window2, put_padded(b2))
    two.sweep(b2, right2, 0, rows2, 16, window2, put_padded(a2))
    for index in range(own_rows // 2 + 4):
        row = wrapped(at_x * (own_rows // 2) - 2 + index, rows2)
        correct(a2, row, b1, a1, spread2, index)
    own_first = at_x * own_rows
    one.sweep(a1, right1, own_first - 2, own_rows + 4, 12, window1, put_padded(b1))
    one.sweep(b1, right1, own_first - 1, own_rows + 2, 10, window1, put_padded(a1))

    rows, columns = conc_new.shape[:2]
    wide = (PAD - HALO, columns + 2 * HALO)
    near_own = pl.ds(pl.multiple_of(at_y * own_columns, PAD), own_columns + 2 * PAD)
    for index in range(own_rows + 2):
        row = wrapped(own_first - 1 + index, rows1)
        for field, (source, target) in enumerate(((conc_in, fine_a0), (chem_in, fine_a1))):
            spread_rows(spread_fine.at[field], index, a1[field][row, near_own, :])
            both = spread_fine[field, index, pl.ds(wide[0] + PAD, wide[1]), :]
            for fine in (HALO - 2 + 2 * index, HALO - 1 + 2 * index):
                put_window((target,), wide)(fine, source[fine] + both)
    fine = fine_level(weights)
    right_side = (right_conc,)
    fine.sweep(
        (fine_a0, fine_a1), right_side, HALO - 1, rows + 2, 9, wide,
        put_window((fine_b0, fine_b1), wide),
    )

    def put_new(row, conc_value, chem_value):
        conc_new[row - HALO] = conc_value
        chem_new[row - HALO] = chem_value

    fine.sweep((fine_b0, fine_b1), right_side, HALO, rows, 8, (PAD, columns), put_new)


def call_kernel(kernel, outs, scratch, *args, specs=None, vmem_mib=8):
    shapes = tuple(jax.ShapeDtypeStruct(shape, jnp.float32) for shape in outs)
    scratch = [pltpu.VMEM(shape, jnp.float32) if isinstance(shape, tuple) else shape for shape in scratch]
    return pl.pallas_call(
        kernel,
        out_shape=shapes,
        in_specs=specs or [whole_block()] * len(args),
        out_specs=tuple(whole_block() for _ in outs),
        scratch_shapes=scratch,
        compiler_params=pltpu.CompilerParams(vmem_limit_bytes=vmem_mib * 1024 * 1024),
    )(*args)


def shifted(values, axis, by):
    count = lax.axis_size(axis)
    return lax.ppermute(values, axis, [(i, (i + by) % count) for i in range(count)])


def swapped(values, axis, mask):
    count = lax.axis_size(axis)
    return lax.ppermute(values, axis, [(i, i ^ mask) for i in range(count)])


def far_masks():
    count_x, count_y = lax.axis_size("gx"), lax.axis_size("gy")
    return list(range(1, count_x)), list(range(2, count_y, 2))


def slot_masks():
    along_x, along_y = far_masks()
    first = [(0, 0)] + [(0, y) for y in along_y] + [(x, 0) for x in along_x]
    return first, [(x, y) for y in along_y for x in along_x]


def gathered(values):
    along_x, along_y = far_masks()
    across = jnp.stack([swapped(values, "gx", mask) for mask in along_x])
    beside = [swapped(values, "gy", mask) for mask in along_y]
    first = jnp.concatenate([jnp.stack([values] + beside), across], axis=0)
    second = jnp.concatenate([swapped(across, "gy", mask) for mask in along_y], axis=0)
    return first, second, swapped(first, "gy", 1), swapped(second, "gy", 1)


def two_phase_solve(conc, chem):
    rows, columns, lanes = conc.shape
    frame = (rows + 2 * HALO, columns + 2 * PAD, lanes)
    inner = (frame[0], columns + 2 * HALO, lanes)
    edge = (2, HALO, columns, lanes)
    block = (rows, columns, lanes)
    fields = jnp.concatenate([conc, chem], axis=0).reshape((2,) + block)
    side, corner = (rows, PAD, lanes), (2 * HALO, PAD, lanes)
    low, high, to_left, to_right = call_kernel(
        edges_kernel, (edge, edge, side, side), (), fields
    )
    before, after = shifted(high, "gx", 1), shifted(low, "gx", -1)
    sides = [shifted(to_right, "gy", 1), shifted(to_left, "gy", -1)]
    to_left, to_right = call_kernel(corners_kernel, (corner, corner), (), before, after)
    sides += [shifted(to_right, "gy", 1), shifted(to_left, "gy", -1)]
    packed, *kept = call_kernel(
        fine_down_kernel,
        ((3, rows // 4, columns // 2, lanes), (2,) + inner, frame, (7,) + inner),
        (frame,) * 4 + ((3, rows // 2, columns, lanes),),
        fields, before, after, *sides,
    )
    place = jnp.stack([lax.axis_index("gx"), lax.axis_index("gy")])
    count_x, count_y = lax.axis_size("gx"), lax.axis_size("gy")
    grids = [(count_x * rows >> level, count_y * columns >> level) for level in range(4)]
    scratch = []
    for level_rows, level_columns in grids[1:]:
        scratch += [(level_rows, level_columns + 2 * PAD, lanes)] * 5
        scratch += [(level_rows, level_columns, lanes)] * 9
    scratch += [(3, grids[2][0], grids[1][1], lanes), (3, grids[3][0], grids[2][1], lanes)]
    scratch += [(2, rows // 4 + 4, grids[1][1], lanes), (2, grids[3][0], grids[2][1], lanes)]
    scratch += [(2, rows // 2 + 2, columns + 4 * PAD, lanes)] + [frame] * 4
    kernel = functools.partial(coarse_kernel, slot_masks(), (count_x, count_y))
    args = (place, *gathered(packed), *kept)
    specs = [pl.BlockSpec(memory_space=pltpu.SMEM)] + [whole_block()] * (len(args) - 1)
    return call_kernel(kernel, (block, block), scratch, *args, specs=specs, vmem_mib=24)


def body(conc_old, chem_old):
    rows, columns, lanes = conc_old.shape
    count_x, count_y = lax.axis_size("gx"), lax.axis_size("gy")
    grid_bytes = count_x * rows * count_y * columns * lanes
    if (
        grid_bytes <= GRID_BYTES_MAX
        and rows % 16 == 0
        and columns % 16 == 0
        and lanes % 128 == 0
        and count_x * rows >= 64
        and count_y * columns >= 64
        and count_x >= 2
        and count_y >= 4
        and count_x & (count_x - 1) == 0
        and count_y & (count_y - 1) == 0
        and rows & (rows - 1) == 0
        and columns & (columns - 1) == 0
    ):
        return two_phase_solve(conc_old, chem_old)
    start_fields = jnp.stack([conc_old, chem_old])
    result = plain_solve(start_fields)
    return (result[0], result[1])


def solution(mesh):
    in_specs = (P(("img", "gx"), "gy", None), P(("img", "gx"), "gy", None))
    out_specs = (P(("img", "gx"), "gy", None), P(("img", "gx"), "gy", None))
    return jax.shard_map(body, mesh=mesh, in_specs=in_specs, out_specs=out_specs, check_vma=False)
```

```python
import functools

import jax
import jax.numpy as jnp
from jax import lax
from jax.experimental import pallas as pl
from jax.experimental.pallas import tpu as pltpu
from jax.sharding import PartitionSpec as P

LEVELS = 4
SWEEPS = 2
COARSE = 6


TIME_STEP = 32.0
GRADIENT_ENERGY = 0.5
STABILIZER = 2.0
DAMPING = 0.7


def extended(cells, sides, width):
    for axis, dim in sides:
        count = lax.axis_size(axis)
        head = lax.slice_in_dim(cells, 0, width, axis=dim)
        tail = lax.slice_in_dim(cells, cells.shape[dim] - width, cells.shape[dim], axis=dim)
        cells = jnp.concatenate(
            [
                lax.ppermute(tail, axis, [(i, (i + 1) % count) for i in range(count)]),
                cells,
                lax.ppermute(head, axis, [((i + 1) % count, i) for i in range(count)]),
            ],
            axis=dim,
        )
    return cells


def mobility_of(concentration):
    return 0.1 + jnp.square(1.0 - concentration * concentration)


def right_of(concentration):
    return jnp.stack(
        [
            concentration,
            concentration * concentration * concentration - (1.0 + STABILIZER) * concentration,
        ]
    )


def face_weights(mob_padded, level_scale):
    middle = mob_padded[1:-1, 1:-1, :]
    half_scale = 0.5 * level_scale
    weights = (
        half_scale * (middle + mob_padded[2:, 1:-1, :]),
        half_scale * (middle + mob_padded[:-2, 1:-1, :]),
        half_scale * (middle + mob_padded[1:-1, 2:, :]),
        half_scale * (middle + mob_padded[1:-1, :-2, :]),
        half_scale * (middle + jnp.roll(middle, -1, axis=2)),
        half_scale * (middle + jnp.roll(middle, 1, axis=2)),
    )
    total_weight = weights[0] + weights[1] + weights[2] + weights[3] + weights[4] + weights[5]
    return (weights, total_weight)


def neighbour_list(padded, middle):
    return (
        padded[2:, 1:-1, :],
        padded[:-2, 1:-1, :],
        padded[1:-1, 2:, :],
        padded[1:-1, :-2, :],
        jnp.roll(middle, -1, axis=2),
        jnp.roll(middle, 1, axis=2),
    )


def apply_operator(padded, weights, level_scale):
    middle = padded[:, 1:-1, 1:-1, :]
    conc_near = neighbour_list(padded[0], middle[0])
    chem_near = neighbour_list(padded[1], middle[1])
    flux = weights[0] * (chem_near[0] - middle[1])
    for position in range(1, 6):
        flux = flux + weights[position] * (chem_near[position] - middle[1])
    laplace = (
        conc_near[0]
        + conc_near[1]
        + conc_near[2]
        + conc_near[3]
        + conc_near[4]
        + conc_near[5]
        - 6.0 * middle[0]
    )
    first_eq = middle[0] - TIME_STEP * flux
    second_eq = middle[1] - STABILIZER * middle[0] + GRADIENT_ENERGY * level_scale * laplace
    return jnp.stack([first_eq, second_eq])


def update(residual, total_weight, level_scale):
    diagonal = STABILIZER + 6.0 * GRADIENT_ENERGY * level_scale
    coupling = TIME_STEP * total_weight
    determinant = 1.0 + coupling * diagonal
    conc_step = (residual[0] - coupling * residual[1]) / determinant
    chem_step = (residual[1] + diagonal * residual[0]) / determinant
    return DAMPING * jnp.stack([conc_step, chem_step])


def sweep_once(padded, right_side, mob_padded, level_scale):
    weights, total_weight = face_weights(mob_padded, level_scale)
    residual = right_side - apply_operator(padded, weights, level_scale)
    return padded[:, 1:-1, 1:-1, :] + update(residual, total_weight, level_scale)


def defect(padded, right_side, mob_padded, level_scale):
    weights = face_weights(mob_padded, level_scale)[0]
    return right_side - apply_operator(padded, weights, level_scale)


def coarsen(values):
    dims_now = values.shape
    grouped = values.reshape(
        dims_now[:-3] + (dims_now[-3] // 2, 2, dims_now[-2] // 2, 2, dims_now[-1] // 2, 2)
    )
    return jnp.sum(grouped, axis=(-5, -3, -1)) * 0.125


def refine(values):
    for axis_pos in (-3, -2, -1):
        values = jnp.repeat(values, 2, axis=axis_pos)
    return values


def trim_rim(values, width):
    return values[..., width:-width, width:-width, :]


def field_rim(fields):
    return extended(fields, (("gx", 1), ("gy", 2)), 1)


def coarsest_solve(right_side, mobility, level_scale):
    mob_padded = extended(mobility, (("gx", 0), ("gy", 1)), 1)
    fields = update(right_side, face_weights(mob_padded, level_scale)[1], level_scale)
    for sweep_index in range(COARSE - 1):
        padded = extended(fields, (("gx", 1), ("gy", 2)), 1)
        fields = sweep_once(padded, right_side, mob_padded, level_scale)
    return fields


def plain_solve(start_fields):
    outer_fields = field_rim(start_fields)
    mob_outer = mobility_of(outer_fields[0])
    mobility = trim_rim(mob_outer, 1)
    level_data = []
    for level_index in range(LEVELS - 1):
        if level_index == 0:
            mob_padded = mob_outer
        else:
            mob_padded = extended(mobility, (("gx", 0), ("gy", 1)), 1)
        level_data.append((mob_padded, 0.25**level_index))
        mobility = coarsen(mobility)
    coarsest_scale = 0.25 ** (LEVELS - 1)

    def cycle_level(level_index, right_side):
        if level_index == LEVELS - 1:
            return coarsest_solve(right_side, mobility, coarsest_scale)
        mob_padded, level_scale = level_data[level_index]
        if level_index == 0:
            fields = sweep_once(outer_fields, right_side, mob_padded, level_scale)
        else:
            fields = update(right_side, face_weights(mob_padded, level_scale)[1], level_scale)
        fields = sweep_once(field_rim(fields), right_side, mob_padded, level_scale)
        residual = defect(field_rim(fields), right_side, mob_padded, level_scale)
        fields = fields + refine(cycle_level(level_index + 1, coarsen(residual)))
        for sweep_index in range(SWEEPS):
            fields = sweep_once(field_rim(fields), right_side, mob_padded, level_scale)
        return fields

    return cycle_level(0, right_of(start_fields[0]))


HALO = 4
PAD = 8
GRID_BYTES_MAX = 2 * 1024 * 1024


def whole_block():
    return pl.BlockSpec(memory_space=pltpu.VMEM)


def lane_roll(values, shift):
    return pltpu.roll(values, shift % values.shape[1], axis=1)


def lane_even(shape, dup):
    return (lax.broadcasted_iota(jnp.int32, shape, 1) // dup) % 2 == 0


def loop_rows(count, unroll, row_group):
    steps, rest = divmod(count, unroll)
    if steps == 1:
        row_group(0, unroll)
    elif steps > 1:

        def step(index, carry):
            row_group(index * unroll, unroll)
            return carry

        lax.fori_loop(0, steps, step, 0)
    if rest:
        row_group(steps * unroll, rest)


def lane_swap(values):
    return jnp.where(lane_even(values.shape, 1), lane_roll(values, -1), lane_roll(values, 1))


class RowCache:
    def __init__(self, ref, rows, first, width):
        self.ref, self.rows, self.first, self.width = ref, rows, first, width
        self.values = {}

    def __getitem__(self, key):
        if key not in self.values:
            total = self.ref.shape[0]
            row = key if self.rows is None else self.rows[key]
            outside = isinstance(row, int) and not 0 <= row < total
            values = self.ref[row % total if outside else row, pl.ds(self.first, self.width), :]
            self.values[key] = lane_swap(values) if outside else values
        return self.values[key]


def chem_right(conc):
    return conc * (conc * conc - (1.0 + STABILIZER))


class Level:
    def __init__(self, level_index, weights, weights_from=PAD, right_from=PAD):
        self.scale = 0.25**level_index
        self.dup = 2**level_index
        self.diagonal = STABILIZER + 6.0 * GRADIENT_ENERGY * self.scale
        self.weights = weights
        self.weights_from, self.right_from = weights_from, right_from

    def set_weights(self, mobility, unroll):
        total, width = mobility.shape[0], self.weights[0].shape[1]
        half = 0.5 * self.scale * TIME_STEP
        face_x, up_y, down_y, up_z, down_z, coupling, gain = self.weights

        def at(row, shift=0):
            return mobility[row, pl.ds(self.weights_from + shift, width), :]

        def group(first, size):
            rows = RowCache(mobility, None, self.weights_from, width)
            before = half * (rows[first - 1] + rows[first])
            for i in range(size):
                r = first + i
                here = rows[r]
                after = half * (here + rows[r + 1])
                to_up_y = half * (here + at(r, 1))
                to_down_y = half * (here + at(r, -1))
                to_up_z = half * (here + lane_roll(here, -self.dup))
                to_down_z = half * (here + lane_roll(here, self.dup))
                total_weight = (before + after) + (to_up_y + to_down_y) + (to_up_z + to_down_z)
                face_x[r] = after
                up_y[r] = to_up_y
                down_y[r] = to_down_y
                up_z[r] = to_up_z
                down_z[r] = to_down_z
                coupling[r] = total_weight
                gain[r] = DAMPING / (1.0 + total_weight * self.diagonal)
                before = after

        loop_rows(total, unroll, group)

    def residuals(self, fields, right, rows, window, fields_from=0):
        conc, chem = fields
        first, width = window
        face_x, up_y, down_y, up_z, down_z, coupling, gain = self.weights

        def at(ref, row, shift=0):
            return ref[row, pl.ds(first - fields_from + shift, width), :]

        def weight(ref, row):
            return ref[row, pl.ds(first - self.weights_from, width), :]

        def right_at(row):
            values = [ref[row, pl.ds(first - self.right_from, width), :] for ref in right]
            return values if len(values) == 2 else values + [chem_right(values[0])]

        total = conc.shape[0]
        if isinstance(rows[0], int):
            centres, listed = [row % total for row in rows[1:-1]], None
        else:
            centres, listed = range(1, len(rows) - 1), rows
        u = RowCache(chem, listed, first - fields_from, width)
        c = RowCache(conc, listed, first - fields_from, width)
        across = RowCache(face_x, listed, first - self.weights_from, width)
        for key in centres:
            r = key if listed is None else listed[key]
            c_here, u_here = c[key], u[key]
            here = weight(coupling, r)
            flux = across[key] * u[key + 1] + across[key - 1] * u[key - 1]
            flux = flux + weight(up_y, r) * at(chem, r, 1) + weight(down_y, r) * at(chem, r, -1)
            flux = flux + weight(up_z, r) * lane_roll(u_here, -self.dup)
            flux = flux + weight(down_z, r) * lane_roll(u_here, self.dup)
            near = (c[key - 1] + c[key + 1]) + (at(conc, r, 1) + at(conc, r, -1))
            near = near + (lane_roll(c_here, self.dup) + lane_roll(c_here, -self.dup))
            conc_right, chem_right_here = right_at(r)
            conc_left = conc_right - c_here + (flux - here * u_here)
            chem_left = chem_right_here - u_here + self.diagonal * c_here
            chem_left = chem_left - (GRADIENT_ENERGY * self.scale) * near
            yield r, c_here, u_here, conc_left, chem_left, here, weight(gain, r)

    def steps(self, conc_left, chem_left, coupling, gain):
        return (
            gain * (conc_left - coupling * chem_left),
            gain * (chem_left + self.diagonal * conc_left),
        )

    def first_sweep(self, right, unroll, put):
        coupling, gain = self.weights[5:]

        def group(first, size):
            for i in range(size):
                r = first + i
                put(r, *self.steps(right[0][r], right[1][r], coupling[r], gain[r]))

        loop_rows(right[0].shape[0], unroll, group)

    def row_window(self, start, first, size):
        return [start + first + i - 1 for i in range(size + 2)]

    def sweep(self, fields, right, start, count, unroll, window, put):
        def group(first, size):
            rows = self.row_window(start, first, size)
            for r, c, u, *left in self.residuals(fields, right, rows, window):
                conc_step, chem_step = self.steps(*left)
                put(r, c + conc_step, u + chem_step)

        loop_rows(count, unroll, group)

    def coarse_right(self, fields, right, start, count, unroll, window, put, fields_from=0):
        def group(first, size):
            rows = self.row_window(start, first, size)
            items = self.residuals(fields, right, rows, window, fields_from)
            half = first // 2 if isinstance(first, int) else lax.shift_right_logical(first, 1)
            kept = None
            for i, (_, _, _, conc_left, chem_left, _, _) in enumerate(items):
                if i % 2 == 0:
                    kept = conc_left, chem_left
                else:
                    put(half + i // 2, kept[0] + conc_left, kept[1] + chem_left)

        loop_rows(count, unroll, group)


def put_padded(refs):
    def put(row, *values):
        for ref, value in zip(refs, values):
            width = value.shape[0]
            ref[row, PAD : PAD + width, :] = value
            ref[row, :PAD, :] = value[width - PAD :]
            ref[row, PAD + width :, :] = value[:PAD]

    return put


def put_window(refs, window):
    def put(row, *values):
        for ref, value in zip(refs, values):
            ref[row, window[0] : window[0] + window[1], :] = value

    return put


def put_sums(sums):
    def put(row, *values):
        for field, value in enumerate(values):
            sums[field, row] = value

    return put


def pair_rows(ref, row, count):
    return ref[row, pl.ds(0, count, stride=2), :] + ref[row, pl.ds(1, count, stride=2), :]


def spread_rows(ref, row, values):
    count = values.shape[0]
    ref[row, pl.ds(0, count, stride=2), :] = values
    ref[row, pl.ds(1, count, stride=2), :] = values


def pair_lanes(values, dup):
    other = jnp.where(
        lane_even(values.shape, dup), lane_roll(values, -dup), lane_roll(values, dup)
    )
    return values + other


def side_tiles(conc, chem, to_left, to_right, at, low):
    columns = conc.shape[0]
    to_left[at] = jnp.where(low, conc[:PAD], half_turn(chem[:PAD]))
    to_right[at] = jnp.where(low, half_turn(chem[columns - PAD :]), conc[columns - PAD :])


def low_half(lanes):
    return lax.broadcasted_iota(jnp.int32, (PAD, lanes), 0) < HALO


def edges_kernel(fields, low_rows, high_rows, to_left, to_right):
    rows, columns, lanes = fields.shape[1:]
    low_rows[...] = fields[:, :HALO]
    high_rows[...] = fields[:, rows - HALO :]
    for row in range(rows):
        side_tiles(fields[0, row], fields[1, row], to_left, to_right, row, low_half(lanes))


def corners_kernel(before, after, to_left, to_right):
    lanes = before.shape[-1]
    for at in range(2 * HALO):
        source, row = (before, at) if at < HALO else (after, at - HALO)
        side_tiles(source[0, row], source[1, row], to_left, to_right, at, low_half(lanes))


def frame_row(row, rows, own, before, after):
    if row < HALO:
        return before[row]
    if row < HALO + rows:
        return own[row - HALO]
    return after[row - HALO - rows]


def half_turn(values):
    return pltpu.roll(values, HALO, axis=0)


def side_row(row, rows, own, corners):
    if row < HALO:
        return corners[row]
    if row < HALO + rows:
        return own[row - HALO]
    return corners[row - rows]


def fine_level(weights):
    return Level(0, weights, HALO, 0)


def fine_down_kernel(
    fields, before, after, own_left, own_right, corner_left, corner_right,
    packed, kept, right_conc, all_weights,
    chem_start, mobility, conc_mid, chem_mid, sums,
):
    conc, chem = fields.at[0], fields.at[1]
    conc_out, chem_out = kept.at[0], kept.at[1]
    weights = [all_weights.at[i] for i in range(7)]
    rows, columns, lanes = conc.shape
    frame = rows + 2 * HALO
    for row in range(frame):
        left = side_row(row, rows, own_left, corner_left)
        right = side_row(row, rows, own_right, corner_right)
        c = jnp.concatenate([left, frame_row(row, rows, conc, before.at[0], after.at[0]), right])
        own = frame_row(row, rows, chem, before.at[1], after.at[1])
        right_conc[row] = c
        chem_start[row] = jnp.concatenate([half_turn(left), own, half_turn(right)])
        gap = 1.0 - c * c
        mobility[row] = 0.1 + gap * gap
    level = fine_level(weights)
    level.set_weights(mobility, frame)
    right_side = (right_conc,)
    wide = (PAD - HALO, columns + 2 * HALO)
    level.sweep(
        (right_conc, chem_start), right_side, 1, frame - 2, 11, wide,
        put_window((conc_mid, chem_mid), wide),
    )
    level.sweep(
        (conc_mid, chem_mid), right_side, 2, frame - 4, 10, wide,
        put_window((conc_out, chem_out), (0, wide[1])),
    )
    level.coarse_right(
        (conc_out, chem_out), right_side, HALO, rows, 8, (PAD, columns), put_sums(sums), wide[0]
    )
    for index in range(rows // 2):
        row = HALO + 2 * index
        own = slice(PAD, PAD + columns)
        sums[2, index] = mobility[row, own, :] + mobility[row + 1, own, :]
    even = lane_even((columns // 2, lanes), 1)
    for field in range(3):
        for index in range(rows // 4):
            a = pair_rows(sums.at[field], 2 * index, columns // 2)
            b = pair_rows(sums.at[field], 2 * index + 1, columns // 2)
            packed[field, index] = 0.125 * jnp.where(
                even, a + lane_roll(a, -1), b + lane_roll(b, 1)
            )


def coarse_kernel(
    slots, grid, place, first, second, first_far, second_far,
    kept, right_conc, all_weights, conc_new, chem_new, *scratch,
):
    conc_in, chem_in = kept.at[0], kept.at[1]
    weights = [all_weights.at[i] for i in range(7)]
    scratch = list(scratch)
    start_even, at_y = place[0] % 2 == 0, place[1]
    levels = []
    for level_index in (1, 2, 3):
        level = Level(level_index, scratch[5:14][2:])
        mobility, a, b, right = scratch[0], scratch[1:3], scratch[3:5], scratch[5:7]
        levels.append((level, mobility, right, a, b))
        del scratch[:14]
    sums1, sums2, spread2, spread3, spread_fine, fine_a0, fine_a1, fine_b0, fine_b1 = scratch
    one, mob1, right1, a1, b1 = levels[0]
    two, mob2, right2, a2, b2 = levels[1]
    three, mob3, right3, a3, b3 = levels[2]
    rows1, columns1, lanes = right1[0].shape
    rows2, columns2 = right2[0].shape[:2]
    rows3, columns3 = right3[0].shape[:2]
    window1, window2, window3 = (PAD, columns1), (PAD, columns2), (PAD, columns3)
    own_rows, own_columns = 2 * rows1 // grid[0], columns1 // grid[1]
    even = lane_even((own_columns, lanes), 1)
    blocks = {}
    for last, sources in enumerate(((first, second), (first_far, second_far))):
        for source, masks in zip(sources, slots):
            for slot, (mask_x, mask_y) in enumerate(masks):
                blocks[mask_x, mask_y ^ last] = source.at[slot]

    for mask_y in range(grid[1]):
        offset = (at_y ^ mask_y) * own_columns
        plain = pl.ds(pl.multiple_of(offset, PAD), own_columns)
        padded = pl.ds(pl.multiple_of(offset + PAD, PAD), own_columns)
        for field, (ref, at) in enumerate(
            ((right1[0], plain), (right1[1], plain), (mob1, padded))
        ):
            for index in range(own_rows // 2):
                own, two_on, one_on, one_back = (
                    blocks[mask_x, mask_y][field, index] for mask_x in (0, 2, 1, 3)
                )
                swap = one_on, one_back
                one_on = jnp.where(start_even, swap[0], swap[1])
                one_back = jnp.where(start_even, swap[1], swap[0])
                for row, a, b in ((0, own, two_on), (own_rows, one_on, one_back)):
                    row = row + 2 * index
                    ref[row, at, :] = jnp.where(even, a, lane_roll(b, 1))
                    ref[row + 1, at, :] = jnp.where(even, lane_roll(a, -1), b)
    for row in range(rows1):
        mob1[row, :PAD, :] = mob1[row, columns1 : columns1 + PAD, :]
        mob1[row, PAD + columns1 :, :] = mob1[row, PAD : 2 * PAD, :]

    def coarsen(mobility, sums, out, out_mobility, dup):
        count, columns = out[0].shape[:2]
        fine = pl.ds(PAD, 2 * columns)
        for index in range(count):
            sums[2, index] = mobility[2 * index, fine, :] + mobility[2 * index + 1, fine, :]
        for index in range(count):
            for field in range(2):
                half = pair_rows(sums.at[field], index, columns)
                out[field][index] = 0.125 * pair_lanes(half, dup)
            half = pair_rows(sums.at[2], index, columns)
            put_padded((out_mobility,))(index, 0.125 * pair_lanes(half, dup))

    one.set_weights(mob1, rows1)
    one.first_sweep(right1, rows1, put_padded(a1))
    one.sweep(a1, right1, 0, rows1, rows1, window1, put_padded(b1))
    one.coarse_right(b1, right1, 0, rows1, rows1, window1, put_sums(sums1))
    coarsen(mob1, sums1, right2, mob2, 2)

    two.set_weights(mob2, rows2)
    two.first_sweep(right2, rows2, put_padded(a2))
    two.sweep(a2, right2, 0, rows2, rows2, window2, put_padded(b2))
    two.coarse_right(b2, right2, 0, rows2, rows2, window2, put_sums(sums2))
    coarsen(mob2, sums2, right3, mob3, 4)

    three.set_weights(mob3, rows3)
    three.first_sweep(right3, rows3, put_padded(a3))
    now, other = a3, b3
    for sweep_index in range(COARSE - 1):
        three.sweep(now, right3, 0, rows3, rows3, window3, put_padded(other))
        now, other = other, now

    def correct(coarse, coarse_row, fine_in, fine_out, spread, index):
        for field in range(2):
            columns = fine_in[field].shape[1] - 2 * PAD
            spread_rows(
                spread.at[field], index, coarse[field][coarse_row, pl.ds(PAD, columns // 2), :]
            )
            both = spread[field, index]
            for row in (2 * coarse_row, 2 * coarse_row + 1):
                put_padded((fine_out[field],))(
                    row, fine_in[field][row, pl.ds(PAD, columns), :] + both
                )

    for row in range(rows3):
        correct(now, row, b2, a2, spread3, row)
    two.sweep(a2, right2, 0, rows2, rows2, window2, put_padded(b2))
    two.sweep(b2, right2, 0, rows2, rows2, window2, put_padded(a2))
    for row in range(rows2):
        correct(a2, row, b1, a1, spread2, row)
    one.sweep(a1, right1, -2, own_rows + 4, own_rows + 4, window1, put_padded(b1))
    one.sweep(b1, right1, -1, own_rows + 2, own_rows + 2, window1, put_padded(a1))

    rows, columns = conc_new.shape[:2]
    wide = (PAD - HALO, columns + 2 * HALO)
    near_own = pl.ds(pl.multiple_of(at_y * own_columns, PAD), own_columns + 2 * PAD)
    for index in range(own_rows + 2):
        inside = 1 <= index <= rows1
        row = index - 1 if inside else (index - 1) % rows1
        for field, (source, target) in enumerate(((conc_in, fine_a0), (chem_in, fine_a1))):
            tile = a1[field][row, near_own, :]
            on_even = lane_even(tile.shape, 1)
            if inside:
                tile = jnp.where(on_even, tile, lane_roll(tile, 1))
            else:
                tile = jnp.where(on_even, lane_roll(tile, -1), tile)
            spread_rows(spread_fine.at[field], index, tile)
            both = spread_fine[field, index, pl.ds(wide[0] + PAD, wide[1]), :]
            for fine in (HALO - 2 + 2 * index, HALO - 1 + 2 * index):
                put_window((target,), wide)(fine, source[fine] + both)
    fine = fine_level(weights)
    right_side = (right_conc,)
    fine.sweep(
        (fine_a0, fine_a1), right_side, HALO - 1, rows + 2, 9, wide,
        put_window((fine_b0, fine_b1), wide),
    )

    def put_new(row, conc_value, chem_value):
        conc_new[row - HALO] = conc_value
        chem_new[row - HALO] = chem_value

    fine.sweep((fine_b0, fine_b1), right_side, HALO, rows, 8, (PAD, columns), put_new)


def call_kernel(kernel, outs, scratch, *args, specs=None, vmem_mib=8):
    shapes = tuple(jax.ShapeDtypeStruct(shape, jnp.float32) for shape in outs)
    scratch = [pltpu.VMEM(shape, jnp.float32) if isinstance(shape, tuple) else shape for shape in scratch]
    return pl.pallas_call(
        kernel,
        out_shape=shapes,
        in_specs=specs or [whole_block()] * len(args),
        out_specs=tuple(whole_block() for _ in outs),
        scratch_shapes=scratch,
        compiler_params=pltpu.CompilerParams(vmem_limit_bytes=vmem_mib * 1024 * 1024),
    )(*args)


def shifted(values, axis, by):
    count = lax.axis_size(axis)
    return lax.ppermute(values, axis, [(i, (i + by) % count) for i in range(count)])


def swapped(values, axis, mask):
    count = lax.axis_size(axis)
    return lax.ppermute(values, axis, [(i, i ^ mask) for i in range(count)])


def far_masks():
    count_x, count_y = lax.axis_size("gx"), lax.axis_size("gy")
    return list(range(1, count_x)), list(range(2, count_y, 2))


def slot_masks():
    along_x, along_y = far_masks()
    first = [(0, 0)] + [(0, y) for y in along_y] + [(x, 0) for x in along_x]
    return first, [(x, y) for y in along_y for x in along_x]


def gathered(values):
    along_x, along_y = far_masks()
    across = jnp.stack([swapped(values, "gx", mask) for mask in along_x])
    beside = [swapped(values, "gy", mask) for mask in along_y]
    first = jnp.concatenate([jnp.stack([values] + beside), across], axis=0)
    second = jnp.concatenate([swapped(across, "gy", mask) for mask in along_y], axis=0)
    return first, second, swapped(first, "gy", 1), swapped(second, "gy", 1)


def two_phase_solve(conc, chem):
    rows, columns, lanes = conc.shape
    frame = (rows + 2 * HALO, columns + 2 * PAD, lanes)
    inner = (frame[0], columns + 2 * HALO, lanes)
    edge = (2, HALO, columns, lanes)
    block = (rows, columns, lanes)
    fields = jnp.concatenate([conc, chem], axis=0).reshape((2,) + block)
    side, corner = (rows, PAD, lanes), (2 * HALO, PAD, lanes)
    low, high, to_left, to_right = call_kernel(
        edges_kernel, (edge, edge, side, side), (), fields
    )
    before, after = shifted(high, "gx", 1), shifted(low, "gx", -1)
    sides = [shifted(to_right, "gy", 1), shifted(to_left, "gy", -1)]
    to_left, to_right = call_kernel(corners_kernel, (corner, corner), (), before, after)
    sides += [shifted(to_right, "gy", 1), shifted(to_left, "gy", -1)]
    packed, *kept = call_kernel(
        fine_down_kernel,
        ((3, rows // 4, columns // 2, lanes), (2,) + inner, frame, (7,) + inner),
        (frame,) * 4 + ((3, rows // 2, columns, lanes),),
        fields, before, after, *sides,
    )
    place = jnp.stack([lax.axis_index("gx"), lax.axis_index("gy")])
    count_x, count_y = lax.axis_size("gx"), lax.axis_size("gy")
    grids = [(count_x * rows >> level + 1, count_y * columns >> level) for level in range(4)]
    scratch = []
    for level_rows, level_columns in grids[1:]:
        scratch += [(level_rows, level_columns + 2 * PAD, lanes)] * 5
        scratch += [(level_rows, level_columns, lanes)] * 9
    scratch += [(3, grids[2][0], grids[1][1], lanes), (3, grids[3][0], grids[2][1], lanes)]
    scratch += [(2, grids[2][0], grids[1][1], lanes), (2, grids[3][0], grids[2][1], lanes)]
    scratch += [(2, rows // 2 + 2, columns + 4 * PAD, lanes)] + [frame] * 4
    kernel = functools.partial(coarse_kernel, slot_masks(), (count_x, count_y))
    args = (place, *gathered(packed), *kept)
    specs = [pl.BlockSpec(memory_space=pltpu.SMEM)] + [whole_block()] * (len(args) - 1)
    return call_kernel(kernel, (block, block), scratch, *args, specs=specs, vmem_mib=24)


def body(conc_old, chem_old):
    rows, columns, lanes = conc_old.shape
    count_x, count_y = lax.axis_size("gx"), lax.axis_size("gy")
    grid_bytes = count_x * rows * count_y * columns * lanes
    if (
        grid_bytes <= GRID_BYTES_MAX
        and rows % 16 == 0
        and lanes % 128 == 0
        and count_x * rows >= 64
        and count_y * columns >= 64
        and count_x == 4
        and count_y >= 4
        and count_y & (count_y - 1) == 0
        and columns == 16
    ):
        return two_phase_solve(conc_old, chem_old)
    start_fields = jnp.stack([conc_old, chem_old])
    result = plain_solve(start_fields)
    return (result[0], result[1])


def solution(mesh):
    in_specs = (P(("img", "gx"), "gy", None), P(("img", "gx"), "gy", None))
    out_specs = (P(("img", "gx"), "gy", None), P(("img", "gx"), "gy", None))
    return jax.shard_map(body, mesh=mesh, in_specs=in_specs, out_specs=out_specs, check_vma=False)
```

```python
import functools

import jax
import jax.numpy as jnp
from jax import lax
from jax.experimental import pallas as pl
from jax.experimental.pallas import tpu as pltpu
from jax.sharding import PartitionSpec as P

LEVELS = 4
SWEEPS = 2
COARSE = 6


TIME_STEP = 32.0
GRADIENT_ENERGY = 0.5
STABILIZER = 2.0
DAMPING = 0.7


def extended(cells, sides, width):
    for axis, dim in sides:
        count = lax.axis_size(axis)
        head = lax.slice_in_dim(cells, 0, width, axis=dim)
        tail = lax.slice_in_dim(cells, cells.shape[dim] - width, cells.shape[dim], axis=dim)
        cells = jnp.concatenate(
            [
                lax.ppermute(tail, axis, [(i, (i + 1) % count) for i in range(count)]),
                cells,
                lax.ppermute(head, axis, [((i + 1) % count, i) for i in range(count)]),
            ],
            axis=dim,
        )
    return cells


def mobility_of(concentration):
    return 0.1 + jnp.square(1.0 - concentration * concentration)


def right_of(concentration):
    return jnp.stack(
        [
            concentration,
            concentration * concentration * concentration - (1.0 + STABILIZER) * concentration,
        ]
    )


def face_weights(mob_padded, level_scale):
    middle = mob_padded[1:-1, 1:-1, :]
    half_scale = 0.5 * level_scale
    weights = (
        half_scale * (middle + mob_padded[2:, 1:-1, :]),
        half_scale * (middle + mob_padded[:-2, 1:-1, :]),
        half_scale * (middle + mob_padded[1:-1, 2:, :]),
        half_scale * (middle + mob_padded[1:-1, :-2, :]),
        half_scale * (middle + jnp.roll(middle, -1, axis=2)),
        half_scale * (middle + jnp.roll(middle, 1, axis=2)),
    )
    total_weight = weights[0] + weights[1] + weights[2] + weights[3] + weights[4] + weights[5]
    return (weights, total_weight)


def neighbour_list(padded, middle):
    return (
        padded[2:, 1:-1, :],
        padded[:-2, 1:-1, :],
        padded[1:-1, 2:, :],
        padded[1:-1, :-2, :],
        jnp.roll(middle, -1, axis=2),
        jnp.roll(middle, 1, axis=2),
    )


def apply_operator(padded, weights, level_scale):
    middle = padded[:, 1:-1, 1:-1, :]
    conc_near = neighbour_list(padded[0], middle[0])
    chem_near = neighbour_list(padded[1], middle[1])
    flux = weights[0] * (chem_near[0] - middle[1])
    for position in range(1, 6):
        flux = flux + weights[position] * (chem_near[position] - middle[1])
    laplace = (
        conc_near[0]
        + conc_near[1]
        + conc_near[2]
        + conc_near[3]
        + conc_near[4]
        + conc_near[5]
        - 6.0 * middle[0]
    )
    first_eq = middle[0] - TIME_STEP * flux
    second_eq = middle[1] - STABILIZER * middle[0] + GRADIENT_ENERGY * level_scale * laplace
    return jnp.stack([first_eq, second_eq])


def update(residual, total_weight, level_scale):
    diagonal = STABILIZER + 6.0 * GRADIENT_ENERGY * level_scale
    coupling = TIME_STEP * total_weight
    determinant = 1.0 + coupling * diagonal
    conc_step = (residual[0] - coupling * residual[1]) / determinant
    chem_step = (residual[1] + diagonal * residual[0]) / determinant
    return DAMPING * jnp.stack([conc_step, chem_step])


def sweep_once(padded, right_side, mob_padded, level_scale):
    weights, total_weight = face_weights(mob_padded, level_scale)
    residual = right_side - apply_operator(padded, weights, level_scale)
    return padded[:, 1:-1, 1:-1, :] + update(residual, total_weight, level_scale)


def defect(padded, right_side, mob_padded, level_scale):
    weights = face_weights(mob_padded, level_scale)[0]
    return right_side - apply_operator(padded, weights, level_scale)


def coarsen(values):
    dims_now = values.shape
    grouped = values.reshape(
        dims_now[:-3] + (dims_now[-3] // 2, 2, dims_now[-2] // 2, 2, dims_now[-1] // 2, 2)
    )
    return jnp.sum(grouped, axis=(-5, -3, -1)) * 0.125


def refine(values):
    for axis_pos in (-3, -2, -1):
        values = jnp.repeat(values, 2, axis=axis_pos)
    return values


def trim_rim(values, width):
    return values[..., width:-width, width:-width, :]


def field_rim(fields):
    return extended(fields, (("gx", 1), ("gy", 2)), 1)


def coarsest_solve(right_side, mobility, level_scale):
    mob_padded = extended(mobility, (("gx", 0), ("gy", 1)), 1)
    fields = update(right_side, face_weights(mob_padded, level_scale)[1], level_scale)
    for sweep_index in range(COARSE - 1):
        padded = extended(fields, (("gx", 1), ("gy", 2)), 1)
        fields = sweep_once(padded, right_side, mob_padded, level_scale)
    return fields


def plain_solve(start_fields):
    outer_fields = field_rim(start_fields)
    mob_outer = mobility_of(outer_fields[0])
    mobility = trim_rim(mob_outer, 1)
    level_data = []
    for level_index in range(LEVELS - 1):
        if level_index == 0:
            mob_padded = mob_outer
        else:
            mob_padded = extended(mobility, (("gx", 0), ("gy", 1)), 1)
        level_data.append((mob_padded, 0.25**level_index))
        mobility = coarsen(mobility)
    coarsest_scale = 0.25 ** (LEVELS - 1)

    def cycle_level(level_index, right_side):
        if level_index == LEVELS - 1:
            return coarsest_solve(right_side, mobility, coarsest_scale)
        mob_padded, level_scale = level_data[level_index]
        if level_index == 0:
            fields = sweep_once(outer_fields, right_side, mob_padded, level_scale)
        else:
            fields = update(right_side, face_weights(mob_padded, level_scale)[1], level_scale)
        fields = sweep_once(field_rim(fields), right_side, mob_padded, level_scale)
        residual = defect(field_rim(fields), right_side, mob_padded, level_scale)
        fields = fields + refine(cycle_level(level_index + 1, coarsen(residual)))
        for sweep_index in range(SWEEPS):
            fields = sweep_once(field_rim(fields), right_side, mob_padded, level_scale)
        return fields

    return cycle_level(0, right_of(start_fields[0]))


HALO = 4
PAD = 8
GRID_BYTES_MAX = 2 * 1024 * 1024


def whole_block():
    return pl.BlockSpec(memory_space=pltpu.VMEM)


def lane_roll(values, shift):
    return pltpu.roll(values, shift % values.shape[1], axis=1)


def lane_even(shape, dup):
    return (lax.broadcasted_iota(jnp.int32, shape, 1) // dup) % 2 == 0


def loop_rows(count, unroll, row_group):
    steps, rest = divmod(count, unroll)
    if steps == 1:
        row_group(0, unroll)
    elif steps > 1:

        def step(index, carry):
            row_group(index * unroll, unroll)
            return carry

        lax.fori_loop(0, steps, step, 0)
    if rest:
        row_group(steps * unroll, rest)


def lane_swap(values):
    return jnp.where(lane_even(values.shape, 1), lane_roll(values, -1), lane_roll(values, 1))


class RowCache:
    def __init__(self, ref, rows, first, width):
        self.ref, self.rows, self.first, self.width = ref, rows, first, width
        self.values = {}

    def __getitem__(self, key):
        if key not in self.values:
            total = self.ref.shape[0]
            row = key if self.rows is None else self.rows[key]
            outside = isinstance(row, int) and not 0 <= row < total
            values = self.ref[row % total if outside else row, pl.ds(self.first, self.width), :]
            self.values[key] = lane_swap(values) if outside else values
        return self.values[key]


def stage(run, *args):
    pl.when(lax.axis_index("gy") >= 0)(functools.partial(run, *args))


def chem_right(conc):
    return conc * (conc * conc - (1.0 + STABILIZER))


class Level:
    def __init__(self, level_index, weights, weights_from=PAD, right_from=PAD):
        self.scale = 0.25**level_index
        self.dup = 2**level_index
        self.diagonal = STABILIZER + 6.0 * GRADIENT_ENERGY * self.scale
        self.weights = weights
        self.weights_from, self.right_from = weights_from, right_from

    def set_weights(self, mobility, unroll):
        total, width = mobility.shape[0], self.weights[0].shape[1]
        half = 0.5 * self.scale * TIME_STEP
        face_x, up_y, down_y, up_z, down_z, coupling, gain = self.weights

        def at(row, shift=0):
            return mobility[row, pl.ds(self.weights_from + shift, width), :]

        def group(first, size):
            rows = RowCache(mobility, None, self.weights_from, width)
            before = half * (rows[first - 1] + rows[first])
            for i in range(size):
                r = first + i
                here = rows[r]
                after = half * (here + rows[r + 1])
                to_up_y = half * (here + at(r, 1))
                to_down_y = half * (here + at(r, -1))
                to_up_z = half * (here + lane_roll(here, -self.dup))
                to_down_z = half * (here + lane_roll(here, self.dup))
                total_weight = (before + after) + (to_up_y + to_down_y) + (to_up_z + to_down_z)
                face_x[r] = after
                up_y[r] = to_up_y
                down_y[r] = to_down_y
                up_z[r] = to_up_z
                down_z[r] = to_down_z
                coupling[r] = total_weight
                gain[r] = DAMPING / (1.0 + total_weight * self.diagonal)
                before = after

        loop_rows(total, unroll, group)

    def residuals(self, fields, right, rows, window, fields_from=0):
        conc, chem = fields
        first, width = window
        face_x, up_y, down_y, up_z, down_z, coupling, gain = self.weights

        def at(ref, row, shift=0):
            return ref[row, pl.ds(first - fields_from + shift, width), :]

        def weight(ref, row):
            return ref[row, pl.ds(first - self.weights_from, width), :]

        def right_at(row):
            values = [ref[row, pl.ds(first - self.right_from, width), :] for ref in right]
            return values if len(values) == 2 else values + [chem_right(values[0])]

        total = conc.shape[0]
        if isinstance(rows[0], int):
            centres, listed = [row % total for row in rows[1:-1]], None
        else:
            centres, listed = range(1, len(rows) - 1), rows
        u = RowCache(chem, listed, first - fields_from, width)
        c = RowCache(conc, listed, first - fields_from, width)
        across = RowCache(face_x, listed, first - self.weights_from, width)
        for key in centres:
            r = key if listed is None else listed[key]
            c_here, u_here = c[key], u[key]
            here = weight(coupling, r)
            flux = across[key] * u[key + 1] + across[key - 1] * u[key - 1]
            flux = flux + weight(up_y, r) * at(chem, r, 1) + weight(down_y, r) * at(chem, r, -1)
            flux = flux + weight(up_z, r) * lane_roll(u_here, -self.dup)
            flux = flux + weight(down_z, r) * lane_roll(u_here, self.dup)
            near = (c[key - 1] + c[key + 1]) + (at(conc, r, 1) + at(conc, r, -1))
            near = near + (lane_roll(c_here, self.dup) + lane_roll(c_here, -self.dup))
            conc_right, chem_right_here = right_at(r)
            conc_left = conc_right - c_here + (flux - here * u_here)
            chem_left = chem_right_here - u_here + self.diagonal * c_here
            chem_left = chem_left - (GRADIENT_ENERGY * self.scale) * near
            yield r, c_here, u_here, conc_left, chem_left, here, weight(gain, r)

    def steps(self, conc_left, chem_left, coupling, gain):
        return (
            gain * (conc_left - coupling * chem_left),
            gain * (chem_left + self.diagonal * conc_left),
        )

    def first_sweep(self, right, unroll, put):
        coupling, gain = self.weights[5:]

        def group(first, size):
            for i in range(size):
                r = first + i
                put(r, *self.steps(right[0][r], right[1][r], coupling[r], gain[r]))

        loop_rows(right[0].shape[0], unroll, group)

    def row_window(self, start, first, size):
        return [start + first + i - 1 for i in range(size + 2)]

    def sweep(self, fields, right, start, count, unroll, window, put):
        def group(first, size):
            rows = self.row_window(start, first, size)
            for r, c, u, *left in self.residuals(fields, right, rows, window):
                conc_step, chem_step = self.steps(*left)
                put(r, c + conc_step, u + chem_step)

        loop_rows(count, unroll, group)

    def coarse_right(self, fields, right, start, count, unroll, window, put, fields_from=0):
        def group(first, size):
            rows = self.row_window(start, first, size)
            items = self.residuals(fields, right, rows, window, fields_from)
            half = first // 2 if isinstance(first, int) else lax.shift_right_logical(first, 1)
            kept = None
            for i, (_, _, _, conc_left, chem_left, _, _) in enumerate(items):
                if i % 2 == 0:
                    kept = conc_left, chem_left
                else:
                    put(half + i // 2, kept[0] + conc_left, kept[1] + chem_left)

        loop_rows(count, unroll, group)


def put_padded(refs):
    def put(row, *values):
        for ref, value in zip(refs, values):
            width = value.shape[0]
            ref[row, PAD : PAD + width, :] = value
            ref[row, :PAD, :] = value[width - PAD :]
            ref[row, PAD + width :, :] = value[:PAD]

    return put


def put_window(refs, window):
    def put(row, *values):
        for ref, value in zip(refs, values):
            ref[row, window[0] : window[0] + window[1], :] = value

    return put


def put_sums(sums):
    def put(row, *values):
        for field, value in enumerate(values):
            sums[field, row] = value

    return put


def pair_rows(ref, row, count):
    return ref[row, pl.ds(0, count, stride=2), :] + ref[row, pl.ds(1, count, stride=2), :]


def spread_rows(ref, row, values):
    count = values.shape[0]
    ref[row, pl.ds(0, count, stride=2), :] = values
    ref[row, pl.ds(1, count, stride=2), :] = values


def pair_lanes(values, dup):
    other = jnp.where(
        lane_even(values.shape, dup), lane_roll(values, -dup), lane_roll(values, dup)
    )
    return values + other


def side_tiles(conc, chem, to_left, to_right, at, low):
    columns = conc.shape[0]
    to_left[at] = jnp.where(low, conc[:PAD], half_turn(chem[:PAD]))
    to_right[at] = jnp.where(low, half_turn(chem[columns - PAD :]), conc[columns - PAD :])


def low_half(lanes):
    return lax.broadcasted_iota(jnp.int32, (PAD, lanes), 0) < HALO


def edges_kernel(fields, low_rows, high_rows, to_left, to_right):
    rows, columns, lanes = fields.shape[1:]
    low_rows[...] = fields[:, :HALO]
    high_rows[...] = fields[:, rows - HALO :]
    for row in range(rows):
        side_tiles(fields[0, row], fields[1, row], to_left, to_right, row, low_half(lanes))


def corners_kernel(before, after, to_left, to_right):
    lanes = before.shape[-1]
    for at in range(2 * HALO):
        source, row = (before, at) if at < HALO else (after, at - HALO)
        side_tiles(source[0, row], source[1, row], to_left, to_right, at, low_half(lanes))


def frame_row(row, rows, own, before, after):
    if row < HALO:
        return before[row]
    if row < HALO + rows:
        return own[row - HALO]
    return after[row - HALO - rows]


def half_turn(values):
    return pltpu.roll(values, HALO, axis=0)


def side_row(row, rows, own, corners):
    if row < HALO:
        return corners[row]
    if row < HALO + rows:
        return own[row - HALO]
    return corners[row - rows]


def fine_level(weights):
    return Level(0, weights, HALO, 0)


def fine_down_kernel(
    fields, before, after, own_left, own_right, corner_left, corner_right,
    packed, kept, right_conc, all_weights,
    chem_start, mobility, conc_mid, chem_mid, sums,
):
    conc, chem = fields.at[0], fields.at[1]
    conc_out, chem_out = kept.at[0], kept.at[1]
    weights = [all_weights.at[i] for i in range(7)]
    rows, columns, lanes = conc.shape
    frame = rows + 2 * HALO
    for row in range(frame):
        left = side_row(row, rows, own_left, corner_left)
        right = side_row(row, rows, own_right, corner_right)
        c = jnp.concatenate([left, frame_row(row, rows, conc, before.at[0], after.at[0]), right])
        own = frame_row(row, rows, chem, before.at[1], after.at[1])
        right_conc[row] = c
        chem_start[row] = jnp.concatenate([half_turn(left), own, half_turn(right)])
        gap = 1.0 - c * c
        mobility[row] = 0.1 + gap * gap
    level = fine_level(weights)
    level.set_weights(mobility, frame)
    right_side = (right_conc,)
    wide = (PAD - HALO, columns + 2 * HALO)
    level.sweep(
        (right_conc, chem_start), right_side, 1, frame - 2, frame - 2, wide,
        put_window((conc_mid, chem_mid), wide),
    )
    level.sweep(
        (conc_mid, chem_mid), right_side, 2, frame - 4, frame - 4, wide,
        put_window((conc_out, chem_out), (0, wide[1])),
    )
    level.coarse_right(
        (conc_out, chem_out), right_side, HALO, rows, rows, (PAD, columns), put_sums(sums), wide[0]
    )
    for index in range(rows // 2):
        row = HALO + 2 * index
        own = slice(PAD, PAD + columns)
        sums[2, index] = mobility[row, own, :] + mobility[row + 1, own, :]
    even = lane_even((columns // 2, lanes), 1)
    for field in range(3):
        for index in range(rows // 4):
            a = pair_rows(sums.at[field], 2 * index, columns // 2)
            b = pair_rows(sums.at[field], 2 * index + 1, columns // 2)
            packed[field, index] = 0.125 * jnp.where(
                even, a + lane_roll(a, -1), b + lane_roll(b, 1)
            )


def coarse_kernel(
    slots, grid, first, second, first_far, second_far,
    kept, right_conc, all_weights, conc_new, chem_new, *scratch,
):
    conc_in, chem_in = kept.at[0], kept.at[1]
    weights = [all_weights.at[i] for i in range(7)]
    scratch = list(scratch)
    start_even, at_y = lax.axis_index("gx") % 2 == 0, lax.axis_index("gy")
    levels = []
    for level_index in (1, 2, 3):
        level = Level(level_index, scratch[5:14][2:])
        mobility, a, b, right = scratch[0], scratch[1:3], scratch[3:5], scratch[5:7]
        levels.append((level, mobility, right, a, b))
        del scratch[:14]
    sums1, sums2, spread2, spread3, spread_fine, fine_a0, fine_a1, fine_b0, fine_b1 = scratch
    one, mob1, right1, a1, b1 = levels[0]
    two, mob2, right2, a2, b2 = levels[1]
    three, mob3, right3, a3, b3 = levels[2]
    rows1, columns1, lanes = right1[0].shape
    rows2, columns2 = right2[0].shape[:2]
    rows3, columns3 = right3[0].shape[:2]
    window1, window2, window3 = (PAD, columns1), (PAD, columns2), (PAD, columns3)
    own_rows, own_columns = 2 * rows1 // grid[0], columns1 // grid[1]
    even = lane_even((own_columns, lanes), 1)
    blocks = {}
    for last, sources in enumerate(((first, second), (first_far, second_far))):
        for source, masks in zip(sources, slots):
            for slot, (mask_x, mask_y) in enumerate(masks):
                blocks[mask_x, mask_y ^ last] = source.at[slot]

    for mask_y in range(grid[1]):
        offset = (at_y ^ mask_y) * own_columns
        plain = pl.ds(pl.multiple_of(offset, PAD), own_columns)
        padded = pl.ds(pl.multiple_of(offset + PAD, PAD), own_columns)
        for field, (ref, at) in enumerate(
            ((right1[0], plain), (right1[1], plain), (mob1, padded))
        ):
            for index in range(own_rows // 2):
                own, two_on, one_on, one_back = (
                    blocks[mask_x, mask_y][field, index] for mask_x in (0, 2, 1, 3)
                )
                swap = one_on, one_back
                one_on = jnp.where(start_even, swap[0], swap[1])
                one_back = jnp.where(start_even, swap[1], swap[0])
                for row, a, b in ((0, own, two_on), (own_rows, one_on, one_back)):
                    row = row + 2 * index
                    ref[row, at, :] = jnp.where(even, a, lane_roll(b, 1))
                    ref[row + 1, at, :] = jnp.where(even, lane_roll(a, -1), b)
    for row in range(rows1):
        mob1[row, :PAD, :] = mob1[row, columns1 : columns1 + PAD, :]
        mob1[row, PAD + columns1 :, :] = mob1[row, PAD : 2 * PAD, :]

    def coarsen(mobility, sums, out, out_mobility, dup):
        count, columns = out[0].shape[:2]
        fine = pl.ds(PAD, 2 * columns)
        for index in range(count):
            sums[2, index] = mobility[2 * index, fine, :] + mobility[2 * index + 1, fine, :]
        for index in range(count):
            for field in range(2):
                half = pair_rows(sums.at[field], index, columns)
                out[field][index] = 0.125 * pair_lanes(half, dup)
            half = pair_rows(sums.at[2], index, columns)
            put_padded((out_mobility,))(index, 0.125 * pair_lanes(half, dup))

    stage(one.set_weights, mob1, rows1)
    stage(one.first_sweep, right1, rows1, put_padded(a1))
    stage(one.sweep, a1, right1, 0, rows1, rows1, window1, put_padded(b1))
    stage(one.coarse_right, b1, right1, 0, rows1, rows1, window1, put_sums(sums1))
    stage(coarsen, mob1, sums1, right2, mob2, 2)

    stage(two.set_weights, mob2, rows2)
    stage(two.first_sweep, right2, rows2, put_padded(a2))
    stage(two.sweep, a2, right2, 0, rows2, rows2, window2, put_padded(b2))
    stage(two.coarse_right, b2, right2, 0, rows2, rows2, window2, put_sums(sums2))
    stage(coarsen, mob2, sums2, right3, mob3, 4)

    stage(three.set_weights, mob3, rows3)
    stage(three.first_sweep, right3, rows3, put_padded(a3))
    now, other = a3, b3
    for sweep_index in range(COARSE - 1):
        stage(three.sweep, now, right3, 0, rows3, rows3, window3, put_padded(other))
        now, other = other, now

    def correct(coarse, coarse_row, fine_in, fine_out, spread, index):
        for field in range(2):
            columns = fine_in[field].shape[1] - 2 * PAD
            spread_rows(
                spread.at[field], index, coarse[field][coarse_row, pl.ds(PAD, columns // 2), :]
            )
            both = spread[field, index]
            for row in (2 * coarse_row, 2 * coarse_row + 1):
                put_padded((fine_out[field],))(
                    row, fine_in[field][row, pl.ds(PAD, columns), :] + both
                )

    for row in range(rows3):
        correct(now, row, b2, a2, spread3, row)
    stage(two.sweep, a2, right2, 0, rows2, rows2, window2, put_padded(b2))
    stage(two.sweep, b2, right2, 0, rows2, rows2, window2, put_padded(a2))
    for row in range(rows2):
        correct(a2, row, b1, a1, spread2, row)
    stage(one.sweep, a1, right1, -2, own_rows + 4, own_rows + 4, window1, put_padded(b1))
    stage(one.sweep, b1, right1, -1, own_rows + 2, own_rows + 2, window1, put_padded(a1))

    rows, columns = conc_new.shape[:2]
    wide = (PAD - HALO, columns + 2 * HALO)
    near_own = pl.ds(pl.multiple_of(at_y * own_columns, PAD), own_columns + 2 * PAD)
    for index in range(own_rows + 2):
        inside = 1 <= index <= rows1
        row = index - 1 if inside else (index - 1) % rows1
        for field, (source, target) in enumerate(((conc_in, fine_a0), (chem_in, fine_a1))):
            tile = a1[field][row, near_own, :]
            on_even = lane_even(tile.shape, 1)
            if inside:
                tile = jnp.where(on_even, tile, lane_roll(tile, 1))
            else:
                tile = jnp.where(on_even, lane_roll(tile, -1), tile)
            spread_rows(spread_fine.at[field], index, tile)
            both = spread_fine[field, index, pl.ds(wide[0] + PAD, wide[1]), :]
            for fine in (HALO - 2 + 2 * index, HALO - 1 + 2 * index):
                put_window((target,), wide)(fine, source[fine] + both)
    fine = fine_level(weights)
    right_side = (right_conc,)
    fine.sweep(
        (fine_a0, fine_a1), right_side, HALO - 1, rows + 2, rows + 2, wide,
        put_window((fine_b0, fine_b1), wide),
    )

    def put_new(row, conc_value, chem_value):
        conc_new[row - HALO] = conc_value
        chem_new[row - HALO] = chem_value

    fine.sweep((fine_b0, fine_b1), right_side, HALO, rows, rows, (PAD, columns), put_new)


def call_kernel(kernel, outs, scratch, *args, vmem_mib=8):
    shapes = tuple(jax.ShapeDtypeStruct(shape, jnp.float32) for shape in outs)
    return pl.pallas_call(
        kernel,
        out_shape=shapes,
        in_specs=[whole_block()] * len(args),
        out_specs=tuple(whole_block() for _ in outs),
        scratch_shapes=[pltpu.VMEM(shape, jnp.float32) for shape in scratch],
        compiler_params=pltpu.CompilerParams(vmem_limit_bytes=vmem_mib * 1024 * 1024),
    )(*args)


def shifted(values, axis, by):
    count = lax.axis_size(axis)
    return lax.ppermute(values, axis, [(i, (i + by) % count) for i in range(count)])


def swapped(values, axis, mask):
    count = lax.axis_size(axis)
    return lax.ppermute(values, axis, [(i, i ^ mask) for i in range(count)])


def far_masks():
    count_x, count_y = lax.axis_size("gx"), lax.axis_size("gy")
    return list(range(1, count_x)), list(range(2, count_y, 2))


def slot_masks():
    along_x, along_y = far_masks()
    first = [(0, 0)] + [(0, y) for y in along_y] + [(x, 0) for x in along_x]
    return first, [(x, y) for y in along_y for x in along_x]


def gathered(values):
    along_x, along_y = far_masks()
    across = jnp.stack([swapped(values, "gx", mask) for mask in along_x])
    beside = [swapped(values, "gy", mask) for mask in along_y]
    first = jnp.concatenate([jnp.stack([values] + beside), across], axis=0)
    second = jnp.concatenate([swapped(across, "gy", mask) for mask in along_y], axis=0)
    return first, second, swapped(first, "gy", 1), swapped(second, "gy", 1)


def two_phase_solve(conc, chem):
    rows, columns, lanes = conc.shape
    frame = (rows + 2 * HALO, columns + 2 * PAD, lanes)
    inner = (frame[0], columns + 2 * HALO, lanes)
    edge = (2, HALO, columns, lanes)
    block = (rows, columns, lanes)
    fields = jnp.concatenate([conc, chem], axis=0).reshape((2,) + block)
    side, corner = (rows, PAD, lanes), (2 * HALO, PAD, lanes)
    low, high, to_left, to_right = call_kernel(
        edges_kernel, (edge, edge, side, side), (), fields
    )
    before, after = shifted(high, "gx", 1), shifted(low, "gx", -1)
    sides = [shifted(to_right, "gy", 1), shifted(to_left, "gy", -1)]
    to_left, to_right = call_kernel(corners_kernel, (corner, corner), (), before, after)
    sides += [shifted(to_right, "gy", 1), shifted(to_left, "gy", -1)]
    packed, *kept = call_kernel(
        fine_down_kernel,
        ((3, rows // 4, columns // 2, lanes), (2,) + inner, frame, (7,) + inner),
        (frame,) * 4 + ((3, rows // 2, columns, lanes),),
        fields, before, after, *sides,
    )
    count_x, count_y = lax.axis_size("gx"), lax.axis_size("gy")
    grids = [(count_x * rows >> level + 1, count_y * columns >> level) for level in range(4)]
    scratch = []
    for level_rows, level_columns in grids[1:]:
        scratch += [(level_rows, level_columns + 2 * PAD, lanes)] * 5
        scratch += [(level_rows, level_columns, lanes)] * 9
    scratch += [(3, grids[2][0], grids[1][1], lanes), (3, grids[3][0], grids[2][1], lanes)]
    scratch += [(2, grids[2][0], grids[1][1], lanes), (2, grids[3][0], grids[2][1], lanes)]
    scratch += [(2, rows // 2 + 2, columns + 4 * PAD, lanes)] + [frame] * 4
    kernel = functools.partial(coarse_kernel, slot_masks(), (count_x, count_y))
    args = (*gathered(packed), *kept)
    return call_kernel(kernel, (block, block), scratch, *args, vmem_mib=24)


def body(conc_old, chem_old):
    rows, columns, lanes = conc_old.shape
    count_x, count_y = lax.axis_size("gx"), lax.axis_size("gy")
    grid_bytes = count_x * rows * count_y * columns * lanes
    if (
        grid_bytes <= GRID_BYTES_MAX
        and rows % 16 == 0
        and lanes % 128 == 0
        and count_x * rows >= 64
        and count_y * columns >= 64
        and count_x == 4
        and count_y >= 4
        and count_y & (count_y - 1) == 0
        and columns == 16
    ):
        return two_phase_solve(conc_old, chem_old)
    start_fields = jnp.stack([conc_old, chem_old])
    result = plain_solve(start_fields)
    return (result[0], result[1])


def solution(mesh):
    in_specs = (P(("img", "gx"), "gy", None), P(("img", "gx"), "gy", None))
    out_specs = (P(("img", "gx"), "gy", None), P(("img", "gx"), "gy", None))
    return jax.shard_map(body, mesh=mesh, in_specs=in_specs, out_specs=out_specs, check_vma=False)
```

```python
import functools

import jax
import jax.numpy as jnp
from jax import lax
from jax.experimental import pallas as pl
from jax.experimental.pallas import tpu as pltpu
from jax.sharding import PartitionSpec as P

LEVELS = 4
SWEEPS = 2
COARSE = 6


TIME_STEP = 32.0
GRADIENT_ENERGY = 0.5
STABILIZER = 2.0
DAMPING = 0.7


def extended(cells, sides, width):
    for axis, dim in sides:
        count = lax.axis_size(axis)
        head = lax.slice_in_dim(cells, 0, width, axis=dim)
        tail = lax.slice_in_dim(cells, cells.shape[dim] - width, cells.shape[dim], axis=dim)
        cells = jnp.concatenate(
            [
                lax.ppermute(tail, axis, [(i, (i + 1) % count) for i in range(count)]),
                cells,
                lax.ppermute(head, axis, [((i + 1) % count, i) for i in range(count)]),
            ],
            axis=dim,
        )
    return cells


def mobility_of(concentration):
    return 0.1 + jnp.square(1.0 - concentration * concentration)


def right_of(concentration):
    return jnp.stack(
        [
            concentration,
            concentration * concentration * concentration - (1.0 + STABILIZER) * concentration,
        ]
    )


def face_weights(mob_padded, level_scale):
    middle = mob_padded[1:-1, 1:-1, :]
    half_scale = 0.5 * level_scale
    weights = (
        half_scale * (middle + mob_padded[2:, 1:-1, :]),
        half_scale * (middle + mob_padded[:-2, 1:-1, :]),
        half_scale * (middle + mob_padded[1:-1, 2:, :]),
        half_scale * (middle + mob_padded[1:-1, :-2, :]),
        half_scale * (middle + jnp.roll(middle, -1, axis=2)),
        half_scale * (middle + jnp.roll(middle, 1, axis=2)),
    )
    total_weight = weights[0] + weights[1] + weights[2] + weights[3] + weights[4] + weights[5]
    return (weights, total_weight)


def neighbour_list(padded, middle):
    return (
        padded[2:, 1:-1, :],
        padded[:-2, 1:-1, :],
        padded[1:-1, 2:, :],
        padded[1:-1, :-2, :],
        jnp.roll(middle, -1, axis=2),
        jnp.roll(middle, 1, axis=2),
    )


def apply_operator(padded, weights, level_scale):
    middle = padded[:, 1:-1, 1:-1, :]
    conc_near = neighbour_list(padded[0], middle[0])
    chem_near = neighbour_list(padded[1], middle[1])
    flux = weights[0] * (chem_near[0] - middle[1])
    for position in range(1, 6):
        flux = flux + weights[position] * (chem_near[position] - middle[1])
    laplace = (
        conc_near[0]
        + conc_near[1]
        + conc_near[2]
        + conc_near[3]
        + conc_near[4]
        + conc_near[5]
        - 6.0 * middle[0]
    )
    first_eq = middle[0] - TIME_STEP * flux
    second_eq = middle[1] - STABILIZER * middle[0] + GRADIENT_ENERGY * level_scale * laplace
    return jnp.stack([first_eq, second_eq])


def update(residual, total_weight, level_scale):
    diagonal = STABILIZER + 6.0 * GRADIENT_ENERGY * level_scale
    coupling = TIME_STEP * total_weight
    determinant = 1.0 + coupling * diagonal
    conc_step = (residual[0] - coupling * residual[1]) / determinant
    chem_step = (residual[1] + diagonal * residual[0]) / determinant
    return DAMPING * jnp.stack([conc_step, chem_step])


def sweep_once(padded, right_side, mob_padded, level_scale):
    weights, total_weight = face_weights(mob_padded, level_scale)
    residual = right_side - apply_operator(padded, weights, level_scale)
    return padded[:, 1:-1, 1:-1, :] + update(residual, total_weight, level_scale)


def defect(padded, right_side, mob_padded, level_scale):
    weights = face_weights(mob_padded, level_scale)[0]
    return right_side - apply_operator(padded, weights, level_scale)


def coarsen(values):
    dims_now = values.shape
    grouped = values.reshape(
        dims_now[:-3] + (dims_now[-3] // 2, 2, dims_now[-2] // 2, 2, dims_now[-1] // 2, 2)
    )
    return jnp.sum(grouped, axis=(-5, -3, -1)) * 0.125


def refine(values):
    for axis_pos in (-3, -2, -1):
        values = jnp.repeat(values, 2, axis=axis_pos)
    return values


def trim_rim(values, width):
    return values[..., width:-width, width:-width, :]


def field_rim(fields):
    return extended(fields, (("gx", 1), ("gy", 2)), 1)


def coarsest_solve(right_side, mobility, level_scale):
    mob_padded = extended(mobility, (("gx", 0), ("gy", 1)), 1)
    fields = update(right_side, face_weights(mob_padded, level_scale)[1], level_scale)
    for sweep_index in range(COARSE - 1):
        padded = extended(fields, (("gx", 1), ("gy", 2)), 1)
        fields = sweep_once(padded, right_side, mob_padded, level_scale)
    return fields


def plain_solve(start_fields):
    outer_fields = field_rim(start_fields)
    mob_outer = mobility_of(outer_fields[0])
    mobility = trim_rim(mob_outer, 1)
    level_data = []
    for level_index in range(LEVELS - 1):
        if level_index == 0:
            mob_padded = mob_outer
        else:
            mob_padded = extended(mobility, (("gx", 0), ("gy", 1)), 1)
        level_data.append((mob_padded, 0.25**level_index))
        mobility = coarsen(mobility)
    coarsest_scale = 0.25 ** (LEVELS - 1)

    def cycle_level(level_index, right_side):
        if level_index == LEVELS - 1:
            return coarsest_solve(right_side, mobility, coarsest_scale)
        mob_padded, level_scale = level_data[level_index]
        if level_index == 0:
            fields = sweep_once(outer_fields, right_side, mob_padded, level_scale)
        else:
            fields = update(right_side, face_weights(mob_padded, level_scale)[1], level_scale)
        fields = sweep_once(field_rim(fields), right_side, mob_padded, level_scale)
        residual = defect(field_rim(fields), right_side, mob_padded, level_scale)
        fields = fields + refine(cycle_level(level_index + 1, coarsen(residual)))
        for sweep_index in range(SWEEPS):
            fields = sweep_once(field_rim(fields), right_side, mob_padded, level_scale)
        return fields

    return cycle_level(0, right_of(start_fields[0]))


HALO = 4
PAD = 8
GRID_BYTES_MAX = 2 * 1024 * 1024


def whole_block():
    return pl.BlockSpec(memory_space=pltpu.VMEM)


def lane_roll(values, shift):
    return pltpu.roll(values, shift % values.shape[1], axis=1)


def lane_even(shape, dup):
    return (lax.broadcasted_iota(jnp.int32, shape, 1) // dup) % 2 == 0


def loop_rows(count, unroll, row_group):
    steps, rest = divmod(count, unroll)
    if steps == 1:
        row_group(0, unroll)
    elif steps > 1:

        def step(index, carry):
            row_group(index * unroll, unroll)
            return carry

        lax.fori_loop(0, steps, step, 0)
    if rest:
        row_group(steps * unroll, rest)


def lane_swap(values):
    return jnp.where(lane_even(values.shape, 1), lane_roll(values, -1), lane_roll(values, 1))


class RowCache:
    def __init__(self, ref, rows, first, width):
        self.ref, self.rows, self.first, self.width = ref, rows, first, width
        self.values = {}

    def __getitem__(self, key):
        if key not in self.values:
            total = self.ref.shape[0]
            row = key if self.rows is None else self.rows[key]
            outside = isinstance(row, int) and not 0 <= row < total
            values = self.ref[row % total if outside else row, pl.ds(self.first, self.width), :]
            self.values[key] = lane_swap(values) if outside else values
        return self.values[key]


def stage(run, *args):
    pl.when(lax.axis_index("gy") >= 0)(functools.partial(run, *args))


def chem_right(conc):
    return conc * (conc * conc - (1.0 + STABILIZER))


class Rows:
    def __init__(self, total, *parts):
        self.places = {
            row: (ref, index) for ref, rows in parts for index, row in enumerate(rows)
        }
        self.shape = (total,) + parts[0][0].shape[1:]

    def place(self, at):
        row, *rest = at if isinstance(at, tuple) else (at,)
        ref, index = self.places[row]
        return ref, (index, *rest)

    def __getitem__(self, at):
        ref, index = self.place(at)
        return ref[index]

    def __setitem__(self, at, values):
        ref, index = self.place(at)
        ref[index] = values


class Level:
    def __init__(self, level_index, weights, weights_from=PAD, right_from=PAD):
        self.scale = 0.25**level_index
        self.dup = 2**level_index
        self.diagonal = STABILIZER + 6.0 * GRADIENT_ENERGY * self.scale
        self.weights = weights
        self.weights_from, self.right_from = weights_from, right_from

    def set_weights(self, mobility, count, start=0):
        width = self.weights[0].shape[1]
        half = 0.5 * self.scale * TIME_STEP
        face_x, up_y, down_y, up_z, down_z, coupling, gain = self.weights

        def at(row, shift=0):
            return mobility[row, pl.ds(self.weights_from + shift, width), :]

        def group(first, size):
            rows = RowCache(mobility, None, self.weights_from, width)
            before = half * (rows[start + first - 1] + rows[start + first])
            for i in range(size):
                r = start + first + i
                here = rows[r]
                after = half * (here + rows[r + 1])
                to_up_y = half * (here + at(r, 1))
                to_down_y = half * (here + at(r, -1))
                to_up_z = half * (here + lane_roll(here, -self.dup))
                to_down_z = half * (here + lane_roll(here, self.dup))
                total_weight = (before + after) + (to_up_y + to_down_y) + (to_up_z + to_down_z)
                face_x[r] = after
                up_y[r] = to_up_y
                down_y[r] = to_down_y
                up_z[r] = to_up_z
                down_z[r] = to_down_z
                coupling[r] = total_weight
                gain[r] = DAMPING / (1.0 + total_weight * self.diagonal)
                before = after

        loop_rows(count, count, group)

    def residuals(self, fields, right, rows, window, fields_from=0):
        conc, chem = fields
        first, width = window
        face_x, up_y, down_y, up_z, down_z, coupling, gain = self.weights

        def at(ref, row, shift=0):
            return ref[row, pl.ds(first - fields_from + shift, width), :]

        def weight(ref, row):
            return ref[row, pl.ds(first - self.weights_from, width), :]

        def right_at(row):
            values = [ref[row, pl.ds(first - self.right_from, width), :] for ref in right]
            return values if len(values) == 2 else values + [chem_right(values[0])]

        total = conc.shape[0]
        if isinstance(rows[0], int):
            centres, listed = [row % total for row in rows[1:-1]], None
        else:
            centres, listed = range(1, len(rows) - 1), rows
        u = RowCache(chem, listed, first - fields_from, width)
        c = RowCache(conc, listed, first - fields_from, width)
        across = RowCache(face_x, listed, first - self.weights_from, width)
        for key in centres:
            r = key if listed is None else listed[key]
            c_here, u_here = c[key], u[key]
            here = weight(coupling, r)
            flux = across[key] * u[key + 1] + across[key - 1] * u[key - 1]
            flux = flux + weight(up_y, r) * at(chem, r, 1) + weight(down_y, r) * at(chem, r, -1)
            flux = flux + weight(up_z, r) * lane_roll(u_here, -self.dup)
            flux = flux + weight(down_z, r) * lane_roll(u_here, self.dup)
            near = (c[key - 1] + c[key + 1]) + (at(conc, r, 1) + at(conc, r, -1))
            near = near + (lane_roll(c_here, self.dup) + lane_roll(c_here, -self.dup))
            conc_right, chem_right_here = right_at(r)
            conc_left = conc_right - c_here + (flux - here * u_here)
            chem_left = chem_right_here - u_here + self.diagonal * c_here
            chem_left = chem_left - (GRADIENT_ENERGY * self.scale) * near
            yield r, c_here, u_here, conc_left, chem_left, here, weight(gain, r)

    def steps(self, conc_left, chem_left, coupling, gain):
        return (
            gain * (conc_left - coupling * chem_left),
            gain * (chem_left + self.diagonal * conc_left),
        )

    def first_sweep(self, right, unroll, put):
        coupling, gain = self.weights[5:]

        def group(first, size):
            for i in range(size):
                r = first + i
                put(r, *self.steps(right[0][r], right[1][r], coupling[r], gain[r]))

        loop_rows(right[0].shape[0], unroll, group)

    def row_window(self, start, first, size):
        return [start + first + i - 1 for i in range(size + 2)]

    def sweep(self, fields, right, start, count, unroll, window, put):
        def group(first, size):
            rows = self.row_window(start, first, size)
            for r, c, u, *left in self.residuals(fields, right, rows, window):
                conc_step, chem_step = self.steps(*left)
                put(r, c + conc_step, u + chem_step)

        loop_rows(count, unroll, group)

    def coarse_right(self, fields, right, start, count, unroll, window, put, fields_from=0):
        def group(first, size):
            rows = self.row_window(start, first, size)
            items = self.residuals(fields, right, rows, window, fields_from)
            half = first // 2 if isinstance(first, int) else lax.shift_right_logical(first, 1)
            kept = None
            for i, (_, _, _, conc_left, chem_left, _, _) in enumerate(items):
                if i % 2 == 0:
                    kept = conc_left, chem_left
                else:
                    put(half + i // 2, kept[0] + conc_left, kept[1] + chem_left)

        loop_rows(count, unroll, group)


def put_padded(refs):
    def put(row, *values):
        for ref, value in zip(refs, values):
            width = value.shape[0]
            ref[row, PAD : PAD + width, :] = value
            ref[row, :PAD, :] = value[width - PAD :]
            ref[row, PAD + width :, :] = value[:PAD]

    return put


def put_window(refs, window):
    def put(row, *values):
        for ref, value in zip(refs, values):
            ref[row, window[0] : window[0] + window[1], :] = value

    return put


def put_sums(sums, offset=0):
    def put(row, *values):
        for field, value in enumerate(values):
            sums[field, offset + row] = value

    return put


def pair_rows(ref, row, count):
    return ref[row, pl.ds(0, count, stride=2), :] + ref[row, pl.ds(1, count, stride=2), :]


def spread_rows(ref, row, values):
    count = values.shape[0]
    ref[row, pl.ds(0, count, stride=2), :] = values
    ref[row, pl.ds(1, count, stride=2), :] = values


def pair_lanes(values, dup):
    other = jnp.where(
        lane_even(values.shape, dup), lane_roll(values, -dup), lane_roll(values, dup)
    )
    return values + other


def side_tiles(conc, chem, to_left, to_right, at, low):
    columns = conc.shape[0]
    to_left[at] = jnp.where(low, conc[:PAD], half_turn(chem[:PAD]))
    to_right[at] = jnp.where(low, half_turn(chem[columns - PAD :]), conc[columns - PAD :])


def low_half(lanes):
    return lax.broadcasted_iota(jnp.int32, (PAD, lanes), 0) < HALO


def edges_kernel(fields, low_rows, high_rows, to_left, to_right):
    rows, columns, lanes = fields.shape[1:]
    low_rows[...] = fields[:, :HALO]
    high_rows[...] = fields[:, rows - HALO :]
    for row in range(rows):
        side_tiles(fields[0, row], fields[1, row], to_left, to_right, row, low_half(lanes))


def corners_kernel(before, after, to_left, to_right):
    lanes = before.shape[-1]
    for at in range(2 * HALO):
        source, row = (before, at) if at < HALO else (after, at - HALO)
        side_tiles(source[0, row], source[1, row], to_left, to_right, at, low_half(lanes))


def frame_row(row, rows, own, before, after):
    if row < HALO:
        return before[row]
    if row < HALO + rows:
        return own[row - HALO]
    return after[row - HALO - rows]


def half_turn(values):
    return pltpu.roll(values, HALO, axis=0)


class FrameRows:
    def __init__(self, rows):
        self.total = rows + 2 * HALO
        end = self.total
        self.own = range(HALO, end - HALO)
        self.weights_early = range(HALO + 1, end - HALO - 1)
        self.swept_early = range(HALO + 2, end - HALO - 2)
        self.joined = [HALO + 1, HALO + 2, end - HALO - 3, end - HALO - 2]
        self.weights_late = [*range(2, HALO + 1), *range(end - HALO - 1, end - 3)]
        self.weights_outer = [0, 1, end - 3, end - 2, end - 1]
        self.right_late = [HALO - 1, end - HALO]
        self.right_outer = [*range(HALO - 1), *range(end - HALO + 1, end)]
        self.swept_late = [*range(2, HALO + 2), *range(end - HALO - 2, end - 2)]
        self.mid_late = [*range(1, HALO + 1), *range(end - HALO - 1, end - 1)]

    def weights(self, early, late):
        return [
            Rows(self.total, (early.at[i], self.weights_early), (late.at[i], self.weights_late))
            for i in range(7)
        ]

    def swept(self, early, late):
        return [
            Rows(self.total, (early.at[i], self.swept_early), (late.at[i], self.swept_late))
            for i in range(2)
        ]


def fine_level(weights):
    return Level(0, weights, HALO, 0)


def set_row(conc, chem, left, right, row, conc_at, chem_at, mobility):
    c = jnp.concatenate([left, conc, right])
    if conc_at is not None:
        conc_at[row] = c
    chem_at[row] = jnp.concatenate([half_turn(left), chem, half_turn(right)])
    gap = 1.0 - c * c
    mobility[row] = 0.1 + gap * gap


def pack(sums, field, index, out):
    count = sums.shape[2] // 2
    even = lane_even((count, sums.shape[3]), 1)
    a = pair_rows(sums.at[field], 2 * index, count)
    b = pair_rows(sums.at[field], 2 * index + 1, count)
    out[field, index] = 0.125 * jnp.where(even, a + lane_roll(a, -1), b + lane_roll(b, 1))


def early_kernel(
    fields, own_left, own_right,
    packed, kept, right_conc, all_weights, joined,
    chem_start, mobility, mid, outer, sums,
):
    rows, columns = fields.shape[1:3]
    at = FrameRows(rows)
    right_side = (Rows(at.total, (right_conc, at.own)),)
    for row in at.own:
        i = row - HALO
        set_row(
            fields[0, i], fields[1, i], own_left[i], own_right[i],
            row, right_side[0], chem_start, mobility,
        )
    weights = [
        Rows(at.total, (all_weights.at[i], at.weights_early), (outer.at[i], [HALO]))
        for i in range(7)
    ]
    level = fine_level(weights)
    level.set_weights(mobility, rows - 1, HALO)
    wide = (PAD - HALO, columns + 2 * HALO)
    middle = [r for r in at.weights_early if r not in at.joined]
    mids = [
        Rows(at.total, (mid.at[i], middle), (joined.at[i], at.joined)) for i in range(2)
    ]
    swept = [Rows(at.total, (kept.at[i], at.swept_early)) for i in range(2)]
    level.sweep(
        (right_side[0], chem_start), right_side, HALO + 1, rows - 2, rows - 2, wide,
        put_window(mids, wide),
    )
    level.sweep(
        mids, right_side, HALO + 2, rows - 4, rows - 4, wide, put_window(swept, (0, wide[1]))
    )
    level.coarse_right(
        swept, right_side, 2 * HALO, rows - 2 * HALO, rows - 2 * HALO, (PAD, columns),
        put_sums(sums, HALO // 2), wide[0],
    )
    own = slice(PAD, PAD + columns)
    for index in range(rows // 2):
        row = HALO + 2 * index
        sums[2, index] = mobility[row, own, :] + mobility[row + 1, own, :]
    for index in range(rows // 4):
        pack(sums, 2, index, packed)
        if HALO // 4 <= index < (rows - HALO) // 4:
            pack(sums, 0, index, packed)
            pack(sums, 1, index, packed)
        else:
            packed[0, index] = jnp.zeros(packed.shape[2:], jnp.float32)
            packed[1, index] = jnp.zeros(packed.shape[2:], jnp.float32)


def late_kernel(
    fields, before, after, own_left, own_right, corner_left, corner_right,
    packed_early, kept_early, right_early, weights_early, joined,
    packed, kept, right_conc, all_weights,
    chem_start, mobility, mid, outer, right_outer, sums,
):
    rows, columns = fields.shape[1:3]
    at = FrameRows(rows)
    end = at.total
    right = Rows(
        end, (right_early, at.own), (right_conc, at.right_late), (right_outer, at.right_outer)
    )
    for row in [*range(HALO + 2), *range(end - HALO - 2, end)]:
        if row in at.own:
            i = row - HALO
            values = fields[0, i], fields[1, i], own_left[i], own_right[i]
            set_row(*values, row, None, chem_start, mobility)
        else:
            source, i = (before, row) if row < HALO else (after, row - rows - HALO)
            corner = row if row < HALO else row - rows
            values = source[0, i], source[1, i], corner_left[corner], corner_right[corner]
            set_row(*values, row, right, chem_start, mobility)
    weights = at.weights(weights_early, all_weights)
    for i, one in enumerate(weights):
        for index, row in enumerate(at.weights_outer):
            one.places[row] = outer.at[i], index
    level = fine_level(weights)
    level.set_weights(mobility, HALO + 1, 0)
    level.set_weights(mobility, HALO + 1, end - HALO - 1)
    wide = (PAD - HALO, columns + 2 * HALO)
    mids = [Rows(end, (joined.at[i], at.joined), (mid.at[i], at.mid_late)) for i in range(2)]
    swept = at.swept(kept_early, kept)
    for start in (1, end - HALO - 1):
        level.sweep(
            (right, chem_start), (right,), start, HALO, HALO, wide, put_window(mids, wide)
        )
    for start in (2, end - HALO - 2):
        level.sweep(mids, (right,), start, HALO, HALO, wide, put_window(swept, (0, wide[1])))
    for start in (HALO, end - 2 * HALO):
        level.coarse_right(
            swept, (right,), start, HALO, HALO, (PAD, columns),
            put_sums(sums, (start - HALO) // 2), wide[0],
        )
    packed[...] = packed_early[...]
    for index in range(rows // 4):
        if not HALO // 4 <= index < (rows - HALO) // 4:
            pack(sums, 0, index, packed)
            pack(sums, 1, index, packed)


def coarse_kernel(
    slots, grid, first, second, first_far, second_far,
    kept_early, right_early, weights_early, kept_late, right_late, weights_late,
    conc_new, chem_new, *scratch,
):
    at = FrameRows(conc_new.shape[0])
    conc_in, chem_in = at.swept(kept_early, kept_late)
    weights = at.weights(weights_early, weights_late)
    right_conc = Rows(at.total, (right_early, at.own), (right_late, at.right_late))
    scratch = list(scratch)
    start_even, at_y = lax.axis_index("gx") % 2 == 0, lax.axis_index("gy")
    levels = []
    for level_index in (1, 2, 3):
        level = Level(level_index, scratch[5:14][2:])
        mobility, a, b, right = scratch[0], scratch[1:3], scratch[3:5], scratch[5:7]
        levels.append((level, mobility, right, a, b))
        del scratch[:14]
    sums1, sums2, spread2, spread3, spread_fine, fine_a0, fine_a1, fine_b0, fine_b1 = scratch
    one, mob1, right1, a1, b1 = levels[0]
    two, mob2, right2, a2, b2 = levels[1]
    three, mob3, right3, a3, b3 = levels[2]
    rows1, columns1, lanes = right1[0].shape
    rows2, columns2 = right2[0].shape[:2]
    rows3, columns3 = right3[0].shape[:2]
    window1, window2, window3 = (PAD, columns1), (PAD, columns2), (PAD, columns3)
    own_rows, own_columns = 2 * rows1 // grid[0], columns1 // grid[1]
    even = lane_even((own_columns, lanes), 1)
    blocks = {}
    for last, sources in enumerate(((first, second), (first_far, second_far))):
        for source, masks in zip(sources, slots):
            for slot, (mask_x, mask_y) in enumerate(masks):
                blocks[mask_x, mask_y ^ last] = source.at[slot]

    for mask_y in range(grid[1]):
        offset = (at_y ^ mask_y) * own_columns
        plain = pl.ds(pl.multiple_of(offset, PAD), own_columns)
        padded = pl.ds(pl.multiple_of(offset + PAD, PAD), own_columns)
        for field, (ref, at) in enumerate(
            ((right1[0], plain), (right1[1], plain), (mob1, padded))
        ):
            for index in range(own_rows // 2):
                own, two_on, one_on, one_back = (
                    blocks[mask_x, mask_y][field, index] for mask_x in (0, 2, 1, 3)
                )
                swap = one_on, one_back
                one_on = jnp.where(start_even, swap[0], swap[1])
                one_back = jnp.where(start_even, swap[1], swap[0])
                for row, a, b in ((0, own, two_on), (own_rows, one_on, one_back)):
                    row = row + 2 * index
                    ref[row, at, :] = jnp.where(even, a, lane_roll(b, 1))
                    ref[row + 1, at, :] = jnp.where(even, lane_roll(a, -1), b)
    for row in range(rows1):
        mob1[row, :PAD, :] = mob1[row, columns1 : columns1 + PAD, :]
        mob1[row, PAD + columns1 :, :] = mob1[row, PAD : 2 * PAD, :]

    def coarsen(mobility, sums, out, out_mobility, dup):
        count, columns = out[0].shape[:2]
        fine = pl.ds(PAD, 2 * columns)
        for index in range(count):
            sums[2, index] = mobility[2 * index, fine, :] + mobility[2 * index + 1, fine, :]
        for index in range(count):
            for field in range(2):
                half = pair_rows(sums.at[field], index, columns)
                out[field][index] = 0.125 * pair_lanes(half, dup)
            half = pair_rows(sums.at[2], index, columns)
            put_padded((out_mobility,))(index, 0.125 * pair_lanes(half, dup))

    stage(one.set_weights, mob1, rows1)
    stage(one.first_sweep, right1, rows1, put_padded(a1))
    stage(one.sweep, a1, right1, 0, rows1, rows1, window1, put_padded(b1))
    stage(one.coarse_right, b1, right1, 0, rows1, rows1, window1, put_sums(sums1))
    stage(coarsen, mob1, sums1, right2, mob2, 2)

    stage(two.set_weights, mob2, rows2)
    stage(two.first_sweep, right2, rows2, put_padded(a2))
    stage(two.sweep, a2, right2, 0, rows2, rows2, window2, put_padded(b2))
    stage(two.coarse_right, b2, right2, 0, rows2, rows2, window2, put_sums(sums2))
    stage(coarsen, mob2, sums2, right3, mob3, 4)

    stage(three.set_weights, mob3, rows3)
    stage(three.first_sweep, right3, rows3, put_padded(a3))
    now, other = a3, b3
    for sweep_index in range(COARSE - 1):
        stage(three.sweep, now, right3, 0, rows3, rows3, window3, put_padded(other))
        now, other = other, now

    def correct(coarse, coarse_row, fine_in, fine_out, spread, index):
        for field in range(2):
            columns = fine_in[field].shape[1] - 2 * PAD
            spread_rows(
                spread.at[field], index, coarse[field][coarse_row, pl.ds(PAD, columns // 2), :]
            )
            both = spread[field, index]
            for row in (2 * coarse_row, 2 * coarse_row + 1):
                put_padded((fine_out[field],))(
                    row, fine_in[field][row, pl.ds(PAD, columns), :] + both
                )

    for row in range(rows3):
        correct(now, row, b2, a2, spread3, row)
    stage(two.sweep, a2, right2, 0, rows2, rows2, window2, put_padded(b2))
    stage(two.sweep, b2, right2, 0, rows2, rows2, window2, put_padded(a2))
    for row in range(rows2):
        correct(a2, row, b1, a1, spread2, row)
    stage(one.sweep, a1, right1, -2, own_rows + 4, own_rows + 4, window1, put_padded(b1))
    stage(one.sweep, b1, right1, -1, own_rows + 2, own_rows + 2, window1, put_padded(a1))

    rows, columns = conc_new.shape[:2]
    wide = (PAD - HALO, columns + 2 * HALO)
    near_own = pl.ds(pl.multiple_of(at_y * own_columns, PAD), own_columns + 2 * PAD)
    for index in range(own_rows + 2):
        inside = 1 <= index <= rows1
        row = index - 1 if inside else (index - 1) % rows1
        for field, (source, target) in enumerate(((conc_in, fine_a0), (chem_in, fine_a1))):
            tile = a1[field][row, near_own, :]
            on_even = lane_even(tile.shape, 1)
            if inside:
                tile = jnp.where(on_even, tile, lane_roll(tile, 1))
            else:
                tile = jnp.where(on_even, lane_roll(tile, -1), tile)
            spread_rows(spread_fine.at[field], index, tile)
            both = spread_fine[field, index, pl.ds(wide[0] + PAD, wide[1]), :]
            for fine in (HALO - 2 + 2 * index, HALO - 1 + 2 * index):
                put_window((target,), wide)(fine, source[fine] + both)
    fine = fine_level(weights)
    right_side = (right_conc,)
    fine.sweep(
        (fine_a0, fine_a1), right_side, HALO - 1, rows + 2, rows + 2, wide,
        put_window((fine_b0, fine_b1), wide),
    )

    def put_new(row, conc_value, chem_value):
        conc_new[row - HALO] = conc_value
        chem_new[row - HALO] = chem_value

    fine.sweep((fine_b0, fine_b1), right_side, HALO, rows, rows, (PAD, columns), put_new)


def call_kernel(kernel, outs, scratch, *args, vmem_mib=8):
    shapes = tuple(jax.ShapeDtypeStruct(shape, jnp.float32) for shape in outs)
    return pl.pallas_call(
        kernel,
        out_shape=shapes,
        in_specs=[whole_block()] * len(args),
        out_specs=tuple(whole_block() for _ in outs),
        scratch_shapes=[pltpu.VMEM(shape, jnp.float32) for shape in scratch],
        compiler_params=pltpu.CompilerParams(vmem_limit_bytes=vmem_mib * 1024 * 1024),
    )(*args)


def shifted(values, axis, by):
    count = lax.axis_size(axis)
    return lax.ppermute(values, axis, [(i, (i + by) % count) for i in range(count)])


def swapped(values, axis, mask):
    count = lax.axis_size(axis)
    return lax.ppermute(values, axis, [(i, i ^ mask) for i in range(count)])


def far_masks():
    count_x, count_y = lax.axis_size("gx"), lax.axis_size("gy")
    return list(range(1, count_x)), list(range(2, count_y, 2))


def slot_masks():
    along_x, along_y = far_masks()
    first = [(0, 0)] + [(0, y) for y in along_y] + [(x, 0) for x in along_x]
    return first, [(x, y) for y in along_y for x in along_x]


def gathered(values):
    along_x, along_y = far_masks()
    across = jnp.stack([swapped(values, "gx", mask) for mask in along_x])
    beside = [swapped(values, "gy", mask) for mask in along_y]
    first = jnp.concatenate([jnp.stack([values] + beside), across], axis=0)
    second = jnp.concatenate([swapped(across, "gy", mask) for mask in along_y], axis=0)
    return first, second, swapped(first, "gy", 1), swapped(second, "gy", 1)


def two_phase_solve(conc, chem):
    rows, columns, lanes = conc.shape
    frame = (rows + 2 * HALO, columns + 2 * PAD, lanes)
    edge = (2, HALO, columns, lanes)
    block = (rows, columns, lanes)
    fields = jnp.concatenate([conc, chem], axis=0).reshape((2,) + block)
    side, corner = (rows, PAD, lanes), (2 * HALO, PAD, lanes)
    low, high, to_left, to_right = call_kernel(
        edges_kernel, (edge, edge, side, side), (), fields
    )
    before, after = shifted(high, "gx", 1), shifted(low, "gx", -1)
    sides = [shifted(to_right, "gy", 1), shifted(to_left, "gy", -1)]
    to_left, to_right = call_kernel(corners_kernel, (corner, corner), (), before, after)
    sides += [shifted(to_right, "gy", 1), shifted(to_left, "gy", -1)]
    at, width = FrameRows(rows), columns + 2 * HALO
    packed_shape, sums = (3, rows // 4, columns // 2, lanes), (3, rows // 2, columns, lanes)

    def part(count, listed, wide):
        return (count, len(listed), wide, lanes)

    right_shapes = [part(0, listed, frame[1])[1:] for listed in (at.own, at.right_late, at.right_outer)]
    early, *kept = call_kernel(
        early_kernel,
        (
            packed_shape, part(2, at.swept_early, width), right_shapes[0],
            part(7, at.weights_early, width), part(2, at.joined, frame[1]),
        ),
        (frame, frame, part(2, at.weights_early, frame[1]), part(7, [0], width), sums),
        fields, *sides[:2],
    )
    packed, *kept_late = call_kernel(
        late_kernel,
        (
            packed_shape, part(2, at.swept_late, width), right_shapes[1],
            part(7, at.weights_late, width),
        ),
        (
            frame, frame, part(2, at.mid_late, frame[1]), part(7, at.weights_outer, width),
            right_shapes[2], sums,
        ),
        fields, before, after, *sides, early, *kept,
    )
    count_x, count_y = lax.axis_size("gx"), lax.axis_size("gy")
    grids = [(count_x * rows >> level + 1, count_y * columns >> level) for level in range(4)]
    scratch = []
    for level_rows, level_columns in grids[1:]:
        scratch += [(level_rows, level_columns + 2 * PAD, lanes)] * 5
        scratch += [(level_rows, level_columns, lanes)] * 9
    scratch += [(3, grids[2][0], grids[1][1], lanes), (3, grids[3][0], grids[2][1], lanes)]
    scratch += [(2, grids[2][0], grids[1][1], lanes), (2, grids[3][0], grids[2][1], lanes)]
    scratch += [(2, rows // 2 + 2, columns + 4 * PAD, lanes)] + [frame] * 4
    kernel = functools.partial(coarse_kernel, slot_masks(), (count_x, count_y))
    args = (*gathered(packed), *kept[:3], *kept_late)
    return call_kernel(kernel, (block, block), scratch, *args, vmem_mib=24)


def body(conc_old, chem_old):
    rows, columns, lanes = conc_old.shape
    count_x, count_y = lax.axis_size("gx"), lax.axis_size("gy")
    grid_bytes = count_x * rows * count_y * columns * lanes
    if (
        grid_bytes <= GRID_BYTES_MAX
        and rows % 16 == 0
        and lanes % 128 == 0
        and count_x * rows >= 64
        and count_y * columns >= 64
        and count_x == 4
        and count_y >= 4
        and count_y & (count_y - 1) == 0
        and columns == 16
    ):
        return two_phase_solve(conc_old, chem_old)
    start_fields = jnp.stack([conc_old, chem_old])
    result = plain_solve(start_fields)
    return (result[0], result[1])


def solution(mesh):
    in_specs = (P(("img", "gx"), "gy", None), P(("img", "gx"), "gy", None))
    out_specs = (P(("img", "gx"), "gy", None), P(("img", "gx"), "gy", None))
    return jax.shard_map(body, mesh=mesh, in_specs=in_specs, out_specs=out_specs, check_vma=False)
```

```python
import functools

import jax
import jax.numpy as jnp
from jax import lax
from jax.experimental import pallas as pl
from jax.experimental.pallas import tpu as pltpu
from jax.sharding import PartitionSpec as P

LEVELS = 4
SWEEPS = 2
COARSE = 6


TIME_STEP = 32.0
GRADIENT_ENERGY = 0.5
STABILIZER = 2.0
DAMPING = 0.7


def extended(cells, sides, width):
    for axis, dim in sides:
        count = lax.axis_size(axis)
        head = lax.slice_in_dim(cells, 0, width, axis=dim)
        tail = lax.slice_in_dim(cells, cells.shape[dim] - width, cells.shape[dim], axis=dim)
        cells = jnp.concatenate(
            [
                lax.ppermute(tail, axis, [(i, (i + 1) % count) for i in range(count)]),
                cells,
                lax.ppermute(head, axis, [((i + 1) % count, i) for i in range(count)]),
            ],
            axis=dim,
        )
    return cells


def mobility_of(concentration):
    return 0.1 + jnp.square(1.0 - concentration * concentration)


def right_of(concentration):
    return jnp.stack(
        [
            concentration,
            concentration * concentration * concentration - (1.0 + STABILIZER) * concentration,
        ]
    )


def face_weights(mob_padded, level_scale):
    middle = mob_padded[1:-1, 1:-1, :]
    half_scale = 0.5 * level_scale
    weights = (
        half_scale * (middle + mob_padded[2:, 1:-1, :]),
        half_scale * (middle + mob_padded[:-2, 1:-1, :]),
        half_scale * (middle + mob_padded[1:-1, 2:, :]),
        half_scale * (middle + mob_padded[1:-1, :-2, :]),
        half_scale * (middle + jnp.roll(middle, -1, axis=2)),
        half_scale * (middle + jnp.roll(middle, 1, axis=2)),
    )
    total_weight = weights[0] + weights[1] + weights[2] + weights[3] + weights[4] + weights[5]
    return (weights, total_weight)


def neighbour_list(padded, middle):
    return (
        padded[2:, 1:-1, :],
        padded[:-2, 1:-1, :],
        padded[1:-1, 2:, :],
        padded[1:-1, :-2, :],
        jnp.roll(middle, -1, axis=2),
        jnp.roll(middle, 1, axis=2),
    )


def apply_operator(padded, weights, level_scale):
    middle = padded[:, 1:-1, 1:-1, :]
    conc_near = neighbour_list(padded[0], middle[0])
    chem_near = neighbour_list(padded[1], middle[1])
    flux = weights[0] * (chem_near[0] - middle[1])
    for position in range(1, 6):
        flux = flux + weights[position] * (chem_near[position] - middle[1])
    laplace = (
        conc_near[0]
        + conc_near[1]
        + conc_near[2]
        + conc_near[3]
        + conc_near[4]
        + conc_near[5]
        - 6.0 * middle[0]
    )
    first_eq = middle[0] - TIME_STEP * flux
    second_eq = middle[1] - STABILIZER * middle[0] + GRADIENT_ENERGY * level_scale * laplace
    return jnp.stack([first_eq, second_eq])


def update(residual, total_weight, level_scale):
    diagonal = STABILIZER + 6.0 * GRADIENT_ENERGY * level_scale
    coupling = TIME_STEP * total_weight
    determinant = 1.0 + coupling * diagonal
    conc_step = (residual[0] - coupling * residual[1]) / determinant
    chem_step = (residual[1] + diagonal * residual[0]) / determinant
    return DAMPING * jnp.stack([conc_step, chem_step])


def sweep_once(padded, right_side, mob_padded, level_scale):
    weights, total_weight = face_weights(mob_padded, level_scale)
    residual = right_side - apply_operator(padded, weights, level_scale)
    return padded[:, 1:-1, 1:-1, :] + update(residual, total_weight, level_scale)


def defect(padded, right_side, mob_padded, level_scale):
    weights = face_weights(mob_padded, level_scale)[0]
    return right_side - apply_operator(padded, weights, level_scale)


def coarsen(values):
    dims_now = values.shape
    grouped = values.reshape(
        dims_now[:-3] + (dims_now[-3] // 2, 2, dims_now[-2] // 2, 2, dims_now[-1] // 2, 2)
    )
    return jnp.sum(grouped, axis=(-5, -3, -1)) * 0.125


def refine(values):
    for axis_pos in (-3, -2, -1):
        values = jnp.repeat(values, 2, axis=axis_pos)
    return values


def trim_rim(values, width):
    return values[..., width:-width, width:-width, :]


def field_rim(fields):
    return extended(fields, (("gx", 1), ("gy", 2)), 1)


def coarsest_solve(right_side, mobility, level_scale):
    mob_padded = extended(mobility, (("gx", 0), ("gy", 1)), 1)
    fields = update(right_side, face_weights(mob_padded, level_scale)[1], level_scale)
    for sweep_index in range(COARSE - 1):
        padded = extended(fields, (("gx", 1), ("gy", 2)), 1)
        fields = sweep_once(padded, right_side, mob_padded, level_scale)
    return fields


def plain_solve(start_fields):
    outer_fields = field_rim(start_fields)
    mob_outer = mobility_of(outer_fields[0])
    mobility = trim_rim(mob_outer, 1)
    level_data = []
    for level_index in range(LEVELS - 1):
        if level_index == 0:
            mob_padded = mob_outer
        else:
            mob_padded = extended(mobility, (("gx", 0), ("gy", 1)), 1)
        level_data.append((mob_padded, 0.25**level_index))
        mobility = coarsen(mobility)
    coarsest_scale = 0.25 ** (LEVELS - 1)

    def cycle_level(level_index, right_side):
        if level_index == LEVELS - 1:
            return coarsest_solve(right_side, mobility, coarsest_scale)
        mob_padded, level_scale = level_data[level_index]
        if level_index == 0:
            fields = sweep_once(outer_fields, right_side, mob_padded, level_scale)
        else:
            fields = update(right_side, face_weights(mob_padded, level_scale)[1], level_scale)
        fields = sweep_once(field_rim(fields), right_side, mob_padded, level_scale)
        residual = defect(field_rim(fields), right_side, mob_padded, level_scale)
        fields = fields + refine(cycle_level(level_index + 1, coarsen(residual)))
        for sweep_index in range(SWEEPS):
            fields = sweep_once(field_rim(fields), right_side, mob_padded, level_scale)
        return fields

    return cycle_level(0, right_of(start_fields[0]))


HALO = 4
PAD = 8
GRID_BYTES_MAX = 2 * 1024 * 1024


def whole_block():
    return pl.BlockSpec(memory_space=pltpu.VMEM)


def lane_roll(values, shift):
    return pltpu.roll(values, shift % values.shape[1], axis=1)


def lane_even(shape, dup):
    return (lax.broadcasted_iota(jnp.int32, shape, 1) // dup) % 2 == 0


def loop_rows(count, unroll, row_group):
    steps, rest = divmod(count, unroll)
    if steps == 1:
        row_group(0, unroll)
    elif steps > 1:

        def step(index, carry):
            row_group(index * unroll, unroll)
            return carry

        lax.fori_loop(0, steps, step, 0)
    if rest:
        row_group(steps * unroll, rest)


def lane_swap(values):
    return jnp.where(lane_even(values.shape, 1), lane_roll(values, -1), lane_roll(values, 1))


class RowCache:
    def __init__(self, ref, rows, first, width):
        self.ref, self.rows, self.first, self.width = ref, rows, first, width
        self.values = {}

    def __getitem__(self, key):
        if key not in self.values:
            total = self.ref.shape[0]
            row = key if self.rows is None else self.rows[key]
            outside = isinstance(row, int) and not 0 <= row < total
            values = self.ref[row % total if outside else row, pl.ds(self.first, self.width), :]
            self.values[key] = lane_swap(values) if outside else values
        return self.values[key]


def stage(run, *args):
    pl.when(lax.axis_index("gy") >= 0)(functools.partial(run, *args))


def chem_right(conc):
    return conc * (conc * conc - (1.0 + STABILIZER))


class Rows:
    def __init__(self, total, *parts):
        self.places = {
            row: (ref, index) for ref, rows in parts for index, row in enumerate(rows)
        }
        self.shape = (total,) + parts[0][0].shape[1:]

    def place(self, at):
        row, *rest = at if isinstance(at, tuple) else (at,)
        ref, index = self.places[row]
        return ref, (index, *rest)

    def __getitem__(self, at):
        ref, index = self.place(at)
        return ref[index]

    def __setitem__(self, at, values):
        ref, index = self.place(at)
        ref[index] = values


class Level:
    def __init__(self, level_index, weights, weights_from=PAD, right_from=PAD):
        self.scale = 0.25**level_index
        self.dup = 2**level_index
        self.diagonal = STABILIZER + 6.0 * GRADIENT_ENERGY * self.scale
        self.weights = weights
        self.weights_from, self.right_from = weights_from, right_from

    def set_weights(self, mobility, count, start=0):
        width = self.weights[0].shape[1]
        half = 0.5 * self.scale * TIME_STEP
        face_x, up_y, down_y, up_z, down_z, coupling, gain = self.weights

        def at(row, shift=0):
            return mobility[row, pl.ds(self.weights_from + shift, width), :]

        def group(first, size):
            rows = RowCache(mobility, None, self.weights_from, width)
            before = half * (rows[start + first - 1] + rows[start + first])
            for i in range(size):
                r = start + first + i
                here = rows[r]
                after = half * (here + rows[r + 1])
                to_up_y = half * (here + at(r, 1))
                to_down_y = half * (here + at(r, -1))
                to_up_z = half * (here + lane_roll(here, -self.dup))
                to_down_z = half * (here + lane_roll(here, self.dup))
                total_weight = (before + after) + (to_up_y + to_down_y) + (to_up_z + to_down_z)
                face_x[r] = after
                up_y[r] = to_up_y
                down_y[r] = to_down_y
                up_z[r] = to_up_z
                down_z[r] = to_down_z
                coupling[r] = total_weight
                gain[r] = DAMPING / (1.0 + total_weight * self.diagonal)
                before = after

        loop_rows(count, count, group)

    def residuals(self, fields, right, rows, window, fields_from=0):
        conc, chem = fields
        first, width = window
        face_x, up_y, down_y, up_z, down_z, coupling, gain = self.weights

        def at(ref, row, shift=0):
            return ref[row, pl.ds(first - fields_from + shift, width), :]

        def weight(ref, row):
            return ref[row, pl.ds(first - self.weights_from, width), :]

        def right_at(row):
            values = [ref[row, pl.ds(first - self.right_from, width), :] for ref in right]
            return values if len(values) == 2 else values + [chem_right(values[0])]

        total = conc.shape[0]
        if isinstance(rows[0], int):
            centres, listed = [row % total for row in rows[1:-1]], None
        else:
            centres, listed = range(1, len(rows) - 1), rows
        u = RowCache(chem, listed, first - fields_from, width)
        c = RowCache(conc, listed, first - fields_from, width)
        across = RowCache(face_x, listed, first - self.weights_from, width)
        for key in centres:
            r = key if listed is None else listed[key]
            c_here, u_here = c[key], u[key]
            here = weight(coupling, r)
            flux = across[key] * u[key + 1] + across[key - 1] * u[key - 1]
            flux = flux + weight(up_y, r) * at(chem, r, 1) + weight(down_y, r) * at(chem, r, -1)
            flux = flux + weight(up_z, r) * lane_roll(u_here, -self.dup)
            flux = flux + weight(down_z, r) * lane_roll(u_here, self.dup)
            near = (c[key - 1] + c[key + 1]) + (at(conc, r, 1) + at(conc, r, -1))
            near = near + (lane_roll(c_here, self.dup) + lane_roll(c_here, -self.dup))
            conc_right, chem_right_here = right_at(r)
            conc_left = conc_right - c_here + (flux - here * u_here)
            chem_left = chem_right_here - u_here + self.diagonal * c_here
            chem_left = chem_left - (GRADIENT_ENERGY * self.scale) * near
            yield r, c_here, u_here, conc_left, chem_left, here, weight(gain, r)

    def steps(self, conc_left, chem_left, coupling, gain):
        return (
            gain * (conc_left - coupling * chem_left),
            gain * (chem_left + self.diagonal * conc_left),
        )

    def first_sweep(self, right, unroll, put):
        coupling, gain = self.weights[5:]

        def group(first, size):
            for i in range(size):
                r = first + i
                put(r, *self.steps(right[0][r], right[1][r], coupling[r], gain[r]))

        loop_rows(right[0].shape[0], unroll, group)

    def row_window(self, start, first, size):
        return [start + first + i - 1 for i in range(size + 2)]

    def sweep(self, fields, right, start, count, unroll, window, put):
        def group(first, size):
            rows = self.row_window(start, first, size)
            for r, c, u, *left in self.residuals(fields, right, rows, window):
                conc_step, chem_step = self.steps(*left)
                put(r, c + conc_step, u + chem_step)

        loop_rows(count, unroll, group)

    def coarse_right(self, fields, right, start, count, unroll, window, put, fields_from=0):
        def group(first, size):
            rows = self.row_window(start, first, size)
            items = self.residuals(fields, right, rows, window, fields_from)
            half = first // 2 if isinstance(first, int) else lax.shift_right_logical(first, 1)
            kept = None
            for i, (_, _, _, conc_left, chem_left, _, _) in enumerate(items):
                if i % 2 == 0:
                    kept = conc_left, chem_left
                else:
                    put(half + i // 2, kept[0] + conc_left, kept[1] + chem_left)

        loop_rows(count, unroll, group)


def put_padded(refs):
    def put(row, *values):
        for ref, value in zip(refs, values):
            width = value.shape[0]
            ref[row, PAD : PAD + width, :] = value
            ref[row, :PAD, :] = value[width - PAD :]
            ref[row, PAD + width :, :] = value[:PAD]

    return put


def put_window(refs, window):
    def put(row, *values):
        for ref, value in zip(refs, values):
            ref[row, window[0] : window[0] + window[1], :] = value

    return put


def put_sums(sums, offset=0):
    def put(row, *values):
        for field, value in enumerate(values):
            sums[field, offset + row] = value

    return put


def pair_rows(ref, row, count):
    return ref[row, pl.ds(0, count, stride=2), :] + ref[row, pl.ds(1, count, stride=2), :]


def spread_rows(ref, row, values):
    count = values.shape[0]
    ref[row, pl.ds(0, count, stride=2), :] = values
    ref[row, pl.ds(1, count, stride=2), :] = values


def pair_lanes(values, dup):
    other = jnp.where(
        lane_even(values.shape, dup), lane_roll(values, -dup), lane_roll(values, dup)
    )
    return values + other


def side_tiles(conc, chem, to_left, to_right, at, low):
    columns = conc.shape[0]
    to_left[at] = jnp.where(low, conc[:PAD], half_turn(chem[:PAD]))
    to_right[at] = jnp.where(low, half_turn(chem[columns - PAD :]), conc[columns - PAD :])


def low_half(lanes):
    return lax.broadcasted_iota(jnp.int32, (PAD, lanes), 0) < HALO


def edges_kernel(fields, low_rows, high_rows, to_left, to_right):
    rows, columns, lanes = fields.shape[1:]
    low_rows[...] = fields[:, :HALO]
    high_rows[...] = fields[:, rows - HALO :]
    for row in range(rows):
        side_tiles(fields[0, row], fields[1, row], to_left, to_right, row, low_half(lanes))


def corners_kernel(before, after, to_left, to_right):
    lanes = before.shape[-1]
    for at in range(2 * HALO):
        source, row = (before, at) if at < HALO else (after, at - HALO)
        side_tiles(source[0, row], source[1, row], to_left, to_right, at, low_half(lanes))


def frame_row(row, rows, own, before, after):
    if row < HALO:
        return before[row]
    if row < HALO + rows:
        return own[row - HALO]
    return after[row - HALO - rows]


def half_turn(values):
    return pltpu.roll(values, HALO, axis=0)


class FrameRows:
    def __init__(self, rows):
        self.total = rows + 2 * HALO
        end = self.total
        self.own = range(HALO, end - HALO)
        self.weights_early = range(HALO + 1, end - HALO - 1)
        self.swept_early = range(HALO + 2, end - HALO - 2)
        self.joined = [HALO + 1, HALO + 2, end - HALO - 3, end - HALO - 2]
        self.weights_late = [*range(2, HALO + 1), *range(end - HALO - 1, end - 3)]
        self.weights_outer = [0, 1, end - 3, end - 2, end - 1]
        self.right_late = [HALO - 1, end - HALO]
        self.right_outer = [*range(HALO - 1), *range(end - HALO + 1, end)]
        self.swept_late = [*range(2, HALO + 2), *range(end - HALO - 2, end - 2)]
        self.mid_late = [*range(1, HALO + 1), *range(end - HALO - 1, end - 1)]

    def weights(self, early, late):
        return [
            Rows(self.total, (early.at[i], self.weights_early), (late.at[i], self.weights_late))
            for i in range(7)
        ]

    def swept(self, early, late):
        return [
            Rows(self.total, (early.at[i], self.swept_early), (late.at[i], self.swept_late))
            for i in range(2)
        ]


def fine_level(weights):
    return Level(0, weights, HALO, 0)


def set_row(conc, chem, left, right, row, conc_at, chem_at, mobility):
    c = jnp.concatenate([left, conc, right])
    if conc_at is not None:
        conc_at[row] = c
    chem_at[row] = jnp.concatenate([half_turn(left), chem, half_turn(right)])
    gap = 1.0 - c * c
    mobility[row] = 0.1 + gap * gap


def pack(sums, field, index, out):
    count = sums.shape[2] // 2
    even = lane_even((count, sums.shape[3]), 1)
    a = pair_rows(sums.at[field], 2 * index, count)
    b = pair_rows(sums.at[field], 2 * index + 1, count)
    out[field, index] = 0.125 * jnp.where(even, a + lane_roll(a, -1), b + lane_roll(b, 1))


def early_kernel(
    fields, own_left, own_right,
    packed, kept, right_conc, all_weights, joined,
    chem_start, mobility, mid, outer, sums,
):
    rows, columns = fields.shape[1:3]
    at = FrameRows(rows)
    right_side = (Rows(at.total, (right_conc, at.own)),)
    for row in at.own:
        i = row - HALO
        set_row(
            fields[0, i], fields[1, i], own_left[i], own_right[i],
            row, right_side[0], chem_start, mobility,
        )
    weights = [
        Rows(at.total, (all_weights.at[i], at.weights_early), (outer.at[i], [HALO]))
        for i in range(7)
    ]
    level = fine_level(weights)
    level.set_weights(mobility, rows - 1, HALO)
    wide = (PAD - HALO, columns + 2 * HALO)
    middle = [r for r in at.weights_early if r not in at.joined]
    mids = [
        Rows(at.total, (mid.at[i], middle), (joined.at[i], at.joined)) for i in range(2)
    ]
    swept = [Rows(at.total, (kept.at[i], at.swept_early)) for i in range(2)]
    level.sweep(
        (right_side[0], chem_start), right_side, HALO + 1, rows - 2, rows - 2, wide,
        put_window(mids, wide),
    )
    level.sweep(
        mids, right_side, HALO + 2, rows - 4, rows - 4, wide, put_window(swept, (0, wide[1]))
    )
    level.coarse_right(
        swept, right_side, 2 * HALO, rows - 2 * HALO, rows - 2 * HALO, (PAD, columns),
        put_sums(sums, HALO // 2), wide[0],
    )
    own = slice(PAD, PAD + columns)
    for index in range(rows // 2):
        row = HALO + 2 * index
        sums[2, index] = mobility[row, own, :] + mobility[row + 1, own, :]
    for index in range(rows // 4):
        pack(sums, 2, index, packed)
        if HALO // 4 <= index < (rows - HALO) // 4:
            pack(sums, 0, index, packed)
            pack(sums, 1, index, packed)
        else:
            packed[0, index] = jnp.zeros(packed.shape[2:], jnp.float32)
            packed[1, index] = jnp.zeros(packed.shape[2:], jnp.float32)


def late_kernel(
    fields, before, after, own_left, own_right, corner_left, corner_right,
    packed_early, kept_early, right_early, weights_early, joined,
    packed, kept, right_conc, all_weights,
    chem_start, mobility, mid, outer, right_outer, sums,
):
    rows, columns = fields.shape[1:3]
    at = FrameRows(rows)
    end = at.total
    right = Rows(
        end, (right_early, at.own), (right_conc, at.right_late), (right_outer, at.right_outer)
    )
    for row in [*range(HALO + 2), *range(end - HALO - 2, end)]:
        if row in at.own:
            i = row - HALO
            values = fields[0, i], fields[1, i], own_left[i], own_right[i]
            set_row(*values, row, None, chem_start, mobility)
        else:
            source, i = (before, row) if row < HALO else (after, row - rows - HALO)
            corner = row if row < HALO else row - rows
            values = source[0, i], source[1, i], corner_left[corner], corner_right[corner]
            set_row(*values, row, right, chem_start, mobility)
    weights = at.weights(weights_early, all_weights)
    for i, one in enumerate(weights):
        for index, row in enumerate(at.weights_outer):
            one.places[row] = outer.at[i], index
    level = fine_level(weights)
    level.set_weights(mobility, HALO + 1, 0)
    level.set_weights(mobility, HALO + 1, end - HALO - 1)
    wide = (PAD - HALO, columns + 2 * HALO)
    mids = [Rows(end, (joined.at[i], at.joined), (mid.at[i], at.mid_late)) for i in range(2)]
    swept = at.swept(kept_early, kept)
    for start in (1, end - HALO - 1):
        level.sweep(
            (right, chem_start), (right,), start, HALO, HALO, wide, put_window(mids, wide)
        )
    for start in (2, end - HALO - 2):
        level.sweep(mids, (right,), start, HALO, HALO, wide, put_window(swept, (0, wide[1])))
    for start in (HALO, end - 2 * HALO):
        level.coarse_right(
            swept, (right,), start, HALO, HALO, (PAD, columns),
            put_sums(sums, (start - HALO) // 2), wide[0],
        )
    packed[...] = packed_early[...]
    for index in range(rows // 4):
        if not HALO // 4 <= index < (rows - HALO) // 4:
            pack(sums, 0, index, packed)
            pack(sums, 1, index, packed)


def coarse_kernel(
    slots, grid, first, second, first_far, second_far,
    kept_early, right_early, weights_early, kept_late, right_late, weights_late,
    conc_new, chem_new, *scratch,
):
    at = FrameRows(conc_new.shape[0])
    conc_in, chem_in = at.swept(kept_early, kept_late)
    weights = at.weights(weights_early, weights_late)
    right_conc = Rows(at.total, (right_early, at.own), (right_late, at.right_late))
    scratch = list(scratch)
    start_even, at_y = lax.axis_index("gx") % 2 == 0, lax.axis_index("gy")
    levels = []
    for level_index in (1, 2, 3):
        level = Level(level_index, scratch[5:14][2:])
        mobility, a, b, right = scratch[0], scratch[1:3], scratch[3:5], scratch[5:7]
        levels.append((level, mobility, right, a, b))
        del scratch[:14]
    sums1, sums2, spread2, spread3, spread_fine, fine_a0, fine_a1, fine_b0, fine_b1 = scratch
    one, mob1, right1, a1, b1 = levels[0]
    two, mob2, right2, a2, b2 = levels[1]
    three, mob3, right3, a3, b3 = levels[2]
    rows1, columns1, lanes = right1[0].shape
    rows2, columns2 = right2[0].shape[:2]
    rows3, columns3 = right3[0].shape[:2]
    window1, window2, window3 = (PAD, columns1), (PAD, columns2), (PAD, columns3)
    own_rows, own_columns = 2 * rows1 // grid[0], columns1 // grid[1]
    even = lane_even((own_columns, lanes), 1)
    blocks = {}
    for last, sources in enumerate(((first, second), (first_far, second_far))):
        for source, masks in zip(sources, slots):
            for slot, (mask_x, mask_y) in enumerate(masks):
                blocks[mask_x, mask_y ^ last] = source.at[slot]

    for mask_y in range(grid[1]):
        offset = (at_y ^ mask_y) * own_columns
        plain = pl.ds(pl.multiple_of(offset, PAD), own_columns)
        padded = pl.ds(pl.multiple_of(offset + PAD, PAD), own_columns)
        for field, (ref, at) in enumerate(
            ((right1[0], plain), (right1[1], plain), (mob1, padded))
        ):
            for index in range(own_rows // 2):
                own, two_on, one_on, one_back = (
                    blocks[mask_x, mask_y][field, index] for mask_x in (0, 2, 1, 3)
                )
                swap = one_on, one_back
                one_on = jnp.where(start_even, swap[0], swap[1])
                one_back = jnp.where(start_even, swap[1], swap[0])
                for row, a, b in ((0, own, two_on), (own_rows, one_on, one_back)):
                    row = row + 2 * index
                    ref[row, at, :] = jnp.where(even, a, lane_roll(b, 1))
                    ref[row + 1, at, :] = jnp.where(even, lane_roll(a, -1), b)
    for row in range(rows1):
        mob1[row, :PAD, :] = mob1[row, columns1 : columns1 + PAD, :]
        mob1[row, PAD + columns1 :, :] = mob1[row, PAD : 2 * PAD, :]

    def coarsen(mobility, sums, out, out_mobility, dup):
        count, columns = out[0].shape[:2]
        fine = pl.ds(PAD, 2 * columns)
        for index in range(count):
            sums[2, index] = mobility[2 * index, fine, :] + mobility[2 * index + 1, fine, :]
        for index in range(count):
            for field in range(2):
                half = pair_rows(sums.at[field], index, columns)
                out[field][index] = 0.125 * pair_lanes(half, dup)
            half = pair_rows(sums.at[2], index, columns)
            put_padded((out_mobility,))(index, 0.125 * pair_lanes(half, dup))

    stage(one.set_weights, mob1, rows1)
    stage(one.first_sweep, right1, rows1, put_padded(a1))
    stage(one.sweep, a1, right1, 0, rows1, rows1, window1, put_padded(b1))
    stage(one.coarse_right, b1, right1, 0, rows1, rows1, window1, put_sums(sums1))
    stage(coarsen, mob1, sums1, right2, mob2, 2)

    stage(two.set_weights, mob2, rows2)
    stage(two.first_sweep, right2, rows2, put_padded(a2))
    stage(two.sweep, a2, right2, 0, rows2, rows2, window2, put_padded(b2))
    stage(two.coarse_right, b2, right2, 0, rows2, rows2, window2, put_sums(sums2))
    stage(coarsen, mob2, sums2, right3, mob3, 4)

    stage(three.set_weights, mob3, rows3)
    stage(three.first_sweep, right3, rows3, put_padded(a3))
    now, other = a3, b3
    for sweep_index in range(COARSE - 1):
        stage(three.sweep, now, right3, 0, rows3, rows3, window3, put_padded(other))
        now, other = other, now

    def correct(coarse, coarse_row, fine_in, fine_out, spread, index):
        for field in range(2):
            columns = fine_in[field].shape[1] - 2 * PAD
            spread_rows(
                spread.at[field], index, coarse[field][coarse_row, pl.ds(PAD, columns // 2), :]
            )
            both = spread[field, index]
            for row in (2 * coarse_row, 2 * coarse_row + 1):
                put_padded((fine_out[field],))(
                    row, fine_in[field][row, pl.ds(PAD, columns), :] + both
                )

    for row in range(rows3):
        correct(now, row, b2, a2, spread3, row)
    stage(two.sweep, a2, right2, 0, rows2, rows2, window2, put_padded(b2))
    stage(two.sweep, b2, right2, 0, rows2, rows2, window2, put_padded(a2))
    for row in range(rows2):
        correct(a2, row, b1, a1, spread2, row)
    stage(one.sweep, a1, right1, -2, own_rows + 4, own_rows + 4, window1, put_padded(b1))
    stage(one.sweep, b1, right1, -1, own_rows + 2, own_rows + 2, window1, put_padded(a1))

    rows, columns = conc_new.shape[:2]
    wide = (PAD - HALO, columns + 2 * HALO)
    near_own = pl.ds(pl.multiple_of(at_y * own_columns, PAD), own_columns + 2 * PAD)
    for index in range(own_rows + 2):
        inside = 1 <= index <= rows1
        row = index - 1 if inside else (index - 1) % rows1
        for field, (source, target) in enumerate(((conc_in, fine_a0), (chem_in, fine_a1))):
            tile = a1[field][row, near_own, :]
            on_even = lane_even(tile.shape, 1)
            if inside:
                tile = jnp.where(on_even, tile, lane_roll(tile, 1))
            else:
                tile = jnp.where(on_even, lane_roll(tile, -1), tile)
            spread_rows(spread_fine.at[field], index, tile)
            both = spread_fine[field, index, pl.ds(wide[0] + PAD, wide[1]), :]
            for fine in (HALO - 2 + 2 * index, HALO - 1 + 2 * index):
                put_window((target,), wide)(fine, source[fine] + both)
    fine = fine_level(weights)
    right_side = (right_conc,)
    fine.sweep(
        (fine_a0, fine_a1), right_side, HALO - 1, rows + 2, rows + 2, wide,
        put_window((fine_b0, fine_b1), wide),
    )

    def put_new(row, conc_value, chem_value):
        conc_new[row - HALO] = conc_value
        chem_new[row - HALO] = chem_value

    fine.sweep((fine_b0, fine_b1), right_side, HALO, rows, rows, (PAD, columns), put_new)


def call_kernel(kernel, outs, scratch, *args, vmem_mib=8):
    shapes = tuple(jax.ShapeDtypeStruct(shape, jnp.float32) for shape in outs)
    return pl.pallas_call(
        kernel,
        out_shape=shapes,
        in_specs=[whole_block()] * len(args),
        out_specs=tuple(whole_block() for _ in outs),
        scratch_shapes=[pltpu.VMEM(shape, jnp.float32) for shape in scratch],
        compiler_params=pltpu.CompilerParams(vmem_limit_bytes=vmem_mib * 1024 * 1024),
    )(*args)


def shifted(values, axis, by):
    count = lax.axis_size(axis)
    return lax.ppermute(values, axis, [(i, (i + by) % count) for i in range(count)])


def swapped(values, axis, mask):
    count = lax.axis_size(axis)
    return lax.ppermute(values, axis, [(i, i ^ mask) for i in range(count)])


def far_masks():
    count_x, count_y = lax.axis_size("gx"), lax.axis_size("gy")
    return list(range(1, count_x)), list(range(2, count_y, 2))


def slot_masks():
    along_x, along_y = far_masks()
    first = [(0, 0)] + [(0, y) for y in along_y] + [(x, 0) for x in along_x]
    second = [(x, y) for y in along_y for x in along_x[1:]]
    return first, second + [(along_x[0], y) for y in along_y]


def swapped_both(values, mask_x, mask_y):
    count_x, count_y = lax.axis_size("gx"), lax.axis_size("gy")
    pairs = [
        (x * count_y + y, (x ^ mask_x) * count_y + (y ^ mask_y))
        for x in range(count_x)
        for y in range(count_y)
    ]
    return lax.ppermute(values, ("gx", "gy"), pairs)


def gathered(values):
    along_x, along_y = far_masks()
    across = [swapped(values, "gx", mask) for mask in along_x]
    beside = [swapped(values, "gy", mask) for mask in along_y]
    later, _ = lax.optimization_barrier((values, across[2]))
    corner = [swapped_both(later, along_x[0], mask) for mask in along_y]
    last = jnp.stack(across[1:])
    first = jnp.stack([values] + beside + across)
    second = [swapped(last, "gy", mask) for mask in along_y]
    second = jnp.concatenate(second + [jnp.stack(corner)], axis=0)
    return first, second, swapped(first, "gy", 1), swapped(second, "gy", 1)


def two_phase_solve(conc, chem):
    rows, columns, lanes = conc.shape
    frame = (rows + 2 * HALO, columns + 2 * PAD, lanes)
    edge = (2, HALO, columns, lanes)
    block = (rows, columns, lanes)
    fields = jnp.concatenate([conc, chem], axis=0).reshape((2,) + block)
    side, corner = (rows, PAD, lanes), (2 * HALO, PAD, lanes)
    low, high, to_left, to_right = call_kernel(
        edges_kernel, (edge, edge, side, side), (), fields
    )
    before, after = shifted(high, "gx", 1), shifted(low, "gx", -1)
    sides = [shifted(to_right, "gy", 1), shifted(to_left, "gy", -1)]
    to_left, to_right = call_kernel(corners_kernel, (corner, corner), (), before, after)
    sides += [shifted(to_right, "gy", 1), shifted(to_left, "gy", -1)]
    at, width = FrameRows(rows), columns + 2 * HALO
    packed_shape, sums = (3, rows // 4, columns // 2, lanes), (3, rows // 2, columns, lanes)

    def part(count, listed, wide):
        return (count, len(listed), wide, lanes)

    right_shapes = [part(0, listed, frame[1])[1:] for listed in (at.own, at.right_late, at.right_outer)]
    early, *kept = call_kernel(
        early_kernel,
        (
            packed_shape, part(2, at.swept_early, width), right_shapes[0],
            part(7, at.weights_early, width), part(2, at.joined, frame[1]),
        ),
        (frame, frame, part(2, at.weights_early, frame[1]), part(7, [0], width), sums),
        fields, *sides[:2],
    )
    packed, *kept_late = call_kernel(
        late_kernel,
        (
            packed_shape, part(2, at.swept_late, width), right_shapes[1],
            part(7, at.weights_late, width),
        ),
        (
            frame, frame, part(2, at.mid_late, frame[1]), part(7, at.weights_outer, width),
            right_shapes[2], sums,
        ),
        fields, before, after, *sides, early, *kept,
    )
    count_x, count_y = lax.axis_size("gx"), lax.axis_size("gy")
    grids = [(count_x * rows >> level + 1, count_y * columns >> level) for level in range(4)]
    scratch = []
    for level_rows, level_columns in grids[1:]:
        scratch += [(level_rows, level_columns + 2 * PAD, lanes)] * 5
        scratch += [(level_rows, level_columns, lanes)] * 9
    scratch += [(3, grids[2][0], grids[1][1], lanes), (3, grids[3][0], grids[2][1], lanes)]
    scratch += [(2, grids[2][0], grids[1][1], lanes), (2, grids[3][0], grids[2][1], lanes)]
    scratch += [(2, rows // 2 + 2, columns + 4 * PAD, lanes)] + [frame] * 4
    kernel = functools.partial(coarse_kernel, slot_masks(), (count_x, count_y))
    args = (*gathered(packed), *kept[:3], *kept_late)
    return call_kernel(kernel, (block, block), scratch, *args, vmem_mib=24)


def body(conc_old, chem_old):
    rows, columns, lanes = conc_old.shape
    count_x, count_y = lax.axis_size("gx"), lax.axis_size("gy")
    grid_bytes = count_x * rows * count_y * columns * lanes
    if (
        grid_bytes <= GRID_BYTES_MAX
        and rows % 16 == 0
        and lanes % 128 == 0
        and count_x * rows >= 64
        and count_y * columns >= 64
        and count_x == 4
        and count_y >= 4
        and count_y & (count_y - 1) == 0
        and columns == 16
    ):
        return two_phase_solve(conc_old, chem_old)
    start_fields = jnp.stack([conc_old, chem_old])
    result = plain_solve(start_fields)
    return (result[0], result[1])


def solution(mesh):
    in_specs = (P(("img", "gx"), "gy", None), P(("img", "gx"), "gy", None))
    out_specs = (P(("img", "gx"), "gy", None), P(("img", "gx"), "gy", None))
    return jax.shard_map(body, mesh=mesh, in_specs=in_specs, out_specs=out_specs, check_vma=False)
```

```python
import functools

import jax
import jax.numpy as jnp
from jax import lax
from jax.experimental import pallas as pl
from jax.experimental.pallas import tpu as pltpu
from jax.sharding import PartitionSpec as P

LEVELS = 4
SWEEPS = 2
COARSE = 6


TIME_STEP = 32.0
GRADIENT_ENERGY = 0.5
STABILIZER = 2.0
DAMPING = 0.7


def extended(cells, sides, width):
    for axis, dim in sides:
        count = lax.axis_size(axis)
        head = lax.slice_in_dim(cells, 0, width, axis=dim)
        tail = lax.slice_in_dim(cells, cells.shape[dim] - width, cells.shape[dim], axis=dim)
        cells = jnp.concatenate(
            [
                lax.ppermute(tail, axis, [(i, (i + 1) % count) for i in range(count)]),
                cells,
                lax.ppermute(head, axis, [((i + 1) % count, i) for i in range(count)]),
            ],
            axis=dim,
        )
    return cells


def mobility_of(concentration):
    return 0.1 + jnp.square(1.0 - concentration * concentration)


def right_of(concentration):
    return jnp.stack(
        [
            concentration,
            concentration * concentration * concentration - (1.0 + STABILIZER) * concentration,
        ]
    )


def face_weights(mob_padded, level_scale):
    middle = mob_padded[1:-1, 1:-1, :]
    half_scale = 0.5 * level_scale
    weights = (
        half_scale * (middle + mob_padded[2:, 1:-1, :]),
        half_scale * (middle + mob_padded[:-2, 1:-1, :]),
        half_scale * (middle + mob_padded[1:-1, 2:, :]),
        half_scale * (middle + mob_padded[1:-1, :-2, :]),
        half_scale * (middle + jnp.roll(middle, -1, axis=2)),
        half_scale * (middle + jnp.roll(middle, 1, axis=2)),
    )
    total_weight = weights[0] + weights[1] + weights[2] + weights[3] + weights[4] + weights[5]
    return (weights, total_weight)


def neighbour_list(padded, middle):
    return (
        padded[2:, 1:-1, :],
        padded[:-2, 1:-1, :],
        padded[1:-1, 2:, :],
        padded[1:-1, :-2, :],
        jnp.roll(middle, -1, axis=2),
        jnp.roll(middle, 1, axis=2),
    )


def apply_operator(padded, weights, level_scale):
    middle = padded[:, 1:-1, 1:-1, :]
    conc_near = neighbour_list(padded[0], middle[0])
    chem_near = neighbour_list(padded[1], middle[1])
    flux = weights[0] * (chem_near[0] - middle[1])
    for position in range(1, 6):
        flux = flux + weights[position] * (chem_near[position] - middle[1])
    laplace = (
        conc_near[0]
        + conc_near[1]
        + conc_near[2]
        + conc_near[3]
        + conc_near[4]
        + conc_near[5]
        - 6.0 * middle[0]
    )
    first_eq = middle[0] - TIME_STEP * flux
    second_eq = middle[1] - STABILIZER * middle[0] + GRADIENT_ENERGY * level_scale * laplace
    return jnp.stack([first_eq, second_eq])


def update(residual, total_weight, level_scale):
    diagonal = STABILIZER + 6.0 * GRADIENT_ENERGY * level_scale
    coupling = TIME_STEP * total_weight
    determinant = 1.0 + coupling * diagonal
    conc_step = (residual[0] - coupling * residual[1]) / determinant
    chem_step = (residual[1] + diagonal * residual[0]) / determinant
    return DAMPING * jnp.stack([conc_step, chem_step])


def sweep_once(padded, right_side, mob_padded, level_scale):
    weights, total_weight = face_weights(mob_padded, level_scale)
    residual = right_side - apply_operator(padded, weights, level_scale)
    return padded[:, 1:-1, 1:-1, :] + update(residual, total_weight, level_scale)


def defect(padded, right_side, mob_padded, level_scale):
    weights = face_weights(mob_padded, level_scale)[0]
    return right_side - apply_operator(padded, weights, level_scale)


def coarsen(values):
    dims_now = values.shape
    grouped = values.reshape(
        dims_now[:-3] + (dims_now[-3] // 2, 2, dims_now[-2] // 2, 2, dims_now[-1] // 2, 2)
    )
    return jnp.sum(grouped, axis=(-5, -3, -1)) * 0.125


def refine(values):
    for axis_pos in (-3, -2, -1):
        values = jnp.repeat(values, 2, axis=axis_pos)
    return values


def trim_rim(values, width):
    return values[..., width:-width, width:-width, :]


def field_rim(fields):
    return extended(fields, (("gx", 1), ("gy", 2)), 1)


def coarsest_solve(right_side, mobility, level_scale):
    mob_padded = extended(mobility, (("gx", 0), ("gy", 1)), 1)
    fields = update(right_side, face_weights(mob_padded, level_scale)[1], level_scale)
    for sweep_index in range(COARSE - 1):
        padded = extended(fields, (("gx", 1), ("gy", 2)), 1)
        fields = sweep_once(padded, right_side, mob_padded, level_scale)
    return fields


def plain_solve(start_fields):
    outer_fields = field_rim(start_fields)
    mob_outer = mobility_of(outer_fields[0])
    mobility = trim_rim(mob_outer, 1)
    level_data = []
    for level_index in range(LEVELS - 1):
        if level_index == 0:
            mob_padded = mob_outer
        else:
            mob_padded = extended(mobility, (("gx", 0), ("gy", 1)), 1)
        level_data.append((mob_padded, 0.25**level_index))
        mobility = coarsen(mobility)
    coarsest_scale = 0.25 ** (LEVELS - 1)

    def cycle_level(level_index, right_side):
        if level_index == LEVELS - 1:
            return coarsest_solve(right_side, mobility, coarsest_scale)
        mob_padded, level_scale = level_data[level_index]
        if level_index == 0:
            fields = sweep_once(outer_fields, right_side, mob_padded, level_scale)
        else:
            fields = update(right_side, face_weights(mob_padded, level_scale)[1], level_scale)
        fields = sweep_once(field_rim(fields), right_side, mob_padded, level_scale)
        residual = defect(field_rim(fields), right_side, mob_padded, level_scale)
        fields = fields + refine(cycle_level(level_index + 1, coarsen(residual)))
        for sweep_index in range(SWEEPS):
            fields = sweep_once(field_rim(fields), right_side, mob_padded, level_scale)
        return fields

    return cycle_level(0, right_of(start_fields[0]))


HALO = 4
PAD = 8
GRID_BYTES_MAX = 2 * 1024 * 1024


def whole_block():
    return pl.BlockSpec(memory_space=pltpu.VMEM)


def lane_roll(values, shift):
    return pltpu.roll(values, shift % values.shape[1], axis=1)


def lane_even(shape, dup):
    return (lax.broadcasted_iota(jnp.int32, shape, 1) // dup) % 2 == 0


def loop_rows(count, unroll, row_group):
    steps, rest = divmod(count, unroll)
    if steps == 1:
        row_group(0, unroll)
    elif steps > 1:

        def step(index, carry):
            row_group(index * unroll, unroll)
            return carry

        lax.fori_loop(0, steps, step, 0)
    if rest:
        row_group(steps * unroll, rest)


def lane_swap(values):
    return jnp.where(lane_even(values.shape, 1), lane_roll(values, -1), lane_roll(values, 1))


class RowCache:
    def __init__(self, ref, rows, first, width):
        self.ref, self.rows, self.first, self.width = ref, rows, first, width
        self.values = {}

    def __getitem__(self, key):
        if key not in self.values:
            total = self.ref.shape[0]
            row = key if self.rows is None else self.rows[key]
            outside = isinstance(row, int) and not 0 <= row < total
            values = self.ref[row % total if outside else row, pl.ds(self.first, self.width), :]
            self.values[key] = lane_swap(values) if outside else values
        return self.values[key]


def stage(run, *args):
    pl.when(lax.axis_index("gy") >= 0)(functools.partial(run, *args))


def chem_right(conc):
    return conc * (conc * conc - (1.0 + STABILIZER))


class Rows:
    def __init__(self, total, *parts):
        self.places = {
            row: (ref, index) for ref, rows in parts for index, row in enumerate(rows)
        }
        self.shape = (total,) + parts[0][0].shape[1:]

    def place(self, at):
        row, *rest = at if isinstance(at, tuple) else (at,)
        ref, index = self.places[row]
        return ref, (index, *rest)

    def __getitem__(self, at):
        ref, index = self.place(at)
        return ref[index]

    def __setitem__(self, at, values):
        ref, index = self.place(at)
        ref[index] = values


class Level:
    def __init__(self, level_index, weights, weights_from=PAD, right_from=PAD):
        self.scale = 0.25**level_index
        self.dup = 2**level_index
        self.diagonal = STABILIZER + 6.0 * GRADIENT_ENERGY * self.scale
        self.weights = weights
        self.weights_from, self.right_from = weights_from, right_from

    def set_weights(self, mobility, count, start=0):
        width = self.weights[0].shape[1]
        half = 0.5 * self.scale * TIME_STEP
        face_x, up_y, down_y, up_z, down_z, coupling, gain = self.weights

        def at(row, shift=0):
            return mobility[row, pl.ds(self.weights_from + shift, width), :]

        def group(first, size):
            rows = RowCache(mobility, None, self.weights_from, width)
            before = half * (rows[start + first - 1] + rows[start + first])
            for i in range(size):
                r = start + first + i
                here = rows[r]
                after = half * (here + rows[r + 1])
                to_up_y = half * (here + at(r, 1))
                to_down_y = half * (here + at(r, -1))
                to_up_z = half * (here + lane_roll(here, -self.dup))
                to_down_z = half * (here + lane_roll(here, self.dup))
                total_weight = (before + after) + (to_up_y + to_down_y) + (to_up_z + to_down_z)
                face_x[r] = after
                up_y[r] = to_up_y
                down_y[r] = to_down_y
                up_z[r] = to_up_z
                down_z[r] = to_down_z
                coupling[r] = total_weight
                gain[r] = DAMPING / (1.0 + total_weight * self.diagonal)
                before = after

        loop_rows(count, count, group)

    def residuals(self, fields, right, rows, window, fields_from=0):
        conc, chem = fields
        first, width = window
        face_x, up_y, down_y, up_z, down_z, coupling, gain = self.weights

        def at(ref, row, shift=0):
            return ref[row, pl.ds(first - fields_from + shift, width), :]

        def weight(ref, row):
            return ref[row, pl.ds(first - self.weights_from, width), :]

        def right_at(row):
            values = [ref[row, pl.ds(first - self.right_from, width), :] for ref in right]
            return values if len(values) == 2 else values + [chem_right(values[0])]

        total = conc.shape[0]
        if isinstance(rows[0], int):
            centres, listed = [row % total for row in rows[1:-1]], None
        else:
            centres, listed = range(1, len(rows) - 1), rows
        u = RowCache(chem, listed, first - fields_from, width)
        c = RowCache(conc, listed, first - fields_from, width)
        across = RowCache(face_x, listed, first - self.weights_from, width)
        for key in centres:
            r = key if listed is None else listed[key]
            c_here, u_here = c[key], u[key]
            here = weight(coupling, r)
            conc_right, chem_right_here = right_at(r)
            flux = across[key] * u[key + 1] + across[key - 1] * u[key - 1]
            flux = flux + (weight(up_y, r) * at(chem, r, 1) + weight(down_y, r) * at(chem, r, -1))
            flux = flux + (conc_right - c_here - here * u_here)
            flux_z = weight(up_z, r) * lane_roll(u_here, -self.dup)
            flux_z = flux_z + weight(down_z, r) * lane_roll(u_here, self.dup)
            conc_left = flux + flux_z
            near = (c[key - 1] + c[key + 1]) + (at(conc, r, 1) + at(conc, r, -1))
            pull = GRADIENT_ENERGY * self.scale
            chem_left = (chem_right_here - u_here + self.diagonal * c_here) - pull * near
            near_z = lane_roll(c_here, self.dup) + lane_roll(c_here, -self.dup)
            chem_left = chem_left - pull * near_z
            yield r, c_here, u_here, conc_left, chem_left, here, weight(gain, r)

    def steps(self, conc_left, chem_left, coupling, gain):
        return (
            gain * (conc_left - coupling * chem_left),
            gain * (chem_left + self.diagonal * conc_left),
        )

    def first_sweep(self, right, unroll, put):
        coupling, gain = self.weights[5:]

        def group(first, size):
            for i in range(size):
                r = first + i
                put(r, *self.steps(right[0][r], right[1][r], coupling[r], gain[r]))

        loop_rows(right[0].shape[0], unroll, group)

    def row_window(self, start, first, size):
        return [start + first + i - 1 for i in range(size + 2)]

    def sweep(self, fields, right, start, count, unroll, window, put):
        def group(first, size):
            rows = self.row_window(start, first, size)
            for r, c, u, *left in self.residuals(fields, right, rows, window):
                conc_step, chem_step = self.steps(*left)
                put(r, c + conc_step, u + chem_step)

        loop_rows(count, unroll, group)

    def coarse_right(self, fields, right, start, count, unroll, window, put, fields_from=0):
        def group(first, size):
            rows = self.row_window(start, first, size)
            items = self.residuals(fields, right, rows, window, fields_from)
            half = first // 2 if isinstance(first, int) else lax.shift_right_logical(first, 1)
            kept = None
            for i, (_, _, _, conc_left, chem_left, _, _) in enumerate(items):
                if i % 2 == 0:
                    kept = conc_left, chem_left
                else:
                    put(half + i // 2, kept[0] + conc_left, kept[1] + chem_left)

        loop_rows(count, unroll, group)


def put_padded(refs):
    def put(row, *values):
        for ref, value in zip(refs, values):
            width = value.shape[0]
            ref[row, PAD : PAD + width, :] = value
            ref[row, :PAD, :] = value[width - PAD :]
            ref[row, PAD + width :, :] = value[:PAD]

    return put


def put_window(refs, window):
    def put(row, *values):
        for ref, value in zip(refs, values):
            ref[row, window[0] : window[0] + window[1], :] = value

    return put


def put_sums(sums, offset=0):
    def put(row, *values):
        for field, value in enumerate(values):
            sums[field, offset + row] = value

    return put


def pair_rows(ref, row, count):
    return ref[row, pl.ds(0, count, stride=2), :] + ref[row, pl.ds(1, count, stride=2), :]


def spread_rows(ref, row, values):
    count = values.shape[0]
    ref[row, pl.ds(0, count, stride=2), :] = values
    ref[row, pl.ds(1, count, stride=2), :] = values


def pair_lanes(values, dup):
    other = jnp.where(
        lane_even(values.shape, dup), lane_roll(values, -dup), lane_roll(values, dup)
    )
    return values + other


def side_tiles(conc, chem, to_left, to_right, at, low):
    columns = conc.shape[0]
    to_left[at] = jnp.where(low, conc[:PAD], half_turn(chem[:PAD]))
    to_right[at] = jnp.where(low, half_turn(chem[columns - PAD :]), conc[columns - PAD :])


def low_half(lanes):
    return lax.broadcasted_iota(jnp.int32, (PAD, lanes), 0) < HALO


def edges_kernel(fields, low_rows, high_rows, to_left, to_right):
    rows, columns, lanes = fields.shape[1:]
    low_rows[...] = fields[:, :HALO]
    high_rows[...] = fields[:, rows - HALO :]
    for row in range(rows):
        side_tiles(fields[0, row], fields[1, row], to_left, to_right, row, low_half(lanes))


def corners_kernel(before, after, to_left, to_right):
    lanes = before.shape[-1]
    for at in range(2 * HALO):
        source, row = (before, at) if at < HALO else (after, at - HALO)
        side_tiles(source[0, row], source[1, row], to_left, to_right, at, low_half(lanes))


def frame_row(row, rows, own, before, after):
    if row < HALO:
        return before[row]
    if row < HALO + rows:
        return own[row - HALO]
    return after[row - HALO - rows]


def half_turn(values):
    return pltpu.roll(values, HALO, axis=0)


class FrameRows:
    def __init__(self, rows):
        self.total = rows + 2 * HALO
        end = self.total
        self.own = range(HALO, end - HALO)
        self.weights_early = range(HALO + 1, end - HALO - 1)
        self.swept_early = range(HALO + 2, end - HALO - 2)
        self.joined = [HALO + 1, HALO + 2, end - HALO - 3, end - HALO - 2]
        self.weights_late = [*range(2, HALO + 1), *range(end - HALO - 1, end - 3)]
        self.weights_outer = [0, 1, end - 3, end - 2, end - 1]
        self.right_late = [HALO - 1, end - HALO]
        self.right_outer = [*range(HALO - 1), *range(end - HALO + 1, end)]
        self.swept_late = [*range(2, HALO + 2), *range(end - HALO - 2, end - 2)]
        self.mid_late = [*range(1, HALO + 1), *range(end - HALO - 1, end - 1)]

    def weights(self, early, late):
        return [
            Rows(self.total, (early.at[i], self.weights_early), (late.at[i], self.weights_late))
            for i in range(7)
        ]

    def swept(self, early, late):
        return [
            Rows(self.total, (early.at[i], self.swept_early), (late.at[i], self.swept_late))
            for i in range(2)
        ]


def fine_level(weights):
    return Level(0, weights, HALO, 0)


def set_row(conc, chem, left, right, row, conc_at, chem_at, mobility):
    c = jnp.concatenate([left, conc, right])
    if conc_at is not None:
        conc_at[row] = c
    chem_at[row] = jnp.concatenate([half_turn(left), chem, half_turn(right)])
    gap = 1.0 - c * c
    mobility[row] = 0.1 + gap * gap


def pack(sums, field, index, out):
    count = sums.shape[2] // 2
    even = lane_even((count, sums.shape[3]), 1)
    a = pair_rows(sums.at[field], 2 * index, count)
    b = pair_rows(sums.at[field], 2 * index + 1, count)
    out[field, index] = 0.125 * jnp.where(even, a + lane_roll(a, -1), b + lane_roll(b, 1))


def early_kernel(
    fields, own_left, own_right,
    packed, kept, right_conc, all_weights, joined,
    chem_start, mobility, mid, outer, sums,
):
    rows, columns = fields.shape[1:3]
    at = FrameRows(rows)
    right_side = (Rows(at.total, (right_conc, at.own)),)
    for row in at.own:
        i = row - HALO
        set_row(
            fields[0, i], fields[1, i], own_left[i], own_right[i],
            row, right_side[0], chem_start, mobility,
        )
    weights = [
        Rows(at.total, (all_weights.at[i], at.weights_early), (outer.at[i], [HALO]))
        for i in range(7)
    ]
    level = fine_level(weights)
    level.set_weights(mobility, rows - 1, HALO)
    wide = (PAD - HALO, columns + 2 * HALO)
    middle = [r for r in at.weights_early if r not in at.joined]
    mids = [
        Rows(at.total, (mid.at[i], middle), (joined.at[i], at.joined)) for i in range(2)
    ]
    swept = [Rows(at.total, (kept.at[i], at.swept_early)) for i in range(2)]
    level.sweep(
        (right_side[0], chem_start), right_side, HALO + 1, rows - 2, rows - 2, wide,
        put_window(mids, wide),
    )
    level.sweep(
        mids, right_side, HALO + 2, rows - 4, rows - 4, wide, put_window(swept, (0, wide[1]))
    )
    level.coarse_right(
        swept, right_side, 2 * HALO, rows - 2 * HALO, rows - 2 * HALO, (PAD, columns),
        put_sums(sums, HALO // 2), wide[0],
    )
    own = slice(PAD, PAD + columns)
    for index in range(rows // 2):
        row = HALO + 2 * index
        sums[2, index] = mobility[row, own, :] + mobility[row + 1, own, :]
    for index in range(rows // 4):
        pack(sums, 2, index, packed)
        if HALO // 4 <= index < (rows - HALO) // 4:
            pack(sums, 0, index, packed)
            pack(sums, 1, index, packed)
        else:
            packed[0, index] = jnp.zeros(packed.shape[2:], jnp.float32)
            packed[1, index] = jnp.zeros(packed.shape[2:], jnp.float32)


def late_kernel(
    fields, before, after, own_left, own_right, corner_left, corner_right,
    packed_early, kept_early, right_early, weights_early, joined,
    packed, kept, right_conc, all_weights,
    chem_start, mobility, mid, outer, right_outer, sums,
):
    rows, columns = fields.shape[1:3]
    at = FrameRows(rows)
    end = at.total
    right = Rows(
        end, (right_early, at.own), (right_conc, at.right_late), (right_outer, at.right_outer)
    )
    for row in [*range(HALO + 2), *range(end - HALO - 2, end)]:
        if row in at.own:
            i = row - HALO
            values = fields[0, i], fields[1, i], own_left[i], own_right[i]
            set_row(*values, row, None, chem_start, mobility)
        else:
            source, i = (before, row) if row < HALO else (after, row - rows - HALO)
            corner = row if row < HALO else row - rows
            values = source[0, i], source[1, i], corner_left[corner], corner_right[corner]
            set_row(*values, row, right, chem_start, mobility)
    weights = at.weights(weights_early, all_weights)
    for i, one in enumerate(weights):
        for index, row in enumerate(at.weights_outer):
            one.places[row] = outer.at[i], index
    level = fine_level(weights)
    level.set_weights(mobility, HALO + 1, 0)
    level.set_weights(mobility, HALO + 1, end - HALO - 1)
    wide = (PAD - HALO, columns + 2 * HALO)
    mids = [Rows(end, (joined.at[i], at.joined), (mid.at[i], at.mid_late)) for i in range(2)]
    swept = at.swept(kept_early, kept)
    for start in (1, end - HALO - 1):
        level.sweep(
            (right, chem_start), (right,), start, HALO, HALO, wide, put_window(mids, wide)
        )
    for start in (2, end - HALO - 2):
        level.sweep(mids, (right,), start, HALO, HALO, wide, put_window(swept, (0, wide[1])))
    for start in (HALO, end - 2 * HALO):
        level.coarse_right(
            swept, (right,), start, HALO, HALO, (PAD, columns),
            put_sums(sums, (start - HALO) // 2), wide[0],
        )
    packed[...] = packed_early[...]
    for index in range(rows // 4):
        if not HALO // 4 <= index < (rows - HALO) // 4:
            pack(sums, 0, index, packed)
            pack(sums, 1, index, packed)


def coarse_kernel(
    slots, grid, first, second, first_far, second_far,
    kept_early, right_early, weights_early, kept_late, right_late, weights_late,
    conc_new, chem_new, *scratch,
):
    at = FrameRows(conc_new.shape[0])
    conc_in, chem_in = at.swept(kept_early, kept_late)
    weights = at.weights(weights_early, weights_late)
    right_conc = Rows(at.total, (right_early, at.own), (right_late, at.right_late))
    scratch = list(scratch)
    start_even, at_y = lax.axis_index("gx") % 2 == 0, lax.axis_index("gy")
    levels = []
    for level_index in (1, 2, 3):
        level = Level(level_index, scratch[5:14][2:])
        mobility, a, b, right = scratch[0], scratch[1:3], scratch[3:5], scratch[5:7]
        levels.append((level, mobility, right, a, b))
        del scratch[:14]
    sums1, sums2, spread2, spread3, spread_fine, fine_a0, fine_a1, fine_b0, fine_b1 = scratch
    one, mob1, right1, a1, b1 = levels[0]
    two, mob2, right2, a2, b2 = levels[1]
    three, mob3, right3, a3, b3 = levels[2]
    rows1, columns1, lanes = right1[0].shape
    rows2, columns2 = right2[0].shape[:2]
    rows3, columns3 = right3[0].shape[:2]
    window1, window2, window3 = (PAD, columns1), (PAD, columns2), (PAD, columns3)
    own_rows, own_columns = 2 * rows1 // grid[0], columns1 // grid[1]
    even = lane_even((own_columns, lanes), 1)
    blocks = {}
    for last, sources in enumerate(((first, second), (first_far, second_far))):
        for source, masks in zip(sources, slots):
            for slot, (mask_x, mask_y) in enumerate(masks):
                blocks[mask_x, mask_y ^ last] = source.at[slot]

    for mask_y in range(grid[1]):
        offset = (at_y ^ mask_y) * own_columns
        plain = pl.ds(pl.multiple_of(offset, PAD), own_columns)
        padded = pl.ds(pl.multiple_of(offset + PAD, PAD), own_columns)
        for field, (ref, at) in enumerate(
            ((right1[0], plain), (right1[1], plain), (mob1, padded))
        ):
            for index in range(own_rows // 2):
                own, two_on, one_on, one_back = (
                    blocks[mask_x, mask_y][field, index] for mask_x in (0, 2, 1, 3)
                )
                swap = one_on, one_back
                one_on = jnp.where(start_even, swap[0], swap[1])
                one_back = jnp.where(start_even, swap[1], swap[0])
                for row, a, b in ((0, own, two_on), (own_rows, one_on, one_back)):
                    row = row + 2 * index
                    ref[row, at, :] = jnp.where(even, a, lane_roll(b, 1))
                    ref[row + 1, at, :] = jnp.where(even, lane_roll(a, -1), b)
    for row in range(rows1):
        mob1[row, :PAD, :] = mob1[row, columns1 : columns1 + PAD, :]
        mob1[row, PAD + columns1 :, :] = mob1[row, PAD : 2 * PAD, :]

    def coarsen(mobility, sums, out, out_mobility, dup):
        count, columns = out[0].shape[:2]
        fine = pl.ds(PAD, 2 * columns)
        for index in range(count):
            sums[2, index] = mobility[2 * index, fine, :] + mobility[2 * index + 1, fine, :]
        for index in range(count):
            for field in range(2):
                half = pair_rows(sums.at[field], index, columns)
                out[field][index] = 0.125 * pair_lanes(half, dup)
            half = pair_rows(sums.at[2], index, columns)
            put_padded((out_mobility,))(index, 0.125 * pair_lanes(half, dup))

    half1 = rows1 // 2
    for start in (0, half1):
        stage(one.set_weights, mob1, half1, start)
    stage(one.first_sweep, right1, rows1, put_padded(a1))
    for start in (0, half1):
        stage(one.sweep, a1, right1, start, half1, half1, window1, put_padded(b1))
    for start in (0, half1):
        put = put_sums(sums1, start // 2)
        stage(one.coarse_right, b1, right1, start, half1, half1, window1, put)
    stage(coarsen, mob1, sums1, right2, mob2, 2)

    stage(two.set_weights, mob2, rows2)
    stage(two.first_sweep, right2, rows2, put_padded(a2))
    stage(two.sweep, a2, right2, 0, rows2, rows2, window2, put_padded(b2))
    stage(two.coarse_right, b2, right2, 0, rows2, rows2, window2, put_sums(sums2))
    stage(coarsen, mob2, sums2, right3, mob3, 4)

    stage(three.set_weights, mob3, rows3)
    stage(three.first_sweep, right3, rows3, put_padded(a3))
    now, other = a3, b3
    for sweep_index in range(COARSE - 1):
        stage(three.sweep, now, right3, 0, rows3, rows3, window3, put_padded(other))
        now, other = other, now

    def correct(coarse, coarse_row, fine_in, fine_out, spread, index):
        for field in range(2):
            columns = fine_in[field].shape[1] - 2 * PAD
            spread_rows(
                spread.at[field], index, coarse[field][coarse_row, pl.ds(PAD, columns // 2), :]
            )
            both = spread[field, index]
            for row in (2 * coarse_row, 2 * coarse_row + 1):
                put_padded((fine_out[field],))(
                    row, fine_in[field][row, pl.ds(PAD, columns), :] + both
                )

    for row in range(rows3):
        correct(now, row, b2, a2, spread3, row)
    stage(two.sweep, a2, right2, 0, rows2, rows2, window2, put_padded(b2))
    stage(two.sweep, b2, right2, 0, rows2, rows2, window2, put_padded(a2))
    for row in range(rows2):
        correct(a2, row, b1, a1, spread2, row)
    for start, count in ((-2, 6), (4, own_rows - 2)):
        stage(one.sweep, a1, right1, start, count, count, window1, put_padded(b1))
    for start, count in ((-1, 5), (4, own_rows - 3)):
        stage(one.sweep, b1, right1, start, count, count, window1, put_padded(a1))

    rows, columns = conc_new.shape[:2]
    wide = (PAD - HALO, columns + 2 * HALO)
    near_own = pl.ds(pl.multiple_of(at_y * own_columns, PAD), own_columns + 2 * PAD)
    for index in range(own_rows + 2):
        inside = 1 <= index <= rows1
        row = index - 1 if inside else (index - 1) % rows1
        for field, (source, target) in enumerate(((conc_in, fine_a0), (chem_in, fine_a1))):
            tile = a1[field][row, near_own, :]
            on_even = lane_even(tile.shape, 1)
            if inside:
                tile = jnp.where(on_even, tile, lane_roll(tile, 1))
            else:
                tile = jnp.where(on_even, lane_roll(tile, -1), tile)
            spread_rows(spread_fine.at[field], index, tile)
            both = spread_fine[field, index, pl.ds(wide[0] + PAD, wide[1]), :]
            for fine in (HALO - 2 + 2 * index, HALO - 1 + 2 * index):
                put_window((target,), wide)(fine, source[fine] + both)
    fine = fine_level(weights)
    right_side = (right_conc,)
    fine.sweep(
        (fine_a0, fine_a1), right_side, HALO - 1, rows + 2, rows + 2, wide,
        put_window((fine_b0, fine_b1), wide),
    )

    def put_new(row, conc_value, chem_value):
        conc_new[row - HALO] = conc_value
        chem_new[row - HALO] = chem_value

    fine.sweep((fine_b0, fine_b1), right_side, HALO, rows, rows, (PAD, columns), put_new)


def call_kernel(kernel, outs, scratch, *args, vmem_mib=8):
    shapes = tuple(jax.ShapeDtypeStruct(shape, jnp.float32) for shape in outs)
    return pl.pallas_call(
        kernel,
        out_shape=shapes,
        in_specs=[whole_block()] * len(args),
        out_specs=tuple(whole_block() for _ in outs),
        scratch_shapes=[pltpu.VMEM(shape, jnp.float32) for shape in scratch],
        compiler_params=pltpu.CompilerParams(vmem_limit_bytes=vmem_mib * 1024 * 1024),
    )(*args)


def shifted(values, axis, by):
    count = lax.axis_size(axis)
    return lax.ppermute(values, axis, [(i, (i + by) % count) for i in range(count)])


def swapped(values, axis, mask):
    count = lax.axis_size(axis)
    return lax.ppermute(values, axis, [(i, i ^ mask) for i in range(count)])


def far_masks():
    count_x, count_y = lax.axis_size("gx"), lax.axis_size("gy")
    return list(range(1, count_x)), list(range(2, count_y, 2))


def slot_masks():
    along_x, along_y = far_masks()
    first = [(0, 0)] + [(0, y) for y in along_y] + [(x, 0) for x in along_x]
    second = [(x, y) for y in along_y for x in along_x[1:]]
    return first, second + [(along_x[0], y) for y in along_y]


def swapped_both(values, mask_x, mask_y):
    count_x, count_y = lax.axis_size("gx"), lax.axis_size("gy")
    pairs = [
        (x * count_y + y, (x ^ mask_x) * count_y + (y ^ mask_y))
        for x in range(count_x)
        for y in range(count_y)
    ]
    return lax.ppermute(values, ("gx", "gy"), pairs)


def gathered(values):
    along_x, along_y = far_masks()
    across = [swapped(values, "gx", mask) for mask in along_x]
    beside = [swapped(values, "gy", mask) for mask in along_y]
    later, _ = lax.optimization_barrier((values, across[2]))
    corner = [swapped_both(later, along_x[0], mask) for mask in along_y]
    first = jnp.stack([values] + beside + across)
    second = [swapped(block, "gy", mask) for mask in along_y for block in across[1:]]
    second = jnp.stack(second + corner)
    return first, second, swapped(first, "gy", 1), swapped(second, "gy", 1)


def two_phase_solve(conc, chem):
    rows, columns, lanes = conc.shape
    frame = (rows + 2 * HALO, columns + 2 * PAD, lanes)
    edge = (2, HALO, columns, lanes)
    block = (rows, columns, lanes)
    fields = jnp.concatenate([conc, chem], axis=0).reshape((2,) + block)
    side, corner = (rows, PAD, lanes), (2 * HALO, PAD, lanes)
    low, high, to_left, to_right = call_kernel(
        edges_kernel, (edge, edge, side, side), (), fields
    )
    before, after = shifted(high, "gx", 1), shifted(low, "gx", -1)
    sides = [shifted(to_right, "gy", 1), shifted(to_left, "gy", -1)]
    to_left, to_right = call_kernel(corners_kernel, (corner, corner), (), before, after)
    sides += [shifted(to_right, "gy", 1), shifted(to_left, "gy", -1)]
    at, width = FrameRows(rows), columns + 2 * HALO
    packed_shape, sums = (3, rows // 4, columns // 2, lanes), (3, rows // 2, columns, lanes)

    def part(count, listed, wide):
        return (count, len(listed), wide, lanes)

    right_shapes = [part(0, listed, frame[1])[1:] for listed in (at.own, at.right_late, at.right_outer)]
    early, *kept = call_kernel(
        early_kernel,
        (
            packed_shape, part(2, at.swept_early, width), right_shapes[0],
            part(7, at.weights_early, width), part(2, at.joined, frame[1]),
        ),
        (frame, frame, part(2, at.weights_early, frame[1]), part(7, [0], width), sums),
        fields, *sides[:2],
    )
    packed, *kept_late = call_kernel(
        late_kernel,
        (
            packed_shape, part(2, at.swept_late, width), right_shapes[1],
            part(7, at.weights_late, width),
        ),
        (
            frame, frame, part(2, at.mid_late, frame[1]), part(7, at.weights_outer, width),
            right_shapes[2], sums,
        ),
        fields, before, after, *sides, early, *kept,
    )
    count_x, count_y = lax.axis_size("gx"), lax.axis_size("gy")
    grids = [(count_x * rows >> level + 1, count_y * columns >> level) for level in range(4)]
    scratch = []
    for level_rows, level_columns in grids[1:]:
        scratch += [(level_rows, level_columns + 2 * PAD, lanes)] * 5
        scratch += [(level_rows, level_columns, lanes)] * 9
    scratch += [(3, grids[2][0], grids[1][1], lanes), (3, grids[3][0], grids[2][1], lanes)]
    scratch += [(2, grids[2][0], grids[1][1], lanes), (2, grids[3][0], grids[2][1], lanes)]
    scratch += [(2, rows // 2 + 2, columns + 4 * PAD, lanes)] + [frame] * 4
    kernel = functools.partial(coarse_kernel, slot_masks(), (count_x, count_y))
    args = (*gathered(packed), *kept[:3], *kept_late)
    return call_kernel(kernel, (block, block), scratch, *args, vmem_mib=24)


def body(conc_old, chem_old):
    rows, columns, lanes = conc_old.shape
    count_x, count_y = lax.axis_size("gx"), lax.axis_size("gy")
    grid_bytes = count_x * rows * count_y * columns * lanes
    if (
        grid_bytes <= GRID_BYTES_MAX
        and rows % 16 == 0
        and lanes % 128 == 0
        and count_x * rows >= 64
        and count_y * columns >= 64
        and count_x == 4
        and count_y >= 4
        and count_y & (count_y - 1) == 0
        and columns == 16
    ):
        return two_phase_solve(conc_old, chem_old)
    start_fields = jnp.stack([conc_old, chem_old])
    result = plain_solve(start_fields)
    return (result[0], result[1])


def solution(mesh):
    in_specs = (P(("img", "gx"), "gy", None), P(("img", "gx"), "gy", None))
    out_specs = (P(("img", "gx"), "gy", None), P(("img", "gx"), "gy", None))
    return jax.shard_map(body, mesh=mesh, in_specs=in_specs, out_specs=out_specs, check_vma=False)
```

```python
import functools

import jax
import jax.numpy as jnp
from jax import lax
from jax.experimental import pallas as pl
from jax.experimental.pallas import tpu as pltpu
from jax.sharding import PartitionSpec as P

LEVELS = 4
SWEEPS = 2
COARSE = 6


TIME_STEP = 32.0
GRADIENT_ENERGY = 0.5
STABILIZER = 2.0
DAMPING = 0.7


def extended(cells, sides, width):
    for axis, dim in sides:
        count = lax.axis_size(axis)
        head = lax.slice_in_dim(cells, 0, width, axis=dim)
        tail = lax.slice_in_dim(cells, cells.shape[dim] - width, cells.shape[dim], axis=dim)
        cells = jnp.concatenate(
            [
                lax.ppermute(tail, axis, [(i, (i + 1) % count) for i in range(count)]),
                cells,
                lax.ppermute(head, axis, [((i + 1) % count, i) for i in range(count)]),
            ],
            axis=dim,
        )
    return cells


def mobility_of(concentration):
    return 0.1 + jnp.square(1.0 - concentration * concentration)


def right_of(concentration):
    return jnp.stack(
        [
            concentration,
            concentration * concentration * concentration - (1.0 + STABILIZER) * concentration,
        ]
    )


def face_weights(mob_padded, level_scale):
    middle = mob_padded[1:-1, 1:-1, :]
    half_scale = 0.5 * level_scale
    weights = (
        half_scale * (middle + mob_padded[2:, 1:-1, :]),
        half_scale * (middle + mob_padded[:-2, 1:-1, :]),
        half_scale * (middle + mob_padded[1:-1, 2:, :]),
        half_scale * (middle + mob_padded[1:-1, :-2, :]),
        half_scale * (middle + jnp.roll(middle, -1, axis=2)),
        half_scale * (middle + jnp.roll(middle, 1, axis=2)),
    )
    total_weight = weights[0] + weights[1] + weights[2] + weights[3] + weights[4] + weights[5]
    return (weights, total_weight)


def neighbour_list(padded, middle):
    return (
        padded[2:, 1:-1, :],
        padded[:-2, 1:-1, :],
        padded[1:-1, 2:, :],
        padded[1:-1, :-2, :],
        jnp.roll(middle, -1, axis=2),
        jnp.roll(middle, 1, axis=2),
    )


def apply_operator(padded, weights, level_scale):
    middle = padded[:, 1:-1, 1:-1, :]
    conc_near = neighbour_list(padded[0], middle[0])
    chem_near = neighbour_list(padded[1], middle[1])
    flux = weights[0] * (chem_near[0] - middle[1])
    for position in range(1, 6):
        flux = flux + weights[position] * (chem_near[position] - middle[1])
    laplace = (
        conc_near[0]
        + conc_near[1]
        + conc_near[2]
        + conc_near[3]
        + conc_near[4]
        + conc_near[5]
        - 6.0 * middle[0]
    )
    first_eq = middle[0] - TIME_STEP * flux
    second_eq = middle[1] - STABILIZER * middle[0] + GRADIENT_ENERGY * level_scale * laplace
    return jnp.stack([first_eq, second_eq])


def update(residual, total_weight, level_scale):
    diagonal = STABILIZER + 6.0 * GRADIENT_ENERGY * level_scale
    coupling = TIME_STEP * total_weight
    determinant = 1.0 + coupling * diagonal
    conc_step = (residual[0] - coupling * residual[1]) / determinant
    chem_step = (residual[1] + diagonal * residual[0]) / determinant
    return DAMPING * jnp.stack([conc_step, chem_step])


def sweep_once(padded, right_side, mob_padded, level_scale):
    weights, total_weight = face_weights(mob_padded, level_scale)
    residual = right_side - apply_operator(padded, weights, level_scale)
    return padded[:, 1:-1, 1:-1, :] + update(residual, total_weight, level_scale)


def defect(padded, right_side, mob_padded, level_scale):
    weights = face_weights(mob_padded, level_scale)[0]
    return right_side - apply_operator(padded, weights, level_scale)


def coarsen(values):
    dims_now = values.shape
    grouped = values.reshape(
        dims_now[:-3] + (dims_now[-3] // 2, 2, dims_now[-2] // 2, 2, dims_now[-1] // 2, 2)
    )
    return jnp.sum(grouped, axis=(-5, -3, -1)) * 0.125


def refine(values):
    for axis_pos in (-3, -2, -1):
        values = jnp.repeat(values, 2, axis=axis_pos)
    return values


def trim_rim(values, width):
    return values[..., width:-width, width:-width, :]


def field_rim(fields):
    return extended(fields, (("gx", 1), ("gy", 2)), 1)


def coarsest_solve(right_side, mobility, level_scale):
    mob_padded = extended(mobility, (("gx", 0), ("gy", 1)), 1)
    fields = update(right_side, face_weights(mob_padded, level_scale)[1], level_scale)
    for sweep_index in range(COARSE - 1):
        padded = extended(fields, (("gx", 1), ("gy", 2)), 1)
        fields = sweep_once(padded, right_side, mob_padded, level_scale)
    return fields


def plain_solve(start_fields):
    outer_fields = field_rim(start_fields)
    mob_outer = mobility_of(outer_fields[0])
    mobility = trim_rim(mob_outer, 1)
    level_data = []
    for level_index in range(LEVELS - 1):
        if level_index == 0:
            mob_padded = mob_outer
        else:
            mob_padded = extended(mobility, (("gx", 0), ("gy", 1)), 1)
        level_data.append((mob_padded, 0.25**level_index))
        mobility = coarsen(mobility)
    coarsest_scale = 0.25 ** (LEVELS - 1)

    def cycle_level(level_index, right_side):
        if level_index == LEVELS - 1:
            return coarsest_solve(right_side, mobility, coarsest_scale)
        mob_padded, level_scale = level_data[level_index]
        if level_index == 0:
            fields = sweep_once(outer_fields, right_side, mob_padded, level_scale)
        else:
            fields = update(right_side, face_weights(mob_padded, level_scale)[1], level_scale)
        fields = sweep_once(field_rim(fields), right_side, mob_padded, level_scale)
        residual = defect(field_rim(fields), right_side, mob_padded, level_scale)
        fields = fields + refine(cycle_level(level_index + 1, coarsen(residual)))
        for sweep_index in range(SWEEPS):
            fields = sweep_once(field_rim(fields), right_side, mob_padded, level_scale)
        return fields

    return cycle_level(0, right_of(start_fields[0]))


HALO = 4
PAD = 8
GRID_BYTES_MAX = 2 * 1024 * 1024


def whole_block():
    return pl.BlockSpec(memory_space=pltpu.VMEM)


def lane_roll(values, shift):
    return pltpu.roll(values, shift % values.shape[1], axis=1)


def lane_even(shape, dup):
    return (lax.broadcasted_iota(jnp.int32, shape, 1) // dup) % 2 == 0


def loop_rows(count, unroll, row_group):
    steps, rest = divmod(count, unroll)
    if steps == 1:
        row_group(0, unroll)
    elif steps > 1:

        def step(index, carry):
            row_group(index * unroll, unroll)
            return carry

        lax.fori_loop(0, steps, step, 0)
    if rest:
        row_group(steps * unroll, rest)


def lane_swap(values):
    return jnp.where(lane_even(values.shape, 1), lane_roll(values, -1), lane_roll(values, 1))


class RowCache:
    def __init__(self, ref, rows, first, width):
        self.ref, self.rows, self.first, self.width = ref, rows, first, width
        self.values = {}

    def __getitem__(self, key):
        if key not in self.values:
            total = self.ref.shape[0]
            row = key if self.rows is None else self.rows[key]
            outside = isinstance(row, int) and not 0 <= row < total
            values = self.ref[row % total if outside else row, pl.ds(self.first, self.width), :]
            self.values[key] = lane_swap(values) if outside else values
        return self.values[key]


def stage(run, *args):
    pl.when(lax.axis_index("gy") >= 0)(functools.partial(run, *args))


def chem_right(conc):
    return conc * (conc * conc - (1.0 + STABILIZER))


class Rows:
    def __init__(self, total, *parts):
        self.places = {
            row: (ref, index) for ref, rows in parts for index, row in enumerate(rows)
        }
        self.shape = (total,) + parts[0][0].shape[1:]

    def place(self, at):
        row, *rest = at if isinstance(at, tuple) else (at,)
        ref, index = self.places[row]
        return ref, (index, *rest)

    def __getitem__(self, at):
        ref, index = self.place(at)
        return ref[index]

    def __setitem__(self, at, values):
        ref, index = self.place(at)
        ref[index] = values


class Level:
    def __init__(self, level_index, weights, weights_from=PAD, right_from=PAD):
        self.scale = 0.25**level_index
        self.dup = 2**level_index
        self.diagonal = STABILIZER + 6.0 * GRADIENT_ENERGY * self.scale
        self.weights = weights
        self.weights_from, self.right_from = weights_from, right_from

    def set_weights(self, mobility, count, start=0):
        width = self.weights[0].shape[1]
        half = 0.5 * self.scale * TIME_STEP
        face_x, up_y, down_y, up_z, down_z, coupling, gain = self.weights

        def at(row, shift=0):
            return mobility[row, pl.ds(self.weights_from + shift, width), :]

        def group(first, size):
            rows = RowCache(mobility, None, self.weights_from, width)
            before = half * (rows[start + first - 1] + rows[start + first])
            for i in range(size):
                r = start + first + i
                here = rows[r]
                after = half * (here + rows[r + 1])
                to_up_y = half * (here + at(r, 1))
                to_down_y = half * (here + at(r, -1))
                to_up_z = half * (here + lane_roll(here, -self.dup))
                to_down_z = half * (here + lane_roll(here, self.dup))
                total_weight = (before + after) + (to_up_y + to_down_y) + (to_up_z + to_down_z)
                face_x[r] = after
                up_y[r] = to_up_y
                down_y[r] = to_down_y
                up_z[r] = to_up_z
                down_z[r] = to_down_z
                coupling[r] = total_weight
                gain[r] = DAMPING / (1.0 + total_weight * self.diagonal)
                before = after

        loop_rows(count, count, group)

    def residuals(self, fields, right, rows, window, fields_from=0):
        conc, chem = fields
        first, width = window
        face_x, up_y, down_y, up_z, down_z, coupling, gain = self.weights

        def at(ref, row, shift=0):
            return ref[row, pl.ds(first - fields_from + shift, width), :]

        def weight(ref, row):
            return ref[row, pl.ds(first - self.weights_from, width), :]

        def right_at(row):
            values = [ref[row, pl.ds(first - self.right_from, width), :] for ref in right]
            return values if len(values) == 2 else values + [chem_right(values[0])]

        total = conc.shape[0]
        if isinstance(rows[0], int):
            centres, listed = [row % total for row in rows[1:-1]], None
        else:
            centres, listed = range(1, len(rows) - 1), rows
        u = RowCache(chem, listed, first - fields_from, width)
        c = RowCache(conc, listed, first - fields_from, width)
        across = RowCache(face_x, listed, first - self.weights_from, width)
        for key in centres:
            r = key if listed is None else listed[key]
            c_here, u_here = c[key], u[key]
            here = weight(coupling, r)
            conc_right, chem_right_here = right_at(r)
            flux = across[key] * u[key + 1] + across[key - 1] * u[key - 1]
            flux = flux + (weight(up_y, r) * at(chem, r, 1) + weight(down_y, r) * at(chem, r, -1))
            flux = flux + (conc_right - c_here - here * u_here)
            flux_z = weight(up_z, r) * lane_roll(u_here, -self.dup)
            flux_z = flux_z + weight(down_z, r) * lane_roll(u_here, self.dup)
            conc_left = flux + flux_z
            near = (c[key - 1] + c[key + 1]) + (at(conc, r, 1) + at(conc, r, -1))
            pull = GRADIENT_ENERGY * self.scale
            chem_left = (chem_right_here - u_here + self.diagonal * c_here) - pull * near
            near_z = lane_roll(c_here, self.dup) + lane_roll(c_here, -self.dup)
            chem_left = chem_left - pull * near_z
            yield r, c_here, u_here, conc_left, chem_left, here, weight(gain, r)

    def steps(self, conc_left, chem_left, coupling, gain):
        return (
            gain * (conc_left - coupling * chem_left),
            gain * (chem_left + self.diagonal * conc_left),
        )

    def first_sweep(self, right, unroll, put):
        coupling, gain = self.weights[5:]

        def group(first, size):
            for i in range(size):
                r = first + i
                put(r, *self.steps(right[0][r], right[1][r], coupling[r], gain[r]))

        loop_rows(right[0].shape[0], unroll, group)

    def row_window(self, start, first, size):
        return [start + first + i - 1 for i in range(size + 2)]

    def sweep(self, fields, right, start, count, unroll, window, put):
        def group(first, size):
            rows = self.row_window(start, first, size)
            for r, c, u, *left in self.residuals(fields, right, rows, window):
                conc_step, chem_step = self.steps(*left)
                put(r, c + conc_step, u + chem_step)

        loop_rows(count, unroll, group)

    def coarse_right(self, fields, right, start, count, unroll, window, put, fields_from=0):
        def group(first, size):
            rows = self.row_window(start, first, size)
            items = self.residuals(fields, right, rows, window, fields_from)
            half = first // 2 if isinstance(first, int) else lax.shift_right_logical(first, 1)
            kept = None
            for i, (_, _, _, conc_left, chem_left, _, _) in enumerate(items):
                if i % 2 == 0:
                    kept = conc_left, chem_left
                else:
                    put(half + i // 2, kept[0] + conc_left, kept[1] + chem_left)

        loop_rows(count, unroll, group)


def put_padded(refs):
    def put(row, *values):
        for ref, value in zip(refs, values):
            width = value.shape[0]
            ref[row, PAD : PAD + width, :] = value
            ref[row, :PAD, :] = value[width - PAD :]
            ref[row, PAD + width :, :] = value[:PAD]

    return put


def put_window(refs, window):
    def put(row, *values):
        for ref, value in zip(refs, values):
            ref[row, window[0] : window[0] + window[1], :] = value

    return put


def put_sums(sums, offset=0):
    def put(row, *values):
        for field, value in enumerate(values):
            sums[field, offset + row] = value

    return put


def pair_rows(ref, row, count):
    return ref[row, pl.ds(0, count, stride=2), :] + ref[row, pl.ds(1, count, stride=2), :]


def spread_rows(ref, row, values):
    count = values.shape[0]
    ref[row, pl.ds(0, count, stride=2), :] = values
    ref[row, pl.ds(1, count, stride=2), :] = values


def pair_lanes(values, dup):
    other = jnp.where(
        lane_even(values.shape, dup), lane_roll(values, -dup), lane_roll(values, dup)
    )
    return values + other


def side_tiles(conc, chem, to_left, to_right, at, low):
    columns = conc.shape[0]
    to_left[at] = jnp.where(low, conc[:PAD], half_turn(chem[:PAD]))
    to_right[at] = jnp.where(low, half_turn(chem[columns - PAD :]), conc[columns - PAD :])


def low_half(lanes):
    return lax.broadcasted_iota(jnp.int32, (PAD, lanes), 0) < HALO


def edges_kernel(fields, low_rows, high_rows, to_left, to_right):
    rows, columns, lanes = fields.shape[1:]
    low_rows[...] = fields[:, :HALO]
    high_rows[...] = fields[:, rows - HALO :]
    for row in range(rows):
        side_tiles(fields[0, row], fields[1, row], to_left, to_right, row, low_half(lanes))


def corners_kernel(before, after, to_left, to_right):
    lanes = before.shape[-1]
    for at in range(2 * HALO):
        source, row = (before, at) if at < HALO else (after, at - HALO)
        side_tiles(source[0, row], source[1, row], to_left, to_right, at, low_half(lanes))


def frame_row(row, rows, own, before, after):
    if row < HALO:
        return before[row]
    if row < HALO + rows:
        return own[row - HALO]
    return after[row - HALO - rows]


def half_turn(values):
    return pltpu.roll(values, HALO, axis=0)


class FrameRows:
    def __init__(self, rows):
        self.total = rows + 2 * HALO
        end = self.total
        self.own = range(HALO, end - HALO)
        self.weights_early = range(HALO + 1, end - HALO - 1)
        self.swept_early = range(HALO + 2, end - HALO - 2)
        self.joined = [HALO + 1, HALO + 2, end - HALO - 3, end - HALO - 2]
        self.weights_late = [*range(2, HALO + 1), *range(end - HALO - 1, end - 3)]
        self.weights_outer = [0, 1, end - 3, end - 2, end - 1]
        self.right_late = [HALO - 1, end - HALO]
        self.right_outer = [*range(HALO - 1), *range(end - HALO + 1, end)]
        self.swept_late = [*range(2, HALO + 2), *range(end - HALO - 2, end - 2)]
        self.mid_late = [*range(1, HALO + 1), *range(end - HALO - 1, end - 1)]

    def weights(self, early, late):
        return [
            Rows(self.total, (early.at[i], self.weights_early), (late.at[i], self.weights_late))
            for i in range(7)
        ]

    def swept(self, early, late):
        return [
            Rows(self.total, (early.at[i], self.swept_early), (late.at[i], self.swept_late))
            for i in range(2)
        ]


def fine_level(weights):
    return Level(0, weights, HALO, 0)


def set_row(conc, chem, left, right, row, conc_at, chem_at, mobility):
    c = jnp.concatenate([left, conc, right])
    if conc_at is not None:
        conc_at[row] = c
    chem_at[row] = jnp.concatenate([half_turn(left), chem, half_turn(right)])
    gap = 1.0 - c * c
    mobility[row] = 0.1 + gap * gap


def pack(sums, field, index, out):
    count = sums.shape[2] // 2
    even = lane_even((count, sums.shape[3]), 1)
    a = pair_rows(sums.at[field], 2 * index, count)
    b = pair_rows(sums.at[field], 2 * index + 1, count)
    out[field, index] = 0.125 * jnp.where(even, a + lane_roll(a, -1), b + lane_roll(b, 1))


def early_kernel(
    fields, own_left, own_right,
    packed, kept, right_conc, all_weights, joined,
    chem_start, mobility, mid, outer, sums,
):
    rows, columns = fields.shape[1:3]
    at = FrameRows(rows)
    right_side = (Rows(at.total, (right_conc, at.own)),)
    for row in at.own:
        i = row - HALO
        set_row(
            fields[0, i], fields[1, i], own_left[i], own_right[i],
            row, right_side[0], chem_start, mobility,
        )
    weights = [
        Rows(at.total, (all_weights.at[i], at.weights_early), (outer.at[i], [HALO]))
        for i in range(7)
    ]
    level = fine_level(weights)
    level.set_weights(mobility, rows - 1, HALO)
    wide = (PAD - HALO, columns + 2 * HALO)
    middle = [r for r in at.weights_early if r not in at.joined]
    mids = [
        Rows(at.total, (mid.at[i], middle), (joined.at[i], at.joined)) for i in range(2)
    ]
    swept = [Rows(at.total, (kept.at[i], at.swept_early)) for i in range(2)]
    level.sweep(
        (right_side[0], chem_start), right_side, HALO + 1, rows - 2, rows - 2, wide,
        put_window(mids, wide),
    )
    level.sweep(
        mids, right_side, HALO + 2, rows - 4, rows - 4, wide, put_window(swept, (0, wide[1]))
    )
    level.coarse_right(
        swept, right_side, 2 * HALO, rows - 2 * HALO, rows - 2 * HALO, (PAD, columns),
        put_sums(sums, HALO // 2), wide[0],
    )
    own = slice(PAD, PAD + columns)
    for index in range(rows // 2):
        row = HALO + 2 * index
        sums[2, index] = mobility[row, own, :] + mobility[row + 1, own, :]
    for index in range(rows // 4):
        pack(sums, 2, index, packed)
        if HALO // 4 <= index < (rows - HALO) // 4:
            pack(sums, 0, index, packed)
            pack(sums, 1, index, packed)
        else:
            packed[0, index] = jnp.zeros(packed.shape[2:], jnp.float32)
            packed[1, index] = jnp.zeros(packed.shape[2:], jnp.float32)


def late_kernel(
    fields, before, after, own_left, own_right, corner_left, corner_right,
    packed_early, kept_early, right_early, weights_early, joined,
    packed, kept, right_conc, all_weights,
    chem_start, mobility, mid, outer, right_outer, sums,
):
    rows, columns = fields.shape[1:3]
    at = FrameRows(rows)
    end = at.total
    right = Rows(
        end, (right_early, at.own), (right_conc, at.right_late), (right_outer, at.right_outer)
    )
    for row in [*range(HALO + 2), *range(end - HALO - 2, end)]:
        if row in at.own:
            i = row - HALO
            values = fields[0, i], fields[1, i], own_left[i], own_right[i]
            set_row(*values, row, None, chem_start, mobility)
        else:
            source, i = (before, row) if row < HALO else (after, row - rows - HALO)
            corner = row if row < HALO else row - rows
            values = source[0, i], source[1, i], corner_left[corner], corner_right[corner]
            set_row(*values, row, right, chem_start, mobility)
    weights = at.weights(weights_early, all_weights)
    for i, one in enumerate(weights):
        for index, row in enumerate(at.weights_outer):
            one.places[row] = outer.at[i], index
    level = fine_level(weights)
    level.set_weights(mobility, HALO + 1, 0)
    level.set_weights(mobility, HALO + 1, end - HALO - 1)
    wide = (PAD - HALO, columns + 2 * HALO)
    mids = [Rows(end, (joined.at[i], at.joined), (mid.at[i], at.mid_late)) for i in range(2)]
    swept = at.swept(kept_early, kept)
    for start in (1, end - HALO - 1):
        level.sweep(
            (right, chem_start), (right,), start, HALO, HALO, wide, put_window(mids, wide)
        )
    for start in (2, end - HALO - 2):
        level.sweep(mids, (right,), start, HALO, HALO, wide, put_window(swept, (0, wide[1])))
    for start in (HALO, end - 2 * HALO):
        level.coarse_right(
            swept, (right,), start, HALO, HALO, (PAD, columns),
            put_sums(sums, (start - HALO) // 2), wide[0],
        )
    packed[...] = packed_early[...]
    for index in range(rows // 4):
        if not HALO // 4 <= index < (rows - HALO) // 4:
            pack(sums, 0, index, packed)
            pack(sums, 1, index, packed)


def coarse_kernel(
    slots, grid, first, second, third, first_far, second_far, third_far,
    kept_early, right_early, weights_early, kept_late, right_late, weights_late,
    conc_new, chem_new, *scratch,
):
    at = FrameRows(conc_new.shape[0])
    conc_in, chem_in = at.swept(kept_early, kept_late)
    weights = at.weights(weights_early, weights_late)
    right_conc = Rows(at.total, (right_early, at.own), (right_late, at.right_late))
    scratch = list(scratch)
    start_even, at_y = lax.axis_index("gx") % 2 == 0, lax.axis_index("gy")
    levels = []
    for level_index in (1, 2, 3):
        level = Level(level_index, scratch[5:14][2:])
        mobility, a, b, right = scratch[0], scratch[1:3], scratch[3:5], scratch[5:7]
        levels.append((level, mobility, right, a, b))
        del scratch[:14]
    sums1, sums2, spread2, spread3, spread_fine, fine_a0, fine_a1, fine_b0, fine_b1 = scratch
    one, mob1, right1, a1, b1 = levels[0]
    two, mob2, right2, a2, b2 = levels[1]
    three, mob3, right3, a3, b3 = levels[2]
    rows1, columns1, lanes = right1[0].shape
    rows2, columns2 = right2[0].shape[:2]
    rows3, columns3 = right3[0].shape[:2]
    window1, window2, window3 = (PAD, columns1), (PAD, columns2), (PAD, columns3)
    own_rows, own_columns = 2 * rows1 // grid[0], columns1 // grid[1]
    even = lane_even((own_columns, lanes), 1)
    blocks = {}
    for last, sources in enumerate(((first, second, third), (first_far, second_far, third_far))):
        for source, masks in zip(sources, slots):
            for slot, (mask_x, mask_y) in enumerate(masks):
                blocks[mask_x, mask_y ^ last] = source.at[slot]

    for mask_y in range(grid[1]):
        offset = (at_y ^ mask_y) * own_columns
        plain = pl.ds(pl.multiple_of(offset, PAD), own_columns)
        padded = pl.ds(pl.multiple_of(offset + PAD, PAD), own_columns)
        for field, (ref, at) in enumerate(
            ((right1[0], plain), (right1[1], plain), (mob1, padded))
        ):
            for index in range(own_rows // 2):
                own, two_on, one_on, one_back = (
                    blocks[mask_x, mask_y][field, index] for mask_x in (0, 2, 1, 3)
                )
                swap = one_on, one_back
                one_on = jnp.where(start_even, swap[0], swap[1])
                one_back = jnp.where(start_even, swap[1], swap[0])
                for row, a, b in ((0, own, two_on), (own_rows, one_on, one_back)):
                    row = row + 2 * index
                    ref[row, at, :] = jnp.where(even, a, lane_roll(b, 1))
                    ref[row + 1, at, :] = jnp.where(even, lane_roll(a, -1), b)
    for row in range(rows1):
        mob1[row, :PAD, :] = mob1[row, columns1 : columns1 + PAD, :]
        mob1[row, PAD + columns1 :, :] = mob1[row, PAD : 2 * PAD, :]

    def coarsen(mobility, sums, out, out_mobility, dup):
        count, columns = out[0].shape[:2]
        fine = pl.ds(PAD, 2 * columns)
        for index in range(count):
            sums[2, index] = mobility[2 * index, fine, :] + mobility[2 * index + 1, fine, :]
        for index in range(count):
            for field in range(2):
                half = pair_rows(sums.at[field], index, columns)
                out[field][index] = 0.125 * pair_lanes(half, dup)
            half = pair_rows(sums.at[2], index, columns)
            put_padded((out_mobility,))(index, 0.125 * pair_lanes(half, dup))

    half1 = rows1 // 2
    for start in (0, half1):
        stage(one.set_weights, mob1, half1, start)
    stage(one.first_sweep, right1, rows1, put_padded(a1))
    for start in (0, half1):
        stage(one.sweep, a1, right1, start, half1, half1, window1, put_padded(b1))
    for start in (0, half1):
        put = put_sums(sums1, start // 2)
        stage(one.coarse_right, b1, right1, start, half1, half1, window1, put)
    stage(coarsen, mob1, sums1, right2, mob2, 2)

    stage(two.set_weights, mob2, rows2)
    stage(two.first_sweep, right2, rows2, put_padded(a2))
    stage(two.sweep, a2, right2, 0, rows2, rows2, window2, put_padded(b2))
    stage(two.coarse_right, b2, right2, 0, rows2, rows2, window2, put_sums(sums2))
    stage(coarsen, mob2, sums2, right3, mob3, 4)

    stage(three.set_weights, mob3, rows3)
    stage(three.first_sweep, right3, rows3, put_padded(a3))
    now, other = a3, b3
    for sweep_index in range(COARSE - 1):
        stage(three.sweep, now, right3, 0, rows3, rows3, window3, put_padded(other))
        now, other = other, now

    def correct(coarse, coarse_row, fine_in, fine_out, spread, index):
        for field in range(2):
            columns = fine_in[field].shape[1] - 2 * PAD
            spread_rows(
                spread.at[field], index, coarse[field][coarse_row, pl.ds(PAD, columns // 2), :]
            )
            both = spread[field, index]
            for row in (2 * coarse_row, 2 * coarse_row + 1):
                put_padded((fine_out[field],))(
                    row, fine_in[field][row, pl.ds(PAD, columns), :] + both
                )

    for row in range(rows3):
        correct(now, row, b2, a2, spread3, row)
    stage(two.sweep, a2, right2, 0, rows2, rows2, window2, put_padded(b2))
    stage(two.sweep, b2, right2, 0, rows2, rows2, window2, put_padded(a2))
    for row in range(rows2):
        correct(a2, row, b1, a1, spread2, row)
    for start, count in ((-2, 6), (4, own_rows - 2)):
        stage(one.sweep, a1, right1, start, count, count, window1, put_padded(b1))
    for start, count in ((-1, 5), (4, own_rows - 3)):
        stage(one.sweep, b1, right1, start, count, count, window1, put_padded(a1))

    rows, columns = conc_new.shape[:2]
    wide = (PAD - HALO, columns + 2 * HALO)
    near_own = pl.ds(pl.multiple_of(at_y * own_columns, PAD), own_columns + 2 * PAD)
    for index in range(own_rows + 2):
        inside = 1 <= index <= rows1
        row = index - 1 if inside else (index - 1) % rows1
        for field, (source, target) in enumerate(((conc_in, fine_a0), (chem_in, fine_a1))):
            tile = a1[field][row, near_own, :]
            on_even = lane_even(tile.shape, 1)
            if inside:
                tile = jnp.where(on_even, tile, lane_roll(tile, 1))
            else:
                tile = jnp.where(on_even, lane_roll(tile, -1), tile)
            spread_rows(spread_fine.at[field], index, tile)
            both = spread_fine[field, index, pl.ds(wide[0] + PAD, wide[1]), :]
            for fine in (HALO - 2 + 2 * index, HALO - 1 + 2 * index):
                put_window((target,), wide)(fine, source[fine] + both)
    fine = fine_level(weights)
    right_side = (right_conc,)
    fine.sweep(
        (fine_a0, fine_a1), right_side, HALO - 1, rows + 2, rows + 2, wide,
        put_window((fine_b0, fine_b1), wide),
    )

    def put_new(row, conc_value, chem_value):
        conc_new[row - HALO] = conc_value
        chem_new[row - HALO] = chem_value

    fine.sweep((fine_b0, fine_b1), right_side, HALO, rows, rows, (PAD, columns), put_new)


def call_kernel(kernel, outs, scratch, *args, vmem_mib=8):
    shapes = tuple(jax.ShapeDtypeStruct(shape, jnp.float32) for shape in outs)
    return pl.pallas_call(
        kernel,
        out_shape=shapes,
        in_specs=[whole_block()] * len(args),
        out_specs=tuple(whole_block() for _ in outs),
        scratch_shapes=[pltpu.VMEM(shape, jnp.float32) for shape in scratch],
        compiler_params=pltpu.CompilerParams(vmem_limit_bytes=vmem_mib * 1024 * 1024),
    )(*args)


def shifted(values, axis, by):
    count = lax.axis_size(axis)
    return lax.ppermute(values, axis, [(i, (i + by) % count) for i in range(count)])


def swapped(values, axis, mask):
    count = lax.axis_size(axis)
    return lax.ppermute(values, axis, [(i, i ^ mask) for i in range(count)])


def far_masks():
    count_x, count_y = lax.axis_size("gx"), lax.axis_size("gy")
    return list(range(1, count_x)), list(range(2, count_y, 2))


def slot_masks():
    along_x, along_y = far_masks()
    first = [(0, 0)] + [(0, y) for y in along_y] + [(x, 0) for x in along_x]
    second = [(x, y) for y in along_y for x in along_x[2:]]
    second += [(along_x[0], y) for y in along_y]
    return first, second, [(along_x[1], y) for y in along_y]


def swapped_both(values, mask_x, mask_y):
    count_x, count_y = lax.axis_size("gx"), lax.axis_size("gy")
    pairs = [
        (x * count_y + y, (x ^ mask_x) * count_y + (y ^ mask_y))
        for x in range(count_x)
        for y in range(count_y)
    ]
    return lax.ppermute(values, ("gx", "gy"), pairs)


def gathered(values):
    along_x, along_y = far_masks()
    across = [swapped(values, "gx", mask) for mask in along_x]
    beside = [swapped(values, "gy", mask) for mask in along_y]
    later, _ = lax.optimization_barrier((values, across[2]))
    corner = [swapped_both(later, along_x[0], mask) for mask in along_y]
    first = jnp.stack([values] + beside + across)
    second = [swapped(block, "gy", mask) for mask in along_y for block in across[2:]]
    second = jnp.stack(second + corner)
    third = jnp.stack([swapped(across[1], "gy", mask) for mask in along_y])
    far = tuple(swapped(group, "gy", 1) for group in (first, second, third))
    return (first, second, third) + far


def two_phase_solve(conc, chem):
    rows, columns, lanes = conc.shape
    frame = (rows + 2 * HALO, columns + 2 * PAD, lanes)
    edge = (2, HALO, columns, lanes)
    block = (rows, columns, lanes)
    fields = jnp.concatenate([conc, chem], axis=0).reshape((2,) + block)
    side, corner = (rows, PAD, lanes), (2 * HALO, PAD, lanes)
    low, high, to_left, to_right = call_kernel(
        edges_kernel, (edge, edge, side, side), (), fields
    )
    before, after = shifted(high, "gx", 1), shifted(low, "gx", -1)
    sides = [shifted(to_right, "gy", 1), shifted(to_left, "gy", -1)]
    to_left, to_right = call_kernel(corners_kernel, (corner, corner), (), before, after)
    sides += [shifted(to_right, "gy", 1), shifted(to_left, "gy", -1)]
    at, width = FrameRows(rows), columns + 2 * HALO
    packed_shape, sums = (3, rows // 4, columns // 2, lanes), (3, rows // 2, columns, lanes)

    def part(count, listed, wide):
        return (count, len(listed), wide, lanes)

    right_shapes = [part(0, listed, frame[1])[1:] for listed in (at.own, at.right_late, at.right_outer)]
    early, *kept = call_kernel(
        early_kernel,
        (
            packed_shape, part(2, at.swept_early, width), right_shapes[0],
            part(7, at.weights_early, width), part(2, at.joined, frame[1]),
        ),
        (frame, frame, part(2, at.weights_early, frame[1]), part(7, [0], width), sums),
        fields, *sides[:2],
    )
    packed, *kept_late = call_kernel(
        late_kernel,
        (
            packed_shape, part(2, at.swept_late, width), right_shapes[1],
            part(7, at.weights_late, width),
        ),
        (
            frame, frame, part(2, at.mid_late, frame[1]), part(7, at.weights_outer, width),
            right_shapes[2], sums,
        ),
        fields, before, after, *sides, early, *kept,
    )
    count_x, count_y = lax.axis_size("gx"), lax.axis_size("gy")
    grids = [(count_x * rows >> level + 1, count_y * columns >> level) for level in range(4)]
    scratch = []
    for level_rows, level_columns in grids[1:]:
        scratch += [(level_rows, level_columns + 2 * PAD, lanes)] * 5
        scratch += [(level_rows, level_columns, lanes)] * 9
    scratch += [(3, grids[2][0], grids[1][1], lanes), (3, grids[3][0], grids[2][1], lanes)]
    scratch += [(2, grids[2][0], grids[1][1], lanes), (2, grids[3][0], grids[2][1], lanes)]
    scratch += [(2, rows // 2 + 2, columns + 4 * PAD, lanes)] + [frame] * 4
    kernel = functools.partial(coarse_kernel, slot_masks(), (count_x, count_y))
    args = (*gathered(packed), *kept[:3], *kept_late)
    return call_kernel(kernel, (block, block), scratch, *args, vmem_mib=24)


def body(conc_old, chem_old):
    rows, columns, lanes = conc_old.shape
    count_x, count_y = lax.axis_size("gx"), lax.axis_size("gy")
    grid_bytes = count_x * rows * count_y * columns * lanes
    if (
        grid_bytes <= GRID_BYTES_MAX
        and rows % 16 == 0
        and lanes % 128 == 0
        and count_x * rows >= 64
        and count_y * columns >= 64
        and count_x == 4
        and count_y >= 4
        and count_y & (count_y - 1) == 0
        and columns == 16
    ):
        return two_phase_solve(conc_old, chem_old)
    start_fields = jnp.stack([conc_old, chem_old])
    result = plain_solve(start_fields)
    return (result[0], result[1])


def solution(mesh):
    in_specs = (P(("img", "gx"), "gy", None), P(("img", "gx"), "gy", None))
    out_specs = (P(("img", "gx"), "gy", None), P(("img", "gx"), "gy", None))
    return jax.shard_map(body, mesh=mesh, in_specs=in_specs, out_specs=out_specs, check_vma=False)
```

```python
import functools

import jax
import jax.numpy as jnp
from jax import lax
from jax.experimental import pallas as pl
from jax.experimental.pallas import tpu as pltpu
from jax.sharding import PartitionSpec as P

LEVELS = 4
SWEEPS = 2
COARSE = 6


TIME_STEP = 32.0
GRADIENT_ENERGY = 0.5
STABILIZER = 2.0
DAMPING = 0.7


def extended(cells, sides, width):
    for axis, dim in sides:
        count = lax.axis_size(axis)
        head = lax.slice_in_dim(cells, 0, width, axis=dim)
        tail = lax.slice_in_dim(cells, cells.shape[dim] - width, cells.shape[dim], axis=dim)
        cells = jnp.concatenate(
            [
                lax.ppermute(tail, axis, [(i, (i + 1) % count) for i in range(count)]),
                cells,
                lax.ppermute(head, axis, [((i + 1) % count, i) for i in range(count)]),
            ],
            axis=dim,
        )
    return cells


def mobility_of(concentration):
    return 0.1 + jnp.square(1.0 - concentration * concentration)


def right_of(concentration):
    return jnp.stack(
        [
            concentration,
            concentration * concentration * concentration - (1.0 + STABILIZER) * concentration,
        ]
    )


def face_weights(mob_padded, level_scale):
    middle = mob_padded[1:-1, 1:-1, :]
    half_scale = 0.5 * level_scale
    weights = (
        half_scale * (middle + mob_padded[2:, 1:-1, :]),
        half_scale * (middle + mob_padded[:-2, 1:-1, :]),
        half_scale * (middle + mob_padded[1:-1, 2:, :]),
        half_scale * (middle + mob_padded[1:-1, :-2, :]),
        half_scale * (middle + jnp.roll(middle, -1, axis=2)),
        half_scale * (middle + jnp.roll(middle, 1, axis=2)),
    )
    total_weight = weights[0] + weights[1] + weights[2] + weights[3] + weights[4] + weights[5]
    return (weights, total_weight)


def neighbour_list(padded, middle):
    return (
        padded[2:, 1:-1, :],
        padded[:-2, 1:-1, :],
        padded[1:-1, 2:, :],
        padded[1:-1, :-2, :],
        jnp.roll(middle, -1, axis=2),
        jnp.roll(middle, 1, axis=2),
    )


def apply_operator(padded, weights, level_scale):
    middle = padded[:, 1:-1, 1:-1, :]
    conc_near = neighbour_list(padded[0], middle[0])
    chem_near = neighbour_list(padded[1], middle[1])
    flux = weights[0] * (chem_near[0] - middle[1])
    for position in range(1, 6):
        flux = flux + weights[position] * (chem_near[position] - middle[1])
    laplace = (
        conc_near[0]
        + conc_near[1]
        + conc_near[2]
        + conc_near[3]
        + conc_near[4]
        + conc_near[5]
        - 6.0 * middle[0]
    )
    first_eq = middle[0] - TIME_STEP * flux
    second_eq = middle[1] - STABILIZER * middle[0] + GRADIENT_ENERGY * level_scale * laplace
    return jnp.stack([first_eq, second_eq])


def update(residual, total_weight, level_scale):
    diagonal = STABILIZER + 6.0 * GRADIENT_ENERGY * level_scale
    coupling = TIME_STEP * total_weight
    determinant = 1.0 + coupling * diagonal
    conc_step = (residual[0] - coupling * residual[1]) / determinant
    chem_step = (residual[1] + diagonal * residual[0]) / determinant
    return DAMPING * jnp.stack([conc_step, chem_step])


def sweep_once(padded, right_side, mob_padded, level_scale):
    weights, total_weight = face_weights(mob_padded, level_scale)
    residual = right_side - apply_operator(padded, weights, level_scale)
    return padded[:, 1:-1, 1:-1, :] + update(residual, total_weight, level_scale)


def defect(padded, right_side, mob_padded, level_scale):
    weights = face_weights(mob_padded, level_scale)[0]
    return right_side - apply_operator(padded, weights, level_scale)


def coarsen(values):
    dims_now = values.shape
    grouped = values.reshape(
        dims_now[:-3] + (dims_now[-3] // 2, 2, dims_now[-2] // 2, 2, dims_now[-1] // 2, 2)
    )
    return jnp.sum(grouped, axis=(-5, -3, -1)) * 0.125


def refine(values):
    for axis_pos in (-3, -2, -1):
        values = jnp.repeat(values, 2, axis=axis_pos)
    return values


def trim_rim(values, width):
    return values[..., width:-width, width:-width, :]


def field_rim(fields):
    return extended(fields, (("gx", 1), ("gy", 2)), 1)


def coarsest_solve(right_side, mobility, level_scale):
    mob_padded = extended(mobility, (("gx", 0), ("gy", 1)), 1)
    fields = update(right_side, face_weights(mob_padded, level_scale)[1], level_scale)
    for sweep_index in range(COARSE - 1):
        padded = extended(fields, (("gx", 1), ("gy", 2)), 1)
        fields = sweep_once(padded, right_side, mob_padded, level_scale)
    return fields


def plain_solve(start_fields):
    outer_fields = field_rim(start_fields)
    mob_outer = mobility_of(outer_fields[0])
    mobility = trim_rim(mob_outer, 1)
    level_data = []
    for level_index in range(LEVELS - 1):
        if level_index == 0:
            mob_padded = mob_outer
        else:
            mob_padded = extended(mobility, (("gx", 0), ("gy", 1)), 1)
        level_data.append((mob_padded, 0.25**level_index))
        mobility = coarsen(mobility)
    coarsest_scale = 0.25 ** (LEVELS - 1)

    def cycle_level(level_index, right_side):
        if level_index == LEVELS - 1:
            return coarsest_solve(right_side, mobility, coarsest_scale)
        mob_padded, level_scale = level_data[level_index]
        if level_index == 0:
            fields = sweep_once(outer_fields, right_side, mob_padded, level_scale)
        else:
            fields = update(right_side, face_weights(mob_padded, level_scale)[1], level_scale)
        fields = sweep_once(field_rim(fields), right_side, mob_padded, level_scale)
        residual = defect(field_rim(fields), right_side, mob_padded, level_scale)
        fields = fields + refine(cycle_level(level_index + 1, coarsen(residual)))
        for sweep_index in range(SWEEPS):
            fields = sweep_once(field_rim(fields), right_side, mob_padded, level_scale)
        return fields

    return cycle_level(0, right_of(start_fields[0]))


HALO = 4
PAD = 8
GRID_BYTES_MAX = 2 * 1024 * 1024


def whole_block():
    return pl.BlockSpec(memory_space=pltpu.VMEM)


def lane_roll(values, shift):
    return pltpu.roll(values, shift % values.shape[1], axis=1)


def lane_even(shape, dup):
    return (lax.broadcasted_iota(jnp.int32, shape, 1) // dup) % 2 == 0


def loop_rows(count, unroll, row_group):
    steps, rest = divmod(count, unroll)
    if steps == 1:
        row_group(0, unroll)
    elif steps > 1:

        def step(index, carry):
            row_group(index * unroll, unroll)
            return carry

        lax.fori_loop(0, steps, step, 0)
    if rest:
        row_group(steps * unroll, rest)


def lane_swap(values):
    return jnp.where(lane_even(values.shape, 1), lane_roll(values, -1), lane_roll(values, 1))


class RowCache:
    def __init__(self, ref, rows, first, width):
        self.ref, self.rows, self.first, self.width = ref, rows, first, width
        self.values = {}

    def __getitem__(self, key):
        if key not in self.values:
            total = self.ref.shape[0]
            row = key if self.rows is None else self.rows[key]
            outside = isinstance(row, int) and not 0 <= row < total
            values = self.ref[row % total if outside else row, pl.ds(self.first, self.width), :]
            self.values[key] = lane_swap(values) if outside else values
        return self.values[key]


def stage(run, *args):
    pl.when(lax.axis_index("gy") >= 0)(functools.partial(run, *args))


def chem_right(conc):
    return conc * (conc * conc - (1.0 + STABILIZER))


class Rows:
    def __init__(self, total, *parts):
        self.places = {
            row: (ref, index) for ref, rows in parts for index, row in enumerate(rows)
        }
        self.shape = (total,) + parts[0][0].shape[1:]

    def place(self, at):
        row, *rest = at if isinstance(at, tuple) else (at,)
        ref, index = self.places[row]
        return ref, (index, *rest)

    def __getitem__(self, at):
        ref, index = self.place(at)
        return ref[index]

    def __setitem__(self, at, values):
        ref, index = self.place(at)
        ref[index] = values


class Level:
    def __init__(self, level_index, weights, weights_from=PAD, right_from=PAD):
        self.scale = 0.25**level_index
        self.dup = 2**level_index
        self.diagonal = STABILIZER + 6.0 * GRADIENT_ENERGY * self.scale
        self.weights = weights
        self.weights_from, self.right_from = weights_from, right_from

    def set_weights(self, mobility, count, start=0):
        width = self.weights[0].shape[1]
        half = 0.5 * self.scale * TIME_STEP
        face_x, up_y, down_y, up_z, down_z, coupling, gain = self.weights

        def at(row, shift=0):
            return mobility[row, pl.ds(self.weights_from + shift, width), :]

        def group(first, size):
            rows = RowCache(mobility, None, self.weights_from, width)
            before = half * (rows[start + first - 1] + rows[start + first])
            for i in range(size):
                r = start + first + i
                here = rows[r]
                after = half * (here + rows[r + 1])
                to_up_y = half * (here + at(r, 1))
                to_down_y = half * (here + at(r, -1))
                to_up_z = half * (here + lane_roll(here, -self.dup))
                to_down_z = half * (here + lane_roll(here, self.dup))
                total_weight = (before + after) + (to_up_y + to_down_y) + (to_up_z + to_down_z)
                face_x[r] = after
                up_y[r] = to_up_y
                down_y[r] = to_down_y
                up_z[r] = to_up_z
                down_z[r] = to_down_z
                coupling[r] = total_weight
                gain[r] = DAMPING / (1.0 + total_weight * self.diagonal)
                before = after

        loop_rows(count, count, group)

    def residuals(self, fields, right, rows, window, fields_from=0):
        conc, chem = fields
        first, width = window
        face_x, up_y, down_y, up_z, down_z, coupling, gain = self.weights

        def at(ref, row, shift=0):
            return ref[row, pl.ds(first - fields_from + shift, width), :]

        def weight(ref, row):
            return ref[row, pl.ds(first - self.weights_from, width), :]

        def right_at(row):
            values = [ref[row, pl.ds(first - self.right_from, width), :] for ref in right]
            return values if len(values) == 2 else values + [chem_right(values[0])]

        total = conc.shape[0]
        if isinstance(rows[0], int):
            centres, listed = [row % total for row in rows[1:-1]], None
        else:
            centres, listed = range(1, len(rows) - 1), rows
        u = RowCache(chem, listed, first - fields_from, width)
        c = RowCache(conc, listed, first - fields_from, width)
        across = RowCache(face_x, listed, first - self.weights_from, width)
        for key in centres:
            r = key if listed is None else listed[key]
            c_here, u_here = c[key], u[key]
            here = weight(coupling, r)
            conc_right, chem_right_here = right_at(r)
            flux = across[key] * u[key + 1] + across[key - 1] * u[key - 1]
            flux = flux + (weight(up_y, r) * at(chem, r, 1) + weight(down_y, r) * at(chem, r, -1))
            flux = flux + (conc_right - c_here - here * u_here)
            flux_z = weight(up_z, r) * lane_roll(u_here, -self.dup)
            flux_z = flux_z + weight(down_z, r) * lane_roll(u_here, self.dup)
            conc_left = flux + flux_z
            near = (c[key - 1] + c[key + 1]) + (at(conc, r, 1) + at(conc, r, -1))
            pull = GRADIENT_ENERGY * self.scale
            chem_left = (chem_right_here - u_here + self.diagonal * c_here) - pull * near
            near_z = lane_roll(c_here, self.dup) + lane_roll(c_here, -self.dup)
            chem_left = chem_left - pull * near_z
            yield r, c_here, u_here, conc_left, chem_left, here, weight(gain, r)

    def steps(self, conc_left, chem_left, coupling, gain):
        return (
            gain * (conc_left - coupling * chem_left),
            gain * (chem_left + self.diagonal * conc_left),
        )

    def first_sweep(self, right, unroll, put):
        coupling, gain = self.weights[5:]

        def group(first, size):
            for i in range(size):
                r = first + i
                put(r, *self.steps(right[0][r], right[1][r], coupling[r], gain[r]))

        loop_rows(right[0].shape[0], unroll, group)

    def row_window(self, start, first, size):
        return [start + first + i - 1 for i in range(size + 2)]

    def sweep(self, fields, right, start, count, unroll, window, put):
        def group(first, size):
            rows = self.row_window(start, first, size)
            for r, c, u, *left in self.residuals(fields, right, rows, window):
                conc_step, chem_step = self.steps(*left)
                put(r, c + conc_step, u + chem_step)

        loop_rows(count, unroll, group)

    def coarse_right(self, fields, right, start, count, unroll, window, put, fields_from=0):
        def group(first, size):
            rows = self.row_window(start, first, size)
            items = self.residuals(fields, right, rows, window, fields_from)
            half = first // 2 if isinstance(first, int) else lax.shift_right_logical(first, 1)
            kept = None
            for i, (_, _, _, conc_left, chem_left, _, _) in enumerate(items):
                if i % 2 == 0:
                    kept = conc_left, chem_left
                else:
                    put(half + i // 2, kept[0] + conc_left, kept[1] + chem_left)

        loop_rows(count, unroll, group)


def put_padded(refs):
    def put(row, *values):
        for ref, value in zip(refs, values):
            width = value.shape[0]
            ref[row, PAD : PAD + width, :] = value
            ref[row, :PAD, :] = value[width - PAD :]
            ref[row, PAD + width :, :] = value[:PAD]

    return put


def put_window(refs, window):
    def put(row, *values):
        for ref, value in zip(refs, values):
            ref[row, window[0] : window[0] + window[1], :] = value

    return put


def put_sums(sums, offset=0):
    def put(row, *values):
        for field, value in enumerate(values):
            sums[field, offset + row] = value

    return put


def pair_rows(ref, row, count):
    return ref[row, pl.ds(0, count, stride=2), :] + ref[row, pl.ds(1, count, stride=2), :]


def spread_rows(ref, row, values):
    count = values.shape[0]
    ref[row, pl.ds(0, count, stride=2), :] = values
    ref[row, pl.ds(1, count, stride=2), :] = values


def pair_lanes(values, dup):
    other = jnp.where(
        lane_even(values.shape, dup), lane_roll(values, -dup), lane_roll(values, dup)
    )
    return values + other


def side_tiles(conc, chem, to_left, to_right, at, low):
    columns = conc.shape[0]
    to_left[at] = jnp.where(low, conc[:PAD], half_turn(chem[:PAD]))
    to_right[at] = jnp.where(low, half_turn(chem[columns - PAD :]), conc[columns - PAD :])


def low_half(lanes):
    return lax.broadcasted_iota(jnp.int32, (PAD, lanes), 0) < HALO


def edges_kernel(fields, low_rows, high_rows, to_left, to_right):
    rows, columns, lanes = fields.shape[1:]
    low_rows[...] = fields[:, :HALO]
    high_rows[...] = fields[:, rows - HALO :]
    for row in range(rows):
        side_tiles(fields[0, row], fields[1, row], to_left, to_right, row, low_half(lanes))


def corners_kernel(before, after, to_left, to_right):
    lanes = before.shape[-1]
    for at in range(2 * HALO):
        source, row = (before, at) if at < HALO else (after, at - HALO)
        side_tiles(source[0, row], source[1, row], to_left, to_right, at, low_half(lanes))


def frame_row(row, rows, own, before, after):
    if row < HALO:
        return before[row]
    if row < HALO + rows:
        return own[row - HALO]
    return after[row - HALO - rows]


def half_turn(values):
    return pltpu.roll(values, HALO, axis=0)


class FrameRows:
    def __init__(self, rows):
        self.total = rows + 2 * HALO
        end = self.total
        self.own = range(HALO, end - HALO)
        self.weights_early = range(HALO + 1, end - HALO - 1)
        self.swept_early = range(HALO + 2, end - HALO - 2)
        self.joined = [HALO + 1, HALO + 2, end - HALO - 3, end - HALO - 2]
        self.weights_late = [*range(2, HALO + 1), *range(end - HALO - 1, end - 3)]
        self.weights_outer = [0, 1, end - 3, end - 2, end - 1]
        self.right_late = [HALO - 1, end - HALO]
        self.right_outer = [*range(HALO - 1), *range(end - HALO + 1, end)]
        self.swept_late = [*range(2, HALO + 2), *range(end - HALO - 2, end - 2)]
        self.mid_late = [*range(1, HALO + 1), *range(end - HALO - 1, end - 1)]

    def weights(self, early, late):
        return [
            Rows(self.total, (early.at[i], self.weights_early), (late.at[i], self.weights_late))
            for i in range(7)
        ]

    def swept(self, early, late):
        return [
            Rows(self.total, (early.at[i], self.swept_early), (late.at[i], self.swept_late))
            for i in range(2)
        ]


def fine_level(weights):
    return Level(0, weights, HALO, 0)


def set_row(conc, chem, left, right, row, conc_at, chem_at, mobility):
    c = jnp.concatenate([left, conc, right])
    if conc_at is not None:
        conc_at[row] = c
    chem_at[row] = jnp.concatenate([half_turn(left), chem, half_turn(right)])
    gap = 1.0 - c * c
    mobility[row] = 0.1 + gap * gap


def pack(sums, field, index, out):
    count = sums.shape[2] // 2
    even = lane_even((count, sums.shape[3]), 1)
    a = pair_rows(sums.at[field], 2 * index, count)
    b = pair_rows(sums.at[field], 2 * index + 1, count)
    out[field, index] = 0.125 * jnp.where(even, a + lane_roll(a, -1), b + lane_roll(b, 1))


def early_kernel(
    fields, own_left, own_right,
    packed, kept, right_conc, all_weights, joined,
    chem_start, mobility, mid, outer, sums,
):
    rows, columns = fields.shape[1:3]
    at = FrameRows(rows)
    right_side = (Rows(at.total, (right_conc, at.own)),)
    for row in at.own:
        i = row - HALO
        set_row(
            fields[0, i], fields[1, i], own_left[i], own_right[i],
            row, right_side[0], chem_start, mobility,
        )
    weights = [
        Rows(at.total, (all_weights.at[i], at.weights_early), (outer.at[i], [HALO]))
        for i in range(7)
    ]
    level = fine_level(weights)
    level.set_weights(mobility, rows - 1, HALO)
    wide = (PAD - HALO, columns + 2 * HALO)
    middle = [r for r in at.weights_early if r not in at.joined]
    mids = [
        Rows(at.total, (mid.at[i], middle), (joined.at[i], at.joined)) for i in range(2)
    ]
    swept = [Rows(at.total, (kept.at[i], at.swept_early)) for i in range(2)]
    level.sweep(
        (right_side[0], chem_start), right_side, HALO + 1, rows - 2, rows - 2, wide,
        put_window(mids, wide),
    )
    level.sweep(
        mids, right_side, HALO + 2, rows - 4, rows - 4, wide, put_window(swept, (0, wide[1]))
    )
    level.coarse_right(
        swept, right_side, 2 * HALO, rows - 2 * HALO, rows - 2 * HALO, (PAD, columns),
        put_sums(sums, HALO // 2), wide[0],
    )
    own = slice(PAD, PAD + columns)
    for index in range(rows // 2):
        row = HALO + 2 * index
        sums[2, index] = mobility[row, own, :] + mobility[row + 1, own, :]
    for index in range(rows // 4):
        pack(sums, 2, index, packed)
        if HALO // 4 <= index < (rows - HALO) // 4:
            pack(sums, 0, index, packed)
            pack(sums, 1, index, packed)
        else:
            packed[0, index] = jnp.zeros(packed.shape[2:], jnp.float32)
            packed[1, index] = jnp.zeros(packed.shape[2:], jnp.float32)


def late_kernel(
    fields, before, after, own_left, own_right, corner_left, corner_right,
    packed_early, kept_early, right_early, weights_early, joined,
    packed, kept, right_conc, all_weights,
    chem_start, mobility, mid, outer, right_outer, sums,
):
    rows, columns = fields.shape[1:3]
    at = FrameRows(rows)
    end = at.total
    right = Rows(
        end, (right_early, at.own), (right_conc, at.right_late), (right_outer, at.right_outer)
    )
    for row in [*range(HALO + 2), *range(end - HALO - 2, end)]:
        if row in at.own:
            i = row - HALO
            values = fields[0, i], fields[1, i], own_left[i], own_right[i]
            set_row(*values, row, None, chem_start, mobility)
        else:
            source, i = (before, row) if row < HALO else (after, row - rows - HALO)
            corner = row if row < HALO else row - rows
            values = source[0, i], source[1, i], corner_left[corner], corner_right[corner]
            set_row(*values, row, right, chem_start, mobility)
    weights = at.weights(weights_early, all_weights)
    for i, one in enumerate(weights):
        for index, row in enumerate(at.weights_outer):
            one.places[row] = outer.at[i], index
    level = fine_level(weights)
    level.set_weights(mobility, HALO + 1, 0)
    level.set_weights(mobility, HALO + 1, end - HALO - 1)
    wide = (PAD - HALO, columns + 2 * HALO)
    mids = [Rows(end, (joined.at[i], at.joined), (mid.at[i], at.mid_late)) for i in range(2)]
    swept = at.swept(kept_early, kept)
    for start in (1, end - HALO - 1):
        level.sweep(
            (right, chem_start), (right,), start, HALO, HALO, wide, put_window(mids, wide)
        )
    for start in (2, end - HALO - 2):
        level.sweep(mids, (right,), start, HALO, HALO, wide, put_window(swept, (0, wide[1])))
    for start in (HALO, end - 2 * HALO):
        level.coarse_right(
            swept, (right,), start, HALO, HALO, (PAD, columns),
            put_sums(sums, (start - HALO) // 2), wide[0],
        )
    packed[...] = packed_early[...]
    for index in range(rows // 4):
        if not HALO // 4 <= index < (rows - HALO) // 4:
            pack(sums, 0, index, packed)
            pack(sums, 1, index, packed)


def coarse_kernel(
    slots, grid, first, second, third, first_far, second_far, third_far,
    kept_early, right_early, weights_early, kept_late, right_late, weights_late,
    conc_new, chem_new, *scratch,
):
    at = FrameRows(conc_new.shape[0])
    conc_in, chem_in = at.swept(kept_early, kept_late)
    weights = at.weights(weights_early, weights_late)
    right_conc = Rows(at.total, (right_early, at.own), (right_late, at.right_late))
    scratch = list(scratch)
    start_even, at_y = lax.axis_index("gx") % 2 == 0, lax.axis_index("gy")
    levels = []
    for level_index in (1, 2, 3):
        level = Level(level_index, scratch[5:14][2:])
        mobility, a, b, right = scratch[0], scratch[1:3], scratch[3:5], scratch[5:7]
        levels.append((level, mobility, right, a, b))
        del scratch[:14]
    sums1, sums2, spread2, spread3, spread_fine, fine_a0, fine_a1, fine_b0, fine_b1 = scratch
    one, mob1, right1, a1, b1 = levels[0]
    two, mob2, right2, a2, b2 = levels[1]
    three, mob3, right3, a3, b3 = levels[2]
    rows1, columns1, lanes = right1[0].shape
    rows2, columns2 = right2[0].shape[:2]
    rows3, columns3 = right3[0].shape[:2]
    window1, window2, window3 = (PAD, columns1), (PAD, columns2), (PAD, columns3)
    own_rows, own_columns = 2 * rows1 // grid[0], columns1 // grid[1]
    even = lane_even((own_columns, lanes), 1)
    blocks = {}
    for last, sources in enumerate(((first, second, third), (first_far, second_far, third_far))):
        for source, masks in zip(sources, slots):
            for slot, (mask_x, mask_y) in enumerate(masks):
                blocks[mask_x, mask_y ^ last] = source.at[slot]

    for mask_y in range(grid[1]):
        offset = (at_y ^ mask_y) * own_columns
        plain = pl.ds(pl.multiple_of(offset, PAD), own_columns)
        padded = pl.ds(pl.multiple_of(offset + PAD, PAD), own_columns)
        for field, (ref, at) in enumerate(
            ((right1[0], plain), (right1[1], plain), (mob1, padded))
        ):
            for index in range(own_rows // 2):
                own, two_on, one_on, one_back = (
                    blocks[mask_x, mask_y][field, index] for mask_x in (0, 2, 1, 3)
                )
                swap = one_on, one_back
                one_on = jnp.where(start_even, swap[0], swap[1])
                one_back = jnp.where(start_even, swap[1], swap[0])
                for row, a, b in ((0, own, two_on), (own_rows, one_on, one_back)):
                    row = row + 2 * index
                    ref[row, at, :] = jnp.where(even, a, lane_roll(b, 1))
                    ref[row + 1, at, :] = jnp.where(even, lane_roll(a, -1), b)
    for row in range(rows1):
        mob1[row, :PAD, :] = mob1[row, columns1 : columns1 + PAD, :]
        mob1[row, PAD + columns1 :, :] = mob1[row, PAD : 2 * PAD, :]

    def coarsen(mobility, sums, out, out_mobility, dup):
        count, columns = out[0].shape[:2]
        fine = pl.ds(PAD, 2 * columns)
        for index in range(count):
            sums[2, index] = mobility[2 * index, fine, :] + mobility[2 * index + 1, fine, :]
        for index in range(count):
            for field in range(2):
                half = pair_rows(sums.at[field], index, columns)
                out[field][index] = 0.125 * pair_lanes(half, dup)
            half = pair_rows(sums.at[2], index, columns)
            put_padded((out_mobility,))(index, 0.125 * pair_lanes(half, dup))

    half1 = rows1 // 2
    for start in (0, half1):
        stage(one.set_weights, mob1, half1, start)
    stage(one.first_sweep, right1, rows1, put_padded(a1))
    for start in (0, half1):
        stage(one.sweep, a1, right1, start, half1, half1, window1, put_padded(b1))
    for start in (0, half1):
        put = put_sums(sums1, start // 2)
        stage(one.coarse_right, b1, right1, start, half1, half1, window1, put)
    stage(coarsen, mob1, sums1, right2, mob2, 2)

    stage(two.set_weights, mob2, rows2)
    stage(two.first_sweep, right2, rows2, put_padded(a2))
    stage(two.sweep, a2, right2, 0, rows2, rows2, window2, put_padded(b2))
    stage(two.coarse_right, b2, right2, 0, rows2, rows2, window2, put_sums(sums2))
    stage(coarsen, mob2, sums2, right3, mob3, 4)

    stage(three.set_weights, mob3, rows3)
    stage(three.first_sweep, right3, rows3, put_padded(a3))
    now, other = a3, b3
    for sweep_index in range(COARSE - 1):
        stage(three.sweep, now, right3, 0, rows3, rows3, window3, put_padded(other))
        now, other = other, now

    def correct(coarse, coarse_row, fine_in, fine_out, spread, index):
        for field in range(2):
            columns = fine_in[field].shape[1] - 2 * PAD
            spread_rows(
                spread.at[field], index, coarse[field][coarse_row, pl.ds(PAD, columns // 2), :]
            )
            both = spread[field, index]
            for row in (2 * coarse_row, 2 * coarse_row + 1):
                put_padded((fine_out[field],))(
                    row, fine_in[field][row, pl.ds(PAD, columns), :] + both
                )

    for row in range(rows3):
        correct(now, row, b2, a2, spread3, row)
    stage(two.sweep, a2, right2, 0, rows2, rows2, window2, put_padded(b2))
    stage(two.sweep, b2, right2, 0, rows2, rows2, window2, put_padded(a2))
    for row in range(rows2):
        correct(a2, row, b1, a1, spread2, row)
    for start, count in ((-2, 6), (4, own_rows - 2)):
        stage(one.sweep, a1, right1, start, count, count, window1, put_padded(b1))
    for start, count in ((-1, 5), (4, own_rows - 3)):
        stage(one.sweep, b1, right1, start, count, count, window1, put_padded(a1))

    rows, columns = conc_new.shape[:2]
    wide = (PAD - HALO, columns + 2 * HALO)
    near_own = pl.ds(pl.multiple_of(at_y * own_columns, PAD), own_columns + 2 * PAD)
    for index in range(own_rows + 2):
        inside = 1 <= index <= rows1
        row = index - 1 if inside else (index - 1) % rows1
        for field, (source, target) in enumerate(((conc_in, fine_a0), (chem_in, fine_a1))):
            tile = a1[field][row, near_own, :]
            on_even = lane_even(tile.shape, 1)
            if inside:
                tile = jnp.where(on_even, tile, lane_roll(tile, 1))
            else:
                tile = jnp.where(on_even, lane_roll(tile, -1), tile)
            spread_rows(spread_fine.at[field], index, tile)
            both = spread_fine[field, index, pl.ds(wide[0] + PAD, wide[1]), :]
            for fine in (HALO - 2 + 2 * index, HALO - 1 + 2 * index):
                put_window((target,), wide)(fine, source[fine] + both)
    fine = fine_level(weights)
    right_side = (right_conc,)
    half = rows // 2
    for start in (HALO - 1, HALO + half):
        stage(
            fine.sweep, (fine_a0, fine_a1), right_side, start, half + 1, half + 1, wide,
            put_window((fine_b0, fine_b1), wide),
        )

    def put_new(row, conc_value, chem_value):
        conc_new[row - HALO] = conc_value
        chem_new[row - HALO] = chem_value

    for start in (HALO, HALO + half):
        stage(
            fine.sweep, (fine_b0, fine_b1), right_side, start, half, half, (PAD, columns), put_new
        )


def call_kernel(kernel, outs, scratch, *args, vmem_mib=8):
    shapes = tuple(jax.ShapeDtypeStruct(shape, jnp.float32) for shape in outs)
    return pl.pallas_call(
        kernel,
        out_shape=shapes,
        in_specs=[whole_block()] * len(args),
        out_specs=tuple(whole_block() for _ in outs),
        scratch_shapes=[pltpu.VMEM(shape, jnp.float32) for shape in scratch],
        compiler_params=pltpu.CompilerParams(vmem_limit_bytes=vmem_mib * 1024 * 1024),
    )(*args)


def shifted(values, axis, by):
    count = lax.axis_size(axis)
    return lax.ppermute(values, axis, [(i, (i + by) % count) for i in range(count)])


def swapped(values, axis, mask):
    count = lax.axis_size(axis)
    return lax.ppermute(values, axis, [(i, i ^ mask) for i in range(count)])


def far_masks():
    count_x, count_y = lax.axis_size("gx"), lax.axis_size("gy")
    return list(range(1, count_x)), list(range(2, count_y, 2))


def slot_masks():
    along_x, along_y = far_masks()
    first = [(0, 0)] + [(0, y) for y in along_y] + [(x, 0) for x in along_x]
    second = [(x, y) for y in along_y for x in along_x[2:]]
    second += [(along_x[0], y) for y in along_y]
    return first, second, [(along_x[1], y) for y in along_y]


def swapped_both(values, mask_x, mask_y):
    count_x, count_y = lax.axis_size("gx"), lax.axis_size("gy")
    pairs = [
        (x * count_y + y, (x ^ mask_x) * count_y + (y ^ mask_y))
        for x in range(count_x)
        for y in range(count_y)
    ]
    return lax.ppermute(values, ("gx", "gy"), pairs)


def gathered(values):
    along_x, along_y = far_masks()
    across = [swapped(values, "gx", mask) for mask in along_x]
    beside = [swapped(values, "gy", mask) for mask in along_y]
    later, _ = lax.optimization_barrier((values, across[2]))
    corner = [swapped_both(later, along_x[0], mask) for mask in along_y]
    first = jnp.stack([values] + beside + across)
    second = [swapped(block, "gy", mask) for mask in along_y for block in across[2:]]
    second = jnp.stack(second + corner)
    third = jnp.stack([swapped(across[1], "gy", mask) for mask in along_y])
    far = tuple(swapped(group, "gy", 1) for group in (first, second, third))
    return (first, second, third) + far


def two_phase_solve(conc, chem):
    rows, columns, lanes = conc.shape
    frame = (rows + 2 * HALO, columns + 2 * PAD, lanes)
    edge = (2, HALO, columns, lanes)
    block = (rows, columns, lanes)
    fields = jnp.concatenate([conc, chem], axis=0).reshape((2,) + block)
    side, corner = (rows, PAD, lanes), (2 * HALO, PAD, lanes)
    low, high, to_left, to_right = call_kernel(
        edges_kernel, (edge, edge, side, side), (), fields
    )
    before, after = shifted(high, "gx", 1), shifted(low, "gx", -1)
    sides = [shifted(to_right, "gy", 1), shifted(to_left, "gy", -1)]
    to_left, to_right = call_kernel(corners_kernel, (corner, corner), (), before, after)
    sides += [shifted(to_right, "gy", 1), shifted(to_left, "gy", -1)]
    at, width = FrameRows(rows), columns + 2 * HALO
    packed_shape, sums = (3, rows // 4, columns // 2, lanes), (3, rows // 2, columns, lanes)

    def part(count, listed, wide):
        return (count, len(listed), wide, lanes)

    right_shapes = [part(0, listed, frame[1])[1:] for listed in (at.own, at.right_late, at.right_outer)]
    early, *kept = call_kernel(
        early_kernel,
        (
            packed_shape, part(2, at.swept_early, width), right_shapes[0],
            part(7, at.weights_early, width), part(2, at.joined, frame[1]),
        ),
        (frame, frame, part(2, at.weights_early, frame[1]), part(7, [0], width), sums),
        fields, *sides[:2],
    )
    packed, *kept_late = call_kernel(
        late_kernel,
        (
            packed_shape, part(2, at.swept_late, width), right_shapes[1],
            part(7, at.weights_late, width),
        ),
        (
            frame, frame, part(2, at.mid_late, frame[1]), part(7, at.weights_outer, width),
            right_shapes[2], sums,
        ),
        fields, before, after, *sides, early, *kept,
    )
    count_x, count_y = lax.axis_size("gx"), lax.axis_size("gy")
    grids = [(count_x * rows >> level + 1, count_y * columns >> level) for level in range(4)]
    scratch = []
    for level_rows, level_columns in grids[1:]:
        scratch += [(level_rows, level_columns + 2 * PAD, lanes)] * 5
        scratch += [(level_rows, level_columns, lanes)] * 9
    scratch += [(3, grids[2][0], grids[1][1], lanes), (3, grids[3][0], grids[2][1], lanes)]
    scratch += [(2, grids[2][0], grids[1][1], lanes), (2, grids[3][0], grids[2][1], lanes)]
    scratch += [(2, rows // 2 + 2, columns + 4 * PAD, lanes)] + [frame] * 4
    kernel = functools.partial(coarse_kernel, slot_masks(), (count_x, count_y))
    args = (*gathered(packed), *kept[:3], *kept_late)
    return call_kernel(kernel, (block, block), scratch, *args, vmem_mib=24)


def body(conc_old, chem_old):
    rows, columns, lanes = conc_old.shape
    count_x, count_y = lax.axis_size("gx"), lax.axis_size("gy")
    grid_bytes = count_x * rows * count_y * columns * lanes
    if (
        grid_bytes <= GRID_BYTES_MAX
        and rows % 16 == 0
        and lanes % 128 == 0
        and count_x * rows >= 64
        and count_y * columns >= 64
        and count_x == 4
        and count_y >= 4
        and count_y & (count_y - 1) == 0
        and columns == 16
    ):
        return two_phase_solve(conc_old, chem_old)
    start_fields = jnp.stack([conc_old, chem_old])
    result = plain_solve(start_fields)
    return (result[0], result[1])


def solution(mesh):
    in_specs = (P(("img", "gx"), "gy", None), P(("img", "gx"), "gy", None))
    out_specs = (P(("img", "gx"), "gy", None), P(("img", "gx"), "gy", None))
    return jax.shard_map(body, mesh=mesh, in_specs=in_specs, out_specs=out_specs, check_vma=False)
```
